32 devices in a mesh: band: 2 (over y), dom: 16 (over z, x, core).
Axes of the slice: x: 2, y: 2, z: 4, core: 2. Of those that a mesh axis runs over, the one named last changes fastest.
Arguments:
- states_in: float32 [128, 16384], P('band', 'dom'), may hold values from -6 to 6
- stiffness: float32 [343, 343], replicated, may hold values from -2 to 2, as said below
- cell_scale: float32 [96], P('dom'), may hold values from 0.5 to 2
- potential: float32 [16384], P('dom'), may hold values from 0 to 2
- inv_mass_sqrt: float32 [16384], P('dom'), may hold values from 0.25 to 1.75
- cell_nodes: int32 [96, 343], P('dom'), may hold values from 0 to 1151, as said below
- shared_nodes: int32 [2048], P('dom'), may hold values from 0 to 1023, as said below
Outputs:
- filtered: float32 [128, 16384], P('band', 'dom')
- margin: float32 [128, 128], P('band')
The draws below stay inside these ranges and needn't reach their ends.
Inputs may be any that keep to these rules, and one draw needn't show every extreme that they name: `stiffness`: symmetric. `cell_nodes`: in the cells of a subdomain, an entry below 1024 is one of its own nodes and an entry l of 1024 or more stands for entry l - 1024 of the next subdomain's (cyclically) shared_nodes list; every value from 0 to 1151 occurs in the subdomain's cells. `shared_nodes`: the 128 entries of each subdomain are distinct.
All inputs are finite; a program needn't handle non-finite values.
Results may differ from the reference program's by a relative error of at most 0.0001.
Values sent between devices are 32-bit elements; how exact they have to be, the bound alone decides.
A program may use at most 64 MiB of HBM per device.

```python
import math
import jax
import jax.numpy as jnp
from jax import lax

NPC = 343
BLOCK = 64
DEGREE = 3
NODES_DEV = 1024
SHARED = 128
CELLS_DEV = 6
STATES = 128
NODES = 16384
CELLS = 96
N_BAND = 2
N_DOM = 16


def draw_stiffness(key, part):
    entries = jnp.clip(jax.random.normal(key, (NPC, NPC), jnp.float32), -4.0, 4.0)
    entries = entries / jnp.sqrt(jnp.float32(NPC))
    return (entries + entries.T) / jnp.sqrt(jnp.float32(2.0))


def draw_cell_nodes(key, part):
    local_count = NODES_DEV + SHARED
    slot_count = CELLS_DEV * NPC

    def one_domain(sub_key):
        key_first, key_second, key_third = jax.random.split(sub_key, 3)
        covering = jax.random.permutation(key_first, local_count).astype(jnp.int32)
        further = jax.random.randint(key_second, (slot_count - local_count,), 0, local_count, dtype=jnp.int32)
        joined = jnp.concatenate([covering, further])
        return jax.random.permutation(key_third, joined).reshape(CELLS_DEV, NPC)
    key_list = jax.random.split(jax.random.fold_in(key, 11), N_DOM)
    return jax.vmap(one_domain)(key_list).reshape(CELLS_DEV * N_DOM, NPC).astype(jnp.int32)


def draw_shared_nodes(key, part):

    def one_domain(sub_key):
        return jax.random.permutation(sub_key, NODES_DEV)[:SHARED].astype(jnp.int32)
    key_list = jax.random.split(jax.random.fold_in(key, 23), N_DOM)
    return jax.vmap(one_domain)(key_list).reshape(SHARED * N_DOM).astype(jnp.int32)


def levels(stream_key, extent, cuts, smallest, top_value):
    factor_of = 1.0
    for axis_at, parts in cuts:
        heights = jax.random.uniform(jax.random.fold_in(jax.random.fold_in(stream_key, 6), axis_at), (parts,), jnp.float32, smallest / len(cuts), top_value / len(cuts))
        factor_of = factor_of * jnp.repeat(jnp.exp(heights), extent[axis_at] // parts).reshape((-1,) + (1,) * (len(extent) - 1 - axis_at))
    return factor_of


def gaussian(own_key, extent, width, most, shards=(), held_as=jnp.bfloat16):
    gain = levels(own_key, extent, shards, -0.22, 0.18) if shards else 1.0
    values = jax.random.normal(own_key, extent, jnp.float32) * width * gain
    return jnp.minimum(jnp.maximum(values, -most), most).astype(held_as)


def setup_inputs(seed: int = 0) -> dict:
    arg_keys = jax.random.split(jax.random.key(seed), 8)
    states_in = gaussian(arg_keys[0], (STATES, NODES), 1.0, 6.0, ((0, 2), (1, 16)), jnp.float32)
    stiffness = draw_stiffness(jax.random.fold_in(arg_keys[7], 71), 0)
    cell_scale = jnp.clip(jnp.exp(math.log(2.0) - 1.3862944 * jax.random.uniform(arg_keys[2], (CELLS,), jnp.float32) ** levels(arg_keys[2], (CELLS,), ((0, 16),), -0.2, 0.2)), 0.5, 2.0)
    potential = jnp.clip(2.0 * jax.random.uniform(arg_keys[3], (NODES,), jnp.float32) ** levels(arg_keys[3], (NODES,), ((0, 16),), -0.2, 0.2), 0.0, 2.0)
    inv_mass_sqrt = jnp.clip(1.0 + 0.15 * jax.random.normal(arg_keys[4], (NODES,), jnp.float32), 0.25, 1.75)
    cell_nodes = draw_cell_nodes(jax.random.fold_in(arg_keys[7], 71), 0)
    shared_nodes = draw_shared_nodes(jax.random.fold_in(arg_keys[7], 71), 0)
    return dict(states_in=states_in, stiffness=stiffness, cell_scale=cell_scale, potential=potential, inv_mass_sqrt=inv_mass_sqrt, cell_nodes=cell_nodes, shared_nodes=shared_nodes)


center_shift = 1.0
half_width = 4.0

def global_nodes(cell_nodes, shared_nodes):
    count = cell_nodes.shape[0]
    holder = (jnp.arange(count, dtype=jnp.int32) // CELLS_DEV)[:, None]
    follower = (holder + 1) % N_DOM
    offset = jnp.clip(cell_nodes - NODES_DEV, 0, SHARED - 1)
    remote = shared_nodes[(follower * SHARED + offset).astype(jnp.int32)]
    inside = holder * NODES_DEV + cell_nodes
    outside = follower * NODES_DEV + remote
    return jnp.where(cell_nodes < NODES_DEV, inside, outside).astype(jnp.int32)

def operate(vector, stiffness, cell_scale, potential, inv_mass_sqrt, indices):
    scaled = vector * inv_mass_sqrt[None, :]
    cellwise = scaled[:, indices]
    product = jnp.einsum('bcj,kj->bck', cellwise, stiffness, precision=lax.Precision.HIGHEST, preferred_element_type=jnp.float32)
    product = product * cell_scale[None, :, None]
    summed = jnp.zeros_like(vector).at[:, indices].add(product)
    return inv_mass_sqrt[None, :] * summed + potential[None, :] * vector

def reference(states_in, stiffness, cell_scale, potential, inv_mass_sqrt, cell_nodes, shared_nodes):
    indices = global_nodes(cell_nodes, shared_nodes)

    def apply_once(vector):
        return operate(vector, stiffness, cell_scale, potential, inv_mass_sqrt, indices)

    def filter_block(block_states):
        previous = block_states
        current = (apply_once(block_states) - center_shift * block_states) / half_width
        for degree_step in range(DEGREE - 1):
            following = 2.0 * (apply_once(current) - center_shift * current) / half_width - previous
            previous = current
            current = following
        return current
    blocks = states_in.reshape(N_BAND, BLOCK, states_in.shape[1])
    filtered = lax.map(filter_block, blocks).reshape(STATES, states_in.shape[1])
    margin = jnp.dot(filtered, filtered.T, precision=lax.Precision.HIGHEST, preferred_element_type=jnp.float32)
    margin = margin / (NODES_DEV * N_DOM)
    return (filtered, margin)
```

```python
import functools

import jax
import jax.numpy as jnp
from jax import lax
from jax.experimental import pallas as pl
from jax.experimental.pallas import tpu as pltpu
from jax.sharding import PartitionSpec as P

DEGREE = 3
CENTER = 1.0
HALF_WIDTH = 4.0
LANES = 128
PLACES = 2
CHUNKS = 2
F32, BF16 = jnp.float32, jnp.bfloat16


def stacked_parts(value):
    high = value.astype(BF16)
    low = (value - high.astype(F32)).astype(BF16)
    return jnp.concatenate([high, low], axis=0)


def folded(value):
    half = value.shape[0] // 2
    return value[:half] + value[half:]


def dot(a, b):
    return jnp.dot(a, b, preferred_element_type=F32)


def dot_nt(a, b):
    return lax.dot_general(a, b, (((1,), (1,)), ((), ())), preferred_element_type=F32)


def narrow(value):
    return value.astype(jnp.int16)


def one_hot(a, b):
    return jnp.where(a == b, jnp.array(1, BF16), jnp.array(0, BF16))


def kernel(
    n_band, n_dom,
    x_hbm, stiff_hbm, scale_hbm, pot_hbm, mass_hbm, cells_hbm, shared_hbm,
    filt_ref, margin_ref,
    x_ref, stiff_ref, scale_ref, pot_ref, mass_ref, cells_ref, shared_ref, load_sem,
    idx, stiff_pad, weight_main, weight_rest, gather, scatter, spread, lead,
    lead_send, lead_recv, ret_send, ret_recv, part_send, part_recv,
    uu, yy, xx, zz, block_send, block_recv, last_cross,
    own_send, own_recv, own_all, cross_send, cross_all, final,
    lead_sem, ret_sem, part_sem, cross_last_sem, block_sem,
    own_pair_sem, own_line_sem, cross_sem, final_sem,
):
    rows, owned = x_ref.shape
    cells, npc = cells_ref.shape
    shared = shared_ref.shape[1]
    width = idx.shape[1]
    main = weight_main.shape[1]
    rest = width - main
    local = owned + shared
    lines = n_dom // PLACES
    band, dom = lax.axis_index("band"), lax.axis_index("dom")
    after, before = lax.rem(dom + 1, n_dom), lax.rem(dom + n_dom - 1, n_dom)
    place, line = lax.rem(dom, PLACES), dom // PLACES
    partner = line * PLACES + 1 - place

    def turned(value, by, size):
        return lax.rem(value + by, size)

    def at(b, d):
        return {"band": b, "dom": d}

    def spot(l, p):
        return turned(line, l, lines) * PLACES + p

    pairs = (
        (shared_hbm, shared_ref), (mass_hbm, mass_ref), (pot_hbm, pot_ref), (x_hbm, x_ref),
        (cells_hbm, cells_ref), (stiff_hbm, stiff_ref), (scale_hbm, scale_ref))
    loads = [pltpu.make_async_copy(src, dst, load_sem.at[k]) for k, (src, dst) in enumerate(pairs)]
    first_loads, later_loads = loads[:4], loads[4:]
    for load in loads:
        load.start()
    barrier = pltpu.get_barrier_semaphore()
    greeted = []
    for k in range(n_band):
        other = turned(band, k, n_band)
        opposite = turned(band, n_band - k, n_band)
        greeted += [at(other, after), at(opposite, before)]
        if k:
            greeted += [at(other, dom)] + [at(other, spot(l, 1 - place)) for l in range(lines)]
        else:
            greeted += [at(band, partner)] + [at(band, spot(l, place)) for l in range(1, lines)]
    for device in greeted:
        pl.semaphore_signal(barrier, inc=1, device_id=device)

    def remote(src, dst, sems, slot, device):
        return pltpu.make_async_remote_copy(
            src_ref=src, dst_ref=dst, send_sem=sems.at[0, slot], recv_sem=sems.at[1, slot],
            device_id=device, device_id_type=pl.DeviceIdType.MESH)

    started = []

    def send(*args):
        copy = remote(*args)
        copy.start()
        started.append(copy)
        return copy

    for load in first_loads:
        load.wait()
    mass, pot = mass_ref[...], pot_ref[...]
    shared_row = shared_ref[...]
    lead[0:rows, :] = x_ref[...]
    lead[rows:rows + 8, :] = jnp.concatenate(
        [mass, pot, jnp.zeros((6, owned), F32)], axis=0)
    wanted = jnp.broadcast_to(shared_row, (rows + 8, shared))
    lane_of, tile_of = wanted & (LANES - 1), wanted >> 7
    picked = None
    for k in range(owned // LANES):
        found = jnp.take_along_axis(lead[:, k * LANES:(k + 1) * LANES], lane_of, axis=1)
        picked = found if picked is None else jnp.where(tile_of == k, found, picked)
    lead_send[...] = picked
    pl.semaphore_wait(barrier, len(greeted))
    lead_copy = send(lead_send, lead_recv, lead_sem, 0, at(band, before))

    for load in later_loads:
        load.wait()
    uu[...] = stacked_parts(mass * x_ref[...])
    idx[...] = jnp.full(idx.shape, -1, jnp.int32)
    idx[0:cells, 0:npc] = cells_ref[...]
    node = narrow(lax.broadcasted_iota(jnp.int32, (LANES, width), 0))
    lane = narrow(lax.broadcasted_iota(jnp.int32, (width, LANES), 1))
    shared_col = jnp.broadcast_to(shared_row, (LANES, shared)).T
    shared_wide = narrow(jnp.concatenate([shared_col] * (width // LANES), axis=1))
    shared_tall = narrow(jnp.broadcast_to(shared_row, (width, shared)))
    for c in range(cells):
        span = slice(c * width, (c + 1) * width)
        slot_row = narrow(jnp.broadcast_to(idx[c:c + 1, :], (LANES, width)))
        for k in range(local // LANES):
            tile = slice(k * LANES, (k + 1) * LANES)
            gather[tile, span] = one_hot(node + jnp.int16(k * LANES), slot_row)
        gather[local:, span] = one_hot(shared_wide, slot_row)
        yy[:, span] = dot(uu[...], gather[0:owned, span])
    for c in range(cells):
        span = slice(c * width, (c + 1) * width)
        slot_col = narrow(jnp.broadcast_to(idx[c:c + 1, :], (LANES, width)).T)
        for k in range(local // LANES):
            tile = slice(k * LANES, (k + 1) * LANES)
            scatter[span, tile] = one_hot(lane + jnp.int16(k * LANES), slot_col)
        scatter[span, local:] = one_hot(shared_tall, slot_col)
    short = narrow(shared_col)
    lane = narrow(lax.broadcasted_iota(jnp.int32, (shared, LANES), 1))
    for k in range(owned // LANES):
        spread[:, k * LANES:(k + 1) * LANES] = one_hot(lane + jnp.int16(k * LANES), short)
    stiff_pad[...] = jnp.zeros(stiff_pad.shape, F32)
    stiff_pad[0:npc, 0:npc] = stiff_ref[...]
    stiff = stiff_pad[...]
    high = stiff.astype(BF16)
    low = (stiff - high.astype(F32)).astype(BF16)
    top, bottom = slice(0, main), slice(main, width)
    weight_main[...] = jnp.concatenate(
        [high[top, top], high[top, top]]
        + ([high[bottom, top], high[bottom, top]] if rest else [])
        + [low[top, top]] + ([low[bottom, top]] if rest else []), axis=0)
    if rest:
        edge = jnp.concatenate([high[top, bottom], low[top, bottom]], axis=1)
        corner = jnp.concatenate([high[bottom, bottom], low[bottom, bottom]], axis=1)
        weight_rest[...] = jnp.concatenate([edge, edge, corner, corner], axis=0)

    mass_shared, pot_shared = lead_send[rows:rows + 1, :], lead_send[rows + 1:rows + 2, :]
    partial = x_ref[...]
    current_shared = lead_send[0:rows, :]
    previous, previous_shared = None, None
    returned = None
    for t in range(DEGREE):
        last = t == DEGREE - 1
        factor = (1.0 if t == 0 else 2.0) / HALF_WIDTH
        if t:
            uu[...] = stacked_parts(mass * partial)
            for c in range(cells):
                span = slice(c * width, (c + 1) * width)
                yy[:, span] = dot(uu[...], gather[0:owned, span])
        if t == 0:
            lead_copy.wait_recv()
            mass_ghost = lead_recv[rows:rows + 1, :]
            ghost = lead_recv[0:rows, :]
            fix = None
            outside = stacked_parts(mass_ghost * ghost)
        else:
            ret_copy.wait_recv()
            part_copy.wait_recv()
            fix = earlier * mass_shared * ret_recv[t - 1]
            ghost = part_recv[t - 1] + earlier * mass_ghost * returned
            current_shared = part + fix
            outside = stacked_parts(
                jnp.concatenate([mass_ghost * ghost, mass_shared * fix], axis=1))
        reach = owned + outside.shape[1]
        for c in range(cells):
            span = slice(c * width, (c + 1) * width)
            y = folded(yy[:, span] + dot(outside, gather[owned:reach, span]))
            y_high = y.astype(BF16)
            y_low = (y - y_high.astype(F32)).astype(BF16)
            xx[c * rows:(c + 1) * rows, :] = jnp.concatenate(
                [y_high[:, top], y_low[:, top]]
                + ([y_high[:, bottom], y_low[:, bottom]] if rest else [])
                + [y_high], axis=1)
        z_main = dot(xx[...], weight_main[...])
        if rest:
            z_rest = dot(xx[:, 0:2 * width], weight_rest[...])
        for c in range(cells):
            state = slice(c * rows, (c + 1) * rows)
            z = z_main[state]
            if rest:
                z = jnp.concatenate([z, z_rest[state, 0:rest] + z_rest[state, rest:]], axis=1)
            zz[:, c * width:(c + 1) * width] = stacked_parts(z * scale_ref[c])
        border = folded(dot(zz[...], scatter[:, owned:]))
        returned = border[:, 0:shared]
        ret_send[t] = returned
        ret_copy = send(ret_send.at[t], ret_recv.at[t], ret_sem, t, at(band, after))
        if not last:
            part = factor * (
                mass_shared * border[:, shared:] + (pot_shared - CENTER) * current_shared)
            if t:
                part = part - previous_shared
            part_send[t] = part
            part_copy = send(part_send.at[t], part_recv.at[t], part_sem, t, at(band, before))
        current = partial
        if t:
            current = current + folded(dot(stacked_parts(fix), spread[...]))
        step = owned // CHUNKS if last else owned
        parts = []
        for j in range(owned // step):
            span = slice(j * step, (j + 1) * step)
            sums = folded(dot(zz[...], scatter[:, span]))
            piece = factor * (mass[:, span] * sums + (pot[:, span] - CENTER) * current[:, span])
            if t:
                piece = piece - previous[:, span]
            parts.append(piece)
            if last:
                block_send[j] = piece
                for k in range(1, n_band):
                    other = turned(band, k, n_band)
                    leads = place == jnp.where(band < other, 0, 1)

                    @pl.when(jnp.logical_not(leads))
                    def _():
                        remote(block_send.at[j], block_recv.at[n_band - k - 1, j], block_sem,
                               (k - 1) * CHUNKS + j, at(other, dom)).start()

                    if j == 0:
                        @pl.when(leads)
                        def _():
                            remote(ret_send.at[t], last_cross.at[n_band - k - 1], cross_last_sem,
                                   k - 1, at(other, after)).start()
        partial = jnp.concatenate(parts, axis=1) if last else parts[0]
        previous, previous_shared = current, current_shared
        earlier = factor

    scaling = 1.0 / (owned * n_dom)

    def packed(block):
        return jnp.concatenate([block[0:rows // 2], block[rows // 2:]], axis=1) * scaling

    def product(mine, theirs):
        both = folded(dot_nt(mine, theirs))
        return packed(both[:, 0:rows] + both[:, rows:])

    def mended(block, returned):
        fix = stacked_parts(earlier * mass_shared * returned)
        return block + folded(dot(fix, spread[...]))

    ret_copy.wait_recv()
    filtered = mended(partial, ret_recv[DEGREE - 1])
    filt_ref[...] = filtered
    uu[...] = stacked_parts(filtered)
    own_send[0] = product(uu[...], uu[...])
    pair_copy = send(own_send.at[0], own_recv, own_pair_sem, 0, at(band, partner))
    span = 2 * lines - 1
    for k in range(1, n_band):
        other = turned(band, k, n_band)
        leads = place == jnp.where(band < other, 0, 1)

        @pl.when(leads)
        def _():
            remote(ret_send.at[0], last_cross.at[k - 1], cross_last_sem, n_band - k - 1,
                   at(other, after)).wait_recv()
            for j in range(CHUNKS):
                remote(block_send.at[j], block_recv.at[k - 1, j], block_sem,
                       (n_band - k - 1) * CHUNKS + j, at(other, dom)).wait_recv()
            theirs = stacked_parts(mended(
                jnp.concatenate([block_recv[k - 1, j] for j in range(CHUNKS)], axis=1),
                last_cross[k - 1]))
            cross_send[k - 1, 0] = product(uu[...], theirs)
            cross_send[k - 1, 1] = product(theirs, uu[...])
            for l in range(lines):
                if l:
                    remote(cross_send.at[k - 1, 0], cross_all.at[k - 1, l], cross_sem,
                           (k - 1) * span + l - 1, at(band, spot(l, place))).start()
                remote(cross_send.at[k - 1, 1], cross_all.at[n_band - k - 1, lines + l],
                       cross_sem, (k - 1) * span + lines - 1 + l,
                       at(other, spot(l, 1 - place))).start()

    pair_copy.wait_recv()
    own_send[1] = own_send[0] + own_recv[...]
    gathers = place == jnp.where(band == 0, 1, 0)

    @pl.when(gathers)
    def _():
        for l in range(1, lines):
            remote(own_send.at[1], own_all.at[l], own_line_sem, l - 1,
                   at(band, spot(l, place))).start()

    for k in range(1, n_band):
        other = turned(band, k, n_band)
        leads = place == jnp.where(band < other, 0, 1)

        @pl.when(leads)
        def _():
            total = cross_send[k - 1, 0]
            waits = []
            for l in range(lines):
                if l:
                    waits.append(remote(
                        cross_send.at[k - 1, 0], cross_all.at[k - 1, l], cross_sem,
                        (k - 1) * span + l - 1, at(band, spot(l, place))))
                waits.append(remote(
                    cross_send.at[k - 1, 1], cross_all.at[k - 1, lines + l], cross_sem,
                    (n_band - k - 1) * span + lines - 1 + l, at(other, spot(l, 1 - place))))
            for copy in waits:
                copy.wait_recv()
            for l in range(1, 2 * lines):
                total = total + cross_all[k - 1, l]
            final[k] = total
            remote(final.at[k], final.at[k], final_sem, k, at(band, partner)).start()

    @pl.when(gathers)
    def _():
        for l in range(1, lines):
            remote(own_send.at[1], own_all.at[l], own_line_sem, l - 1,
                   at(band, spot(l, place))).wait()
        total = own_send[1]
        for l in range(1, lines):
            total = total + own_all[l]
        final[0] = total
        remote(final.at[0], final.at[0], final_sem, 0, at(band, partner)).start()

    for k in range(n_band):
        other = turned(band, k, n_band)
        holds = place == jnp.where(band < other, 0, 1) if k else gathers
        copy = remote(final.at[k], final.at[k], final_sem, k, at(band, partner))

        @pl.when(holds)
        def _():
            copy.wait_send()

        @pl.when(jnp.logical_not(holds))
        def _():
            copy.wait_recv()

    pieces = []
    for b in range(n_band):
        piece = final[0]
        for k in range(1, n_band):
            piece = jnp.where(turned(band, k, n_band) == b, final[k], piece)
        pieces.append(jnp.concatenate([piece[:, 0:rows], piece[:, rows:]], axis=0))
    margin_ref[...] = jnp.concatenate(pieces, axis=1)
    for copy in started:
        copy.wait_send()
    for k in range(1, n_band):
        other = turned(band, k, n_band)
        leads = place == jnp.where(band < other, 0, 1)

        @pl.when(leads)
        def _():
            remote(ret_send.at[0], last_cross.at[k - 1], cross_last_sem, k - 1,
                   at(other, after)).wait_send()
            for l in range(lines):
                if l:
                    remote(cross_send.at[k - 1, 0], cross_all.at[k - 1, l], cross_sem,
                           (k - 1) * span + l - 1, at(band, spot(l, place))).wait_send()
                remote(cross_send.at[k - 1, 1], cross_all.at[k - 1, lines + l], cross_sem,
                       (k - 1) * span + lines - 1 + l,
                       at(other, spot(l, 1 - place))).wait_send()

        @pl.when(jnp.logical_not(leads))
        def _():
            for j in range(CHUNKS):
                remote(block_send.at[j], block_recv.at[k - 1, j], block_sem,
                       (k - 1) * CHUNKS + j, at(other, dom)).wait_send()


def rounded_up(value):
    return -(-value // LANES) * LANES


def per_device(
    n_band, n_dom,
    states_in, stiffness, cell_scale, potential, inv_mass_sqrt, cell_nodes, shared_nodes
):
    rows, owned = states_in.shape
    cells, npc = cell_nodes.shape
    shared = shared_nodes.shape[0]
    width = rounded_up(npc)
    nodes = owned + 2 * shared
    states = n_band * rows
    main = width // (2 * LANES) * 2 * LANES
    rest = width - main
    lines = n_dom // PLACES
    others = n_band - 1
    block = (rows // 2, 2 * rows)
    pairs = lambda count: pltpu.SemaphoreType.DMA((2, count))
    vmem = pltpu.VMEM
    in_vmem = pl.BlockSpec(memory_space=pltpu.VMEM)
    return pl.pallas_call(
        functools.partial(kernel, n_band, n_dom),
        out_shape=(
            jax.ShapeDtypeStruct((rows, owned), F32),
            jax.ShapeDtypeStruct((rows, states), F32),
        ),
        in_specs=[pl.BlockSpec(memory_space=pltpu.HBM)] * 7,
        out_specs=(in_vmem, in_vmem),
        scratch_shapes=[
            vmem((rows, owned), F32),
            vmem((npc, npc), F32),
            pltpu.SMEM((cells,), F32),
            vmem((1, owned), F32),
            vmem((1, owned), F32),
            vmem((cells, npc), jnp.int32),
            vmem((1, shared), jnp.int32),
            pltpu.SemaphoreType.DMA((7,)),
            vmem((-(-cells // 8) * 8, width), jnp.int32),
            vmem((width, width), F32),
            vmem((3 * width, main), BF16),
            vmem((2 * width, 2 * max(rest, LANES)), BF16),
            vmem((nodes, cells * width), BF16),
            vmem((cells * width, nodes), BF16),
            vmem((shared, owned), BF16),
            vmem((rows + 8, owned), F32),
            vmem((rows + 8, shared), F32),
            vmem((rows + 8, shared), F32),
            vmem((DEGREE, rows, shared), F32),
            vmem((DEGREE, rows, shared), F32),
            vmem((DEGREE - 1, rows, shared), F32),
            vmem((DEGREE - 1, rows, shared), F32),
            vmem((2 * rows, owned), BF16),
            vmem((2 * rows, cells * width), F32),
            vmem((cells * rows, 3 * width), BF16),
            vmem((2 * rows, cells * width), BF16),
            vmem((CHUNKS, rows, owned // CHUNKS), F32),
            vmem((others, CHUNKS, rows, owned // CHUNKS), F32),
            vmem((others, rows, shared), F32),
            vmem((2, *block), F32),
            vmem(block, F32),
            vmem((lines, *block), F32),
            vmem((others, 2, *block), F32),
            vmem((others, 2 * lines, *block), F32),
            vmem((n_band, *block), F32),
            pairs(1),
            pairs(DEGREE),
            pairs(DEGREE - 1),
            pairs(others),
            pairs(others * CHUNKS),
            pairs(1),
            pairs(lines - 1),
            pairs(others * (2 * lines - 1)),
            pairs(n_band),
        ],
        compiler_params=pltpu.CompilerParams(collective_id=0, has_side_effects=True, vmem_limit_bytes=28 << 20),
    )(*[pltpu.with_memory_space_constraint(value, pltpu.HBM) for value in (
        states_in, stiffness, cell_scale, potential[None, :], inv_mass_sqrt[None, :],
        cell_nodes, shared_nodes[None, :],
    )])


def solution(mesh):
    n_band, n_dom = mesh.shape["band"], mesh.shape["dom"]
    return jax.shard_map(
        functools.partial(per_device, n_band, n_dom),
        mesh=mesh,
        in_specs=(P("band", "dom"), P(), P("dom"), P("dom"), P("dom"), P("dom", None), P("dom")),
        out_specs=(P("band", "dom"), P("band", None)),
        check_vma=False,
    )
```

```python
import functools

import jax
import jax.numpy as jnp
from jax import lax
from jax.experimental import pallas as pl
from jax.experimental.pallas import tpu as pltpu
from jax.sharding import PartitionSpec as P

DEGREE = 3
CENTER = 1.0
HALF_WIDTH = 4.0
LANES = 128
PLACES = 2
CHUNKS = 4
F32, BF16 = jnp.float32, jnp.bfloat16


def stacked_parts(value):
    high = value.astype(BF16)
    low = (value - high.astype(F32)).astype(BF16)
    return jnp.concatenate([high, low], axis=0)


def folded(value):
    half = value.shape[0] // 2
    return value[:half] + value[half:]


def dot(a, b):
    return jnp.dot(a, b, preferred_element_type=F32)


def dot_nt(a, b):
    return lax.dot_general(a, b, (((1,), (1,)), ((), ())), preferred_element_type=F32)


def narrow(value):
    return value.astype(jnp.int16)


def one_hot(a, b):
    return jnp.where(a == b, jnp.array(1, BF16), jnp.array(0, BF16))


def kernel(
    n_band, n_dom,
    x_hbm, stiff_hbm, scale_hbm, pot_hbm, mass_hbm, cells_hbm, shared_hbm,
    filt_ref, margin_ref,
    x_ref, stiff_ref, scale_ref, pot_ref, mass_ref, cells_ref, shared_ref, load_sem,
    idx, stiff_pad, weight_main, weight_rest, gather, scatter, spread, lead,
    lead_send, lead_recv, ret_send, ret_recv, part_send, part_recv,
    uu, yy, xx, zz, block_send, block_recv, last_cross,
    own_send, own_recv, own_all, cross_send, cross_all, final,
    lead_sem, ret_sem, part_sem, cross_last_sem, block_sem,
    own_pair_sem, own_line_sem, cross_sem, final_sem, known_sem,
):
    rows, owned = x_ref.shape
    cells, npc = cells_ref.shape
    shared = shared_ref.shape[1]
    width = idx.shape[1]
    main = weight_main.shape[1]
    rest = width - main
    local = owned + shared
    lines = n_dom // PLACES
    band, dom = lax.axis_index("band"), lax.axis_index("dom")
    after, before = lax.rem(dom + 1, n_dom), lax.rem(dom + n_dom - 1, n_dom)
    place, line = lax.rem(dom, PLACES), dom // PLACES
    partner = line * PLACES + 1 - place

    def turned(value, by, size):
        return lax.rem(value + by, size)

    def at(b, d):
        return {"band": b, "dom": d}

    def spot(l, p):
        return turned(line, l, lines) * PLACES + p

    pairs = (
        (shared_hbm, shared_ref), (mass_hbm, mass_ref), (pot_hbm, pot_ref), (x_hbm, x_ref),
        (cells_hbm, cells_ref), (stiff_hbm, stiff_ref), (scale_hbm, scale_ref))
    loads = [pltpu.make_async_copy(src, dst, load_sem.at[k]) for k, (src, dst) in enumerate(pairs)]
    first_loads, later_loads = loads[:4], loads[4:]
    barrier = pltpu.get_barrier_semaphore()
    others = [at(turned(band, k, n_band), dom) for k in range(1, n_band)]
    greeted = [at(band, after), at(band, before)] + others
    for device in greeted:
        pl.semaphore_signal(barrier, inc=1, device_id=device)
    for load in loads:
        load.start()

    rounds = []
    reach = 1
    while reach * 4 <= n_dom or not rounds:
        there = [at(band, lax.rem(dom + reach, n_dom)), at(band, lax.rem(dom + n_dom - reach, n_dom))]
        rounds.append(there + (others if reach == 1 else []))
        reach *= 2

    def tell(r):
        for device in rounds[r]:
            pl.semaphore_signal(known_sem.at[r], inc=1, device_id=device)

    def learn(r):
        pl.semaphore_wait(known_sem.at[r], len(rounds[r]))

    def remote(src, dst, sems, slot, device):
        return pltpu.make_async_remote_copy(
            src_ref=src, dst_ref=dst, send_sem=sems.at[0, slot], recv_sem=sems.at[1, slot],
            device_id=device, device_id_type=pl.DeviceIdType.MESH)

    started = []

    def send(*args):
        copy = remote(*args)
        copy.start()
        started.append(copy)
        return copy

    for load in first_loads:
        load.wait()
    mass, pot = mass_ref[...], pot_ref[...]
    shared_row = shared_ref[...]
    lead[0:rows, :] = x_ref[...]
    lead[rows:rows + 8, :] = jnp.concatenate(
        [mass, pot, jnp.zeros((6, owned), F32)], axis=0)
    wanted = jnp.broadcast_to(shared_row, (rows + 8, shared))
    lane_of, tile_of = wanted & (LANES - 1), wanted >> 7
    picked = None
    for k in range(owned // LANES):
        found = jnp.take_along_axis(lead[:, k * LANES:(k + 1) * LANES], lane_of, axis=1)
        picked = found if picked is None else jnp.where(tile_of == k, found, picked)
    lead_send[...] = picked
    pl.semaphore_wait(barrier, len(greeted))
    lead_copy = send(lead_send, lead_recv, lead_sem, 0, at(band, before))
    tell(0)

    for load in later_loads:
        load.wait()
    uu[...] = stacked_parts(mass * x_ref[...])
    idx[...] = jnp.full(idx.shape, -1, jnp.int32)
    idx[0:cells, 0:npc] = cells_ref[...]
    node = narrow(lax.broadcasted_iota(jnp.int32, (LANES, width), 0))
    lane = narrow(lax.broadcasted_iota(jnp.int32, (width, LANES), 1))
    shared_col = jnp.broadcast_to(shared_row, (LANES, shared)).T
    shared_wide = narrow(jnp.concatenate([shared_col] * (width // LANES), axis=1))
    shared_tall = narrow(jnp.broadcast_to(shared_row, (width, shared)))
    for c in range(cells):
        span = slice(c * width, (c + 1) * width)
        slot_row = narrow(jnp.broadcast_to(idx[c:c + 1, :], (LANES, width)))
        for k in range(local // LANES):
            tile = slice(k * LANES, (k + 1) * LANES)
            gather[tile, span] = one_hot(node + jnp.int16(k * LANES), slot_row)
        gather[local:, span] = one_hot(shared_wide, slot_row)
        yy[:, span] = dot(uu[...], gather[0:owned, span])
    for c in range(cells):
        span = slice(c * width, (c + 1) * width)
        slot_col = narrow(jnp.broadcast_to(idx[c:c + 1, :], (LANES, width)).T)
        for k in range(local // LANES):
            tile = slice(k * LANES, (k + 1) * LANES)
            scatter[span, tile] = one_hot(lane + jnp.int16(k * LANES), slot_col)
        scatter[span, local:] = one_hot(shared_tall, slot_col)
    short = narrow(shared_col)
    lane = narrow(lax.broadcasted_iota(jnp.int32, (shared, LANES), 1))
    for k in range(owned // LANES):
        spread[:, k * LANES:(k + 1) * LANES] = one_hot(lane + jnp.int16(k * LANES), short)
    stiff_pad[...] = jnp.zeros(stiff_pad.shape, F32)
    stiff_pad[0:npc, 0:npc] = stiff_ref[...]
    stiff = stiff_pad[...]
    high = stiff.astype(BF16)
    low = (stiff - high.astype(F32)).astype(BF16)
    top, bottom = slice(0, main), slice(main, width)
    weight_main[...] = jnp.concatenate(
        [high[top, top], high[top, top]]
        + ([high[bottom, top], high[bottom, top]] if rest else [])
        + [low[top, top]] + ([low[bottom, top]] if rest else []), axis=0)
    if rest:
        edge = jnp.concatenate([high[top, bottom], low[top, bottom]], axis=1)
        corner = jnp.concatenate([high[bottom, bottom], low[bottom, bottom]], axis=1)
        weight_rest[...] = jnp.concatenate([edge, edge, corner, corner], axis=0)

    mass_shared, pot_shared = lead_send[rows:rows + 1, :], lead_send[rows + 1:rows + 2, :]
    partial = x_ref[...]
    current_shared = lead_send[0:rows, :]
    previous, previous_shared = None, None
    returned = None
    for t in range(DEGREE):
        last = t == DEGREE - 1
        factor = (1.0 if t == 0 else 2.0) / HALF_WIDTH
        if t:
            uu[...] = stacked_parts(mass * partial)
            for c in range(cells):
                span = slice(c * width, (c + 1) * width)
                yy[:, span] = dot(uu[...], gather[0:owned, span])
        if t == 0:
            lead_copy.wait_recv()
            learn(0)
            if len(rounds) > 1:
                tell(1)
            mass_ghost = lead_recv[rows:rows + 1, :]
            ghost = lead_recv[0:rows, :]
            fix = None
            outside = stacked_parts(mass_ghost * ghost)
        else:
            ret_copy.wait_recv()
            part_copy.wait_recv()
            for r in range(t, len(rounds) if t == DEGREE - 1 else t + 1):
                learn(r)
                if r + 1 < len(rounds):
                    tell(r + 1)
            fix = earlier * mass_shared * ret_recv[t - 1]
            ghost = part_recv[t - 1] + earlier * mass_ghost * returned
            current_shared = part + fix
            outside = stacked_parts(
                jnp.concatenate([mass_ghost * ghost, mass_shared * fix], axis=1))
        stop = owned + outside.shape[1]
        for c in range(cells):
            span = slice(c * width, (c + 1) * width)
            y = folded(yy[:, span] + dot(outside, gather[owned:stop, span]))
            y_high = y.astype(BF16)
            y_low = (y - y_high.astype(F32)).astype(BF16)
            xx[c * rows:(c + 1) * rows, :] = jnp.concatenate(
                [y_high[:, top], y_low[:, top]]
                + ([y_high[:, bottom], y_low[:, bottom]] if rest else [])
                + [y_high], axis=1)
        z_main = dot(xx[...], weight_main[...])
        if rest:
            z_rest = dot(xx[:, 0:2 * width], weight_rest[...])
        for c in range(cells):
            state = slice(c * rows, (c + 1) * rows)
            z = z_main[state]
            if rest:
                z = jnp.concatenate([z, z_rest[state, 0:rest] + z_rest[state, rest:]], axis=1)
            zz[:, c * width:(c + 1) * width] = stacked_parts(z * scale_ref[c])
        border = folded(dot(zz[...], scatter[:, owned:]))
        returned = border[:, 0:shared]
        ret_send[t] = returned
        ret_copy = send(ret_send.at[t], ret_recv.at[t], ret_sem, t, at(band, after))
        if last:
            for k in range(1, n_band):
                other = turned(band, k, n_band)

                @pl.when(place == jnp.where(band < other, 0, 1))
                def _():
                    remote(ret_send.at[t], last_cross.at[n_band - k - 1], cross_last_sem,
                           k - 1, at(other, after)).start()
        else:
            part = factor * (
                mass_shared * border[:, shared:] + (pot_shared - CENTER) * current_shared)
            if t:
                part = part - previous_shared
            part_send[t] = part
            part_copy = send(part_send.at[t], part_recv.at[t], part_sem, t, at(band, before))
        current = partial
        if t:
            current = current + folded(dot(stacked_parts(fix), spread[...]))
        step = owned // CHUNKS if last else owned
        parts = []
        for j in range(owned // step):
            span = slice(j * step, (j + 1) * step)
            sums = folded(dot(zz[...], scatter[:, span]))
            piece = factor * (mass[:, span] * sums + (pot[:, span] - CENTER) * current[:, span])
            if t:
                piece = piece - previous[:, span]
            parts.append(piece)
            if last:
                block_send[j] = piece
                for k in range(1, n_band):
                    other = turned(band, k, n_band)
                    leads = place == jnp.where(band < other, 0, 1)

                    @pl.when(jnp.logical_not(leads))
                    def _():
                        remote(block_send.at[j], block_recv.at[n_band - k - 1, j], block_sem,
                               (k - 1) * CHUNKS + j, at(other, dom)).start()
        partial = jnp.concatenate(parts, axis=1) if last else parts[0]
        previous, previous_shared = current, current_shared
        earlier = factor

    scaling = 1.0 / (owned * n_dom)

    def packed(block):
        return jnp.concatenate([block[0:rows // 2], block[rows // 2:]], axis=1) * scaling

    def product(mine, theirs):
        both = folded(dot_nt(mine, theirs))
        return packed(both[:, 0:rows] + both[:, rows:])

    def mended(block, returned):
        fix = stacked_parts(earlier * mass_shared * returned)
        return block + folded(dot(fix, spread[...]))

    ret_copy.wait_recv()
    filtered = mended(partial, ret_recv[DEGREE - 1])
    filt_ref[...] = filtered
    uu[...] = stacked_parts(filtered)
    own_send[0] = product(uu[...], uu[...])
    pair_copy = send(own_send.at[0], own_recv, own_pair_sem, 0, at(band, partner))
    span = 2 * lines - 1
    for k in range(1, n_band):
        other = turned(band, k, n_band)
        leads = place == jnp.where(band < other, 0, 1)

        @pl.when(leads)
        def _():
            remote(ret_send.at[0], last_cross.at[k - 1], cross_last_sem, n_band - k - 1,
                   at(other, after)).wait_recv()
            for j in range(CHUNKS):
                remote(block_send.at[j], block_recv.at[k - 1, j], block_sem,
                       (n_band - k - 1) * CHUNKS + j, at(other, dom)).wait_recv()
            theirs = stacked_parts(mended(
                jnp.concatenate([block_recv[k - 1, j] for j in range(CHUNKS)], axis=1),
                last_cross[k - 1]))
            cross_send[k - 1, 0] = product(uu[...], theirs)
            cross_send[k - 1, 1] = product(theirs, uu[...])
            for l in range(lines):
                if l:
                    remote(cross_send.at[k - 1, 0], cross_all.at[k - 1, l], cross_sem,
                           (k - 1) * span + l - 1, at(band, spot(l, place))).start()
                remote(cross_send.at[k - 1, 1], cross_all.at[n_band - k - 1, lines + l],
                       cross_sem, (k - 1) * span + lines - 1 + l,
                       at(other, spot(l, 1 - place))).start()

    pair_copy.wait_recv()
    own_send[1] = own_send[0] + own_recv[...]
    gathers = place == jnp.where(band == 0, 1, 0)

    @pl.when(gathers)
    def _():
        for l in range(1, lines):
            remote(own_send.at[1], own_all.at[l], own_line_sem, l - 1,
                   at(band, spot(l, place))).start()

    for k in range(1, n_band):
        other = turned(band, k, n_band)
        leads = place == jnp.where(band < other, 0, 1)

        @pl.when(leads)
        def _():
            total = cross_send[k - 1, 0]
            waits = []
            for l in range(lines):
                if l:
                    waits.append(remote(
                        cross_send.at[k - 1, 0], cross_all.at[k - 1, l], cross_sem,
                        (k - 1) * span + l - 1, at(band, spot(l, place))))
                waits.append(remote(
                    cross_send.at[k - 1, 1], cross_all.at[k - 1, lines + l], cross_sem,
                    (n_band - k - 1) * span + lines - 1 + l, at(other, spot(l, 1 - place))))
            for copy in waits:
                copy.wait_recv()
            for l in range(1, 2 * lines):
                total = total + cross_all[k - 1, l]
            final[k] = total
            remote(final.at[k], final.at[k], final_sem, k, at(band, partner)).start()

    @pl.when(gathers)
    def _():
        for l in range(1, lines):
            remote(own_send.at[1], own_all.at[l], own_line_sem, l - 1,
                   at(band, spot(l, place))).wait()
        total = own_send[1]
        for l in range(1, lines):
            total = total + own_all[l]
        final[0] = total
        remote(final.at[0], final.at[0], final_sem, 0, at(band, partner)).start()

    for k in range(n_band):
        other = turned(band, k, n_band)
        holds = place == jnp.where(band < other, 0, 1) if k else gathers
        copy = remote(final.at[k], final.at[k], final_sem, k, at(band, partner))

        @pl.when(holds)
        def _():
            copy.wait_send()

        @pl.when(jnp.logical_not(holds))
        def _():
            copy.wait_recv()

    pieces = []
    for b in range(n_band):
        piece = final[0]
        for k in range(1, n_band):
            piece = jnp.where(turned(band, k, n_band) == b, final[k], piece)
        pieces.append(jnp.concatenate([piece[:, 0:rows], piece[:, rows:]], axis=0))
    margin_ref[...] = jnp.concatenate(pieces, axis=1)
    for copy in started:
        copy.wait_send()
    for k in range(1, n_band):
        other = turned(band, k, n_band)
        leads = place == jnp.where(band < other, 0, 1)

        @pl.when(leads)
        def _():
            remote(ret_send.at[0], last_cross.at[k - 1], cross_last_sem, k - 1,
                   at(other, after)).wait_send()
            for l in range(lines):
                if l:
                    remote(cross_send.at[k - 1, 0], cross_all.at[k - 1, l], cross_sem,
                           (k - 1) * span + l - 1, at(band, spot(l, place))).wait_send()
                remote(cross_send.at[k - 1, 1], cross_all.at[k - 1, lines + l], cross_sem,
                       (k - 1) * span + lines - 1 + l,
                       at(other, spot(l, 1 - place))).wait_send()

        @pl.when(jnp.logical_not(leads))
        def _():
            for j in range(CHUNKS):
                remote(block_send.at[j], block_recv.at[k - 1, j], block_sem,
                       (k - 1) * CHUNKS + j, at(other, dom)).wait_send()


def finish(filt_ref, margin_ref, filt_out, margin_out, sem):
    copies = [
        pltpu.make_async_copy(filt_ref, filt_out, sem.at[0]),
        pltpu.make_async_copy(margin_ref, margin_out, sem.at[1])]
    for copy in copies:
        copy.start()
    for copy in copies:
        copy.wait()


def rounded_up(value):
    return -(-value // LANES) * LANES


def per_device(
    n_band, n_dom,
    states_in, stiffness, cell_scale, potential, inv_mass_sqrt, cell_nodes, shared_nodes
):
    rows, owned = states_in.shape
    cells, npc = cell_nodes.shape
    shared = shared_nodes.shape[0]
    width = rounded_up(npc)
    nodes = owned + 2 * shared
    states = n_band * rows
    main = width // (2 * LANES) * 2 * LANES
    rest = width - main
    lines = n_dom // PLACES
    others = n_band - 1
    block = (rows // 2, 2 * rows)
    pairs = lambda count: pltpu.SemaphoreType.DMA((2, count))
    vmem = pltpu.VMEM
    in_vmem = pl.BlockSpec(memory_space=pltpu.VMEM)
    found = pl.pallas_call(
        functools.partial(kernel, n_band, n_dom),
        out_shape=(
            jax.ShapeDtypeStruct((rows, owned), F32),
            jax.ShapeDtypeStruct((rows, states), F32),
        ),
        in_specs=[pl.BlockSpec(memory_space=pltpu.HBM)] * 7,
        out_specs=(in_vmem, in_vmem),
        scratch_shapes=[
            vmem((rows, owned), F32),
            vmem((npc, npc), F32),
            pltpu.SMEM((cells,), F32),
            vmem((1, owned), F32),
            vmem((1, owned), F32),
            vmem((cells, npc), jnp.int32),
            vmem((1, shared), jnp.int32),
            pltpu.SemaphoreType.DMA((7,)),
            vmem((-(-cells // 8) * 8, width), jnp.int32),
            vmem((width, width), F32),
            vmem((3 * width, main), BF16),
            vmem((2 * width, 2 * max(rest, LANES)), BF16),
            vmem((nodes, cells * width), BF16),
            vmem((cells * width, nodes), BF16),
            vmem((shared, owned), BF16),
            vmem((rows + 8, owned), F32),
            vmem((rows + 8, shared), F32),
            vmem((rows + 8, shared), F32),
            vmem((DEGREE, rows, shared), F32),
            vmem((DEGREE, rows, shared), F32),
            vmem((DEGREE - 1, rows, shared), F32),
            vmem((DEGREE - 1, rows, shared), F32),
            vmem((2 * rows, owned), BF16),
            vmem((2 * rows, cells * width), F32),
            vmem((cells * rows, 3 * width), BF16),
            vmem((2 * rows, cells * width), BF16),
            vmem((CHUNKS, rows, owned // CHUNKS), F32),
            vmem((others, CHUNKS, rows, owned // CHUNKS), F32),
            vmem((others, rows, shared), F32),
            vmem((2, *block), F32),
            vmem(block, F32),
            vmem((lines, *block), F32),
            vmem((others, 2, *block), F32),
            vmem((others, 2 * lines, *block), F32),
            vmem((n_band, *block), F32),
            pairs(1),
            pairs(DEGREE),
            pairs(DEGREE - 1),
            pairs(others),
            pairs(others * CHUNKS),
            pairs(1),
            pairs(lines - 1),
            pairs(others * (2 * lines - 1)),
            pairs(n_band),
            pltpu.SemaphoreType.REGULAR((max(n_dom.bit_length() - 2, 1),)),
        ],
        compiler_params=pltpu.CompilerParams(collective_id=0, has_side_effects=True, vmem_limit_bytes=28 << 20),
    )(*[pltpu.with_memory_space_constraint(value, pltpu.HBM) for value in (
        states_in, stiffness, cell_scale, potential[None, :], inv_mass_sqrt[None, :],
        cell_nodes, shared_nodes[None, :],
    )])
    return pl.pallas_call(
        finish,
        out_shape=tuple(jax.ShapeDtypeStruct(value.shape, F32) for value in found),
        in_specs=[in_vmem, in_vmem],
        out_specs=(pl.BlockSpec(memory_space=pltpu.HBM),) * 2,
        scratch_shapes=[pltpu.SemaphoreType.DMA((2,))],
    )(*[pltpu.with_memory_space_constraint(value, pltpu.VMEM) for value in found])


def solution(mesh):
    n_band, n_dom = mesh.shape["band"], mesh.shape["dom"]
    return jax.shard_map(
        functools.partial(per_device, n_band, n_dom),
        mesh=mesh,
        in_specs=(P("band", "dom"), P(), P("dom"), P("dom"), P("dom"), P("dom", None), P("dom")),
        out_specs=(P("band", "dom"), P("band", None)),
        check_vma=False,
    )
```

```python
import functools

import jax
import jax.numpy as jnp
from jax import lax
from jax.experimental import pallas as pl
from jax.experimental.pallas import tpu as pltpu
from jax.sharding import PartitionSpec as P

DEGREE = 3
CENTER = 1.0
HALF_WIDTH = 4.0
LANES = 128
PLACES = 2
CHUNKS = 4
F32, BF16 = jnp.float32, jnp.bfloat16


def stacked_parts(value):
    high = value.astype(BF16)
    low = (value - high.astype(F32)).astype(BF16)
    return jnp.concatenate([high, low], axis=0)


def folded(value):
    half = value.shape[0] // 2
    return value[:half] + value[half:]


def dot(a, b):
    return jnp.dot(a, b, preferred_element_type=F32)


def dot_nt(a, b):
    return lax.dot_general(a, b, (((1,), (1,)), ((), ())), preferred_element_type=F32)


def narrow(value):
    return value.astype(jnp.int16)


def one_hot(a, b):
    return jnp.where(a == b, jnp.array(1, BF16), jnp.array(0, BF16))


def kernel(
    n_band, n_dom,
    x_hbm, stiff_hbm, scale_hbm, pot_hbm, mass_hbm, cells_hbm, shared_hbm,
    filt_ref, margin_ref,
    x_ref, stiff_ref, scale_ref, pot_ref, mass_ref, cells_ref, shared_ref, load_sem,
    idx, stiff_pad, weight_main, weight_rest, gather, scatter, spread, lead,
    lead_send, lead_recv, ret_send, ret_recv, part_send, part_recv,
    uu, yy, xx, zz, tt, weight_edge, block_send, block_recv, last_cross,
    own_send, own_recv, own_all, cross_send, cross_all, final,
    lead_sem, ret_sem, part_sem, cross_last_sem, block_sem,
    own_pair_sem, own_line_sem, cross_sem, final_sem, known_sem,
):
    rows, owned = x_ref.shape
    cells, npc = cells_ref.shape
    shared = shared_ref.shape[1]
    width = idx.shape[1]
    main = weight_main.shape[1]
    rest = width - main
    local = owned + shared
    lines = n_dom // PLACES
    band, dom = lax.axis_index("band"), lax.axis_index("dom")
    after, before = lax.rem(dom + 1, n_dom), lax.rem(dom + n_dom - 1, n_dom)
    place, line = lax.rem(dom, PLACES), dom // PLACES
    partner = line * PLACES + 1 - place

    def turned(value, by, size):
        return lax.rem(value + by, size)

    def at(b, d):
        return {"band": b, "dom": d}

    def spot(l, p):
        return turned(line, l, lines) * PLACES + p

    pairs = (
        (shared_hbm, shared_ref), (mass_hbm, mass_ref), (pot_hbm, pot_ref), (x_hbm, x_ref),
        (cells_hbm, cells_ref), (stiff_hbm, stiff_ref), (scale_hbm, scale_ref))
    loads = [pltpu.make_async_copy(src, dst, load_sem.at[k]) for k, (src, dst) in enumerate(pairs)]
    first_loads, later_loads = loads[:4], loads[4:]
    barrier = pltpu.get_barrier_semaphore()
    others = [at(turned(band, k, n_band), dom) for k in range(1, n_band)]
    greeted = [at(band, after), at(band, before)] + others
    for device in greeted:
        pl.semaphore_signal(barrier, inc=1, device_id=device)
    for load in loads:
        load.start()

    rounds = []
    reach = 1
    while reach * 4 <= n_dom or not rounds:
        there = [at(band, lax.rem(dom + reach, n_dom)), at(band, lax.rem(dom + n_dom - reach, n_dom))]
        rounds.append(there + (others if reach == 1 else []))
        reach *= 2

    def tell(r):
        for device in rounds[r]:
            pl.semaphore_signal(known_sem.at[r], inc=1, device_id=device)

    def learn(r):
        pl.semaphore_wait(known_sem.at[r], len(rounds[r]))

    def remote(src, dst, sems, slot, device):
        return pltpu.make_async_remote_copy(
            src_ref=src, dst_ref=dst, send_sem=sems.at[0, slot], recv_sem=sems.at[1, slot],
            device_id=device, device_id_type=pl.DeviceIdType.MESH)

    started = []

    def send(*args):
        copy = remote(*args)
        copy.start()
        started.append(copy)
        return copy

    for load in first_loads:
        load.wait()
    mass, pot = mass_ref[...], pot_ref[...]
    shared_row = shared_ref[...]
    lead[0:rows, :] = x_ref[...]
    lead[rows:rows + 8, :] = jnp.concatenate(
        [mass, pot, jnp.zeros((6, owned), F32)], axis=0)
    wanted = jnp.broadcast_to(shared_row, (rows + 8, shared))
    lane_of, tile_of = wanted & (LANES - 1), wanted >> 7
    picked = None
    for k in range(owned // LANES):
        found = jnp.take_along_axis(lead[:, k * LANES:(k + 1) * LANES], lane_of, axis=1)
        picked = found if picked is None else jnp.where(tile_of == k, found, picked)
    lead_send[...] = picked
    pl.semaphore_wait(barrier, len(greeted))
    lead_copy = send(lead_send, lead_recv, lead_sem, 0, at(band, before))
    tell(0)

    for load in later_loads:
        load.wait()
    uu[...] = stacked_parts(mass * x_ref[...])
    idx[...] = jnp.full(idx.shape, -1, jnp.int32)
    idx[0:cells, 0:npc] = cells_ref[...]
    node = narrow(lax.broadcasted_iota(jnp.int32, (LANES, width), 0))
    lane = narrow(lax.broadcasted_iota(jnp.int32, (width, LANES), 1))
    shared_col = jnp.broadcast_to(shared_row, (LANES, shared)).T
    shared_wide = narrow(jnp.concatenate([shared_col] * (width // LANES), axis=1))
    shared_tall = narrow(jnp.broadcast_to(shared_row, (width, shared)))
    for c in range(cells):
        span = slice(c * width, (c + 1) * width)
        slot_row = narrow(jnp.broadcast_to(idx[c:c + 1, :], (LANES, width)))
        for k in range(local // LANES):
            tile = slice(k * LANES, (k + 1) * LANES)
            gather[tile, span] = one_hot(node + jnp.int16(k * LANES), slot_row)
        gather[local:, span] = one_hot(shared_wide, slot_row)
        yy[:, span] = dot(uu[...], gather[0:owned, span])
    for c in range(cells):
        span = slice(c * width, (c + 1) * width)
        slot_col = narrow(jnp.broadcast_to(idx[c:c + 1, :], (LANES, width)).T)
        for k in range(local // LANES):
            tile = slice(k * LANES, (k + 1) * LANES)
            scatter[span, tile] = one_hot(lane + jnp.int16(k * LANES), slot_col)
        scatter[span, local:] = one_hot(shared_tall, slot_col)
    short = narrow(shared_col)
    lane = narrow(lax.broadcasted_iota(jnp.int32, (shared, LANES), 1))
    for k in range(owned // LANES):
        spread[:, k * LANES:(k + 1) * LANES] = one_hot(lane + jnp.int16(k * LANES), short)
    stiff_pad[...] = jnp.zeros(stiff_pad.shape, F32)
    stiff_pad[0:npc, 0:npc] = stiff_ref[...]
    stiff = stiff_pad[...]
    high = stiff.astype(BF16)
    low = (stiff - high.astype(F32)).astype(BF16)
    top, bottom = slice(0, main), slice(main, width)
    weight_main[...] = jnp.concatenate([high[:, top], high[:, top], low[:, top]], axis=0)
    if rest:
        paired = jnp.concatenate([high[:, bottom], low[:, bottom]], axis=1)
        weight_rest[...] = jnp.concatenate([paired, paired], axis=0)

    def triple(value):
        value_high = value.astype(BF16)
        value_low = (value - value_high.astype(F32)).astype(BF16)
        return jnp.concatenate([value_high, value_low, value_high], axis=1)

    def wide(z_main, z_rest):
        if not rest:
            return z_main
        return jnp.concatenate([z_main, z_rest[:, 0:rest] + z_rest[:, rest:]], axis=1)

    def cell_products(outside):
        for c in range(cells):
            span = slice(c * width, (c + 1) * width)
            y = yy[:, span]
            if outside is not None:
                y = folded(y) + folded(dot(outside, gather[owned:owned + outside.shape[1], span]))
            else:
                y = folded(y)
            xx[c * rows:(c + 1) * rows, :] = triple(y)
        z_main = dot(xx[...], weight_main[...])
        z_rest = dot(xx[:, 0:2 * width], weight_rest[...]) if rest else None
        for c in range(cells):
            state = slice(c * rows, (c + 1) * rows)
            z = wide(z_main[state], z_rest[state] if rest else None)
            zz[:, c * width:(c + 1) * width] = stacked_parts(z * scale_ref[c])

    def border_sums():
        return folded(dot(zz[...], scatter[:, owned:]))

    for c in range(cells):
        span = slice(c * width, (c + 1) * width)
        picks = gather[owned:, span]
        z = wide(
            dot(jnp.concatenate([picks, picks], axis=1), weight_main[width:, :]),
            dot(picks, weight_rest[0:width, :]) if rest else None)
        tt[:, span] = stacked_parts(z * scale_ref[c])
    response = folded(dot(tt[...], scatter[:, owned:]))
    response_high = response.astype(BF16)
    response_low = (response - response_high.astype(F32)).astype(BF16)
    weight_edge[...] = jnp.concatenate([response_high, response_high, response_low], axis=0)

    mass_shared, pot_shared = lead_send[rows:rows + 1, :], lead_send[rows + 1:rows + 2, :]
    partial = x_ref[...]
    current_shared = lead_send[0:rows, :]
    previous, previous_shared = None, None
    returned = None
    for t in range(DEGREE):
        last = t == DEGREE - 1
        factor = (1.0 if t == 0 else 2.0) / HALF_WIDTH
        if t:
            uu[...] = stacked_parts(mass * partial)
            for c in range(cells):
                span = slice(c * width, (c + 1) * width)
                yy[:, span] = dot(uu[...], gather[0:owned, span])
        if not last:
            cell_products(None)
            inside = border_sums()
        if t == 0:
            lead_copy.wait_recv()
            learn(0)
            if len(rounds) > 1:
                tell(1)
            mass_ghost = lead_recv[rows:rows + 1, :]
            ghost = lead_recv[0:rows, :]
            fix = None
            outside = mass_ghost * ghost
        else:
            ret_copy.wait_recv()
            part_copy.wait_recv()
            for r in range(t, len(rounds) if last else t + 1):
                learn(r)
                if r + 1 < len(rounds):
                    tell(r + 1)
            fix = earlier * mass_shared * ret_recv[t - 1]
            ghost = part_recv[t - 1] + earlier * mass_ghost * returned
            current_shared = part + fix
            outside = jnp.concatenate([mass_ghost * ghost, mass_shared * fix], axis=1)
        if last:
            cell_products(stacked_parts(outside))
            border = border_sums()
        else:
            used = outside.shape[1]
            edge = jnp.concatenate(
                [weight_edge[k * 2 * shared:k * 2 * shared + used, :] for k in range(3)], axis=0)
            border = inside + dot(triple(outside), edge)
        returned = border[:, 0:shared]
        ret_send[t] = returned
        ret_copy = send(ret_send.at[t], ret_recv.at[t], ret_sem, t, at(band, after))
        if last:
            for k in range(1, n_band):
                other = turned(band, k, n_band)

                @pl.when(place == jnp.where(band < other, 0, 1))
                def _():
                    remote(ret_send.at[t], last_cross.at[n_band - k - 1], cross_last_sem,
                           k - 1, at(other, after)).start()
        else:
            part = factor * (
                mass_shared * border[:, shared:] + (pot_shared - CENTER) * current_shared)
            if t:
                part = part - previous_shared
            part_send[t] = part
            part_copy = send(part_send.at[t], part_recv.at[t], part_sem, t, at(band, before))
        if not last:
            cell_products(stacked_parts(outside))
        current = partial
        if t:
            current = current + folded(dot(stacked_parts(fix), spread[...]))
        step = owned // CHUNKS if last else owned
        parts = []
        for j in range(owned // step):
            span = slice(j * step, (j + 1) * step)
            sums = folded(dot(zz[...], scatter[:, span]))
            piece = factor * (mass[:, span] * sums + (pot[:, span] - CENTER) * current[:, span])
            if t:
                piece = piece - previous[:, span]
            parts.append(piece)
            if last:
                block_send[j] = piece
                for k in range(1, n_band):
                    other = turned(band, k, n_band)
                    leads = place == jnp.where(band < other, 0, 1)

                    @pl.when(jnp.logical_not(leads))
                    def _():
                        remote(block_send.at[j], block_recv.at[n_band - k - 1, j], block_sem,
                               (k - 1) * CHUNKS + j, at(other, dom)).start()
        partial = jnp.concatenate(parts, axis=1) if last else parts[0]
        previous, previous_shared = current, current_shared
        earlier = factor

    scaling = 1.0 / (owned * n_dom)

    def packed(block):
        return jnp.concatenate([block[0:rows // 2], block[rows // 2:]], axis=1) * scaling

    def product(mine, theirs):
        both = folded(dot_nt(mine, theirs))
        return packed(both[:, 0:rows] + both[:, rows:])

    def mended(block, returned):
        fix = stacked_parts(earlier * mass_shared * returned)
        return block + folded(dot(fix, spread[...]))

    ret_copy.wait_recv()
    filtered = mended(partial, ret_recv[DEGREE - 1])
    filt_ref[...] = filtered
    uu[...] = stacked_parts(filtered)
    own_send[0] = product(uu[...], uu[...])
    pair_copy = send(own_send.at[0], own_recv, own_pair_sem, 0, at(band, partner))
    span = 2 * lines - 1
    for k in range(1, n_band):
        other = turned(band, k, n_band)
        leads = place == jnp.where(band < other, 0, 1)

        @pl.when(leads)
        def _():
            remote(ret_send.at[0], last_cross.at[k - 1], cross_last_sem, n_band - k - 1,
                   at(other, after)).wait_recv()
            for j in range(CHUNKS):
                remote(block_send.at[j], block_recv.at[k - 1, j], block_sem,
                       (n_band - k - 1) * CHUNKS + j, at(other, dom)).wait_recv()
            theirs = stacked_parts(mended(
                jnp.concatenate([block_recv[k - 1, j] for j in range(CHUNKS)], axis=1),
                last_cross[k - 1]))
            cross_send[k - 1, 0] = product(uu[...], theirs)
            cross_send[k - 1, 1] = product(theirs, uu[...])
            for l in range(lines):
                if l:
                    remote(cross_send.at[k - 1, 0], cross_all.at[k - 1, l], cross_sem,
                           (k - 1) * span + l - 1, at(band, spot(l, place))).start()
                remote(cross_send.at[k - 1, 1], cross_all.at[n_band - k - 1, lines + l],
                       cross_sem, (k - 1) * span + lines - 1 + l,
                       at(other, spot(l, 1 - place))).start()

    pair_copy.wait_recv()
    own_send[1] = own_send[0] + own_recv[...]
    gathers = place == jnp.where(band == 0, 1, 0)

    @pl.when(gathers)
    def _():
        for l in range(1, lines):
            remote(own_send.at[1], own_all.at[l], own_line_sem, l - 1,
                   at(band, spot(l, place))).start()

    for k in range(1, n_band):
        other = turned(band, k, n_band)
        leads = place == jnp.where(band < other, 0, 1)

        @pl.when(leads)
        def _():
            total = cross_send[k - 1, 0]
            waits = []
            for l in range(lines):
                if l:
                    waits.append(remote(
                        cross_send.at[k - 1, 0], cross_all.at[k - 1, l], cross_sem,
                        (k - 1) * span + l - 1, at(band, spot(l, place))))
                waits.append(remote(
                    cross_send.at[k - 1, 1], cross_all.at[k - 1, lines + l], cross_sem,
                    (n_band - k - 1) * span + lines - 1 + l, at(other, spot(l, 1 - place))))
            for copy in waits:
                copy.wait_recv()
            for l in range(1, 2 * lines):
                total = total + cross_all[k - 1, l]
            final[k] = total
            remote(final.at[k], final.at[k], final_sem, k, at(band, partner)).start()

    @pl.when(gathers)
    def _():
        for l in range(1, lines):
            remote(own_send.at[1], own_all.at[l], own_line_sem, l - 1,
                   at(band, spot(l, place))).wait()
        total = own_send[1]
        for l in range(1, lines):
            total = total + own_all[l]
        final[0] = total
        remote(final.at[0], final.at[0], final_sem, 0, at(band, partner)).start()

    for k in range(n_band):
        other = turned(band, k, n_band)
        holds = place == jnp.where(band < other, 0, 1) if k else gathers
        copy = remote(final.at[k], final.at[k], final_sem, k, at(band, partner))

        @pl.when(holds)
        def _():
            copy.wait_send()

        @pl.when(jnp.logical_not(holds))
        def _():
            copy.wait_recv()

    pieces = []
    for b in range(n_band):
        piece = final[0]
        for k in range(1, n_band):
            piece = jnp.where(turned(band, k, n_band) == b, final[k], piece)
        pieces.append(jnp.concatenate([piece[:, 0:rows], piece[:, rows:]], axis=0))
    margin_ref[...] = jnp.concatenate(pieces, axis=1)
    for copy in started:
        copy.wait_send()
    for k in range(1, n_band):
        other = turned(band, k, n_band)
        leads = place == jnp.where(band < other, 0, 1)

        @pl.when(leads)
        def _():
            remote(ret_send.at[0], last_cross.at[k - 1], cross_last_sem, k - 1,
                   at(other, after)).wait_send()
            for l in range(lines):
                if l:
                    remote(cross_send.at[k - 1, 0], cross_all.at[k - 1, l], cross_sem,
                           (k - 1) * span + l - 1, at(band, spot(l, place))).wait_send()
                remote(cross_send.at[k - 1, 1], cross_all.at[k - 1, lines + l], cross_sem,
                       (k - 1) * span + lines - 1 + l,
                       at(other, spot(l, 1 - place))).wait_send()

        @pl.when(jnp.logical_not(leads))
        def _():
            for j in range(CHUNKS):
                remote(block_send.at[j], block_recv.at[k - 1, j], block_sem,
                       (k - 1) * CHUNKS + j, at(other, dom)).wait_send()


def finish(filt_ref, margin_ref, filt_out, margin_out, sem):
    copies = [
        pltpu.make_async_copy(filt_ref, filt_out, sem.at[0]),
        pltpu.make_async_copy(margin_ref, margin_out, sem.at[1])]
    for copy in copies:
        copy.start()
    for copy in copies:
        copy.wait()


def rounded_up(value):
    return -(-value // LANES) * LANES


def per_device(
    n_band, n_dom,
    states_in, stiffness, cell_scale, potential, inv_mass_sqrt, cell_nodes, shared_nodes
):
    rows, owned = states_in.shape
    cells, npc = cell_nodes.shape
    shared = shared_nodes.shape[0]
    width = rounded_up(npc)
    nodes = owned + 2 * shared
    states = n_band * rows
    main = width // (2 * LANES) * 2 * LANES
    rest = width - main
    lines = n_dom // PLACES
    others = n_band - 1
    block = (rows // 2, 2 * rows)
    pairs = lambda count: pltpu.SemaphoreType.DMA((2, count))
    vmem = pltpu.VMEM
    in_vmem = pl.BlockSpec(memory_space=pltpu.VMEM)
    found = pl.pallas_call(
        functools.partial(kernel, n_band, n_dom),
        out_shape=(
            jax.ShapeDtypeStruct((rows, owned), F32),
            jax.ShapeDtypeStruct((rows, states), F32),
        ),
        in_specs=[pl.BlockSpec(memory_space=pltpu.HBM)] * 7,
        out_specs=(in_vmem, in_vmem),
        scratch_shapes=[
            vmem((rows, owned), F32),
            vmem((npc, npc), F32),
            pltpu.SMEM((cells,), F32),
            vmem((1, owned), F32),
            vmem((1, owned), F32),
            vmem((cells, npc), jnp.int32),
            vmem((1, shared), jnp.int32),
            pltpu.SemaphoreType.DMA((7,)),
            vmem((-(-cells // 8) * 8, width), jnp.int32),
            vmem((width, width), F32),
            vmem((3 * width, main), BF16),
            vmem((2 * width, 2 * max(rest, LANES)), BF16),
            vmem((nodes, cells * width), BF16),
            vmem((cells * width, nodes), BF16),
            vmem((shared, owned), BF16),
            vmem((rows + 8, owned), F32),
            vmem((rows + 8, shared), F32),
            vmem((rows + 8, shared), F32),
            vmem((DEGREE, rows, shared), F32),
            vmem((DEGREE, rows, shared), F32),
            vmem((DEGREE - 1, rows, shared), F32),
            vmem((DEGREE - 1, rows, shared), F32),
            vmem((2 * rows, owned), BF16),
            vmem((2 * rows, cells * width), F32),
            vmem((cells * rows, 3 * width), BF16),
            vmem((2 * rows, cells * width), BF16),
            vmem((4 * shared, cells * width), BF16),
            vmem((6 * shared, 2 * shared), BF16),
            vmem((CHUNKS, rows, owned // CHUNKS), F32),
            vmem((others, CHUNKS, rows, owned // CHUNKS), F32),
            vmem((others, rows, shared), F32),
            vmem((2, *block), F32),
            vmem(block, F32),
            vmem((lines, *block), F32),
            vmem((others, 2, *block), F32),
            vmem((others, 2 * lines, *block), F32),
            vmem((n_band, *block), F32),
            pairs(1),
            pairs(DEGREE),
            pairs(DEGREE - 1),
            pairs(others),
            pairs(others * CHUNKS),
            pairs(1),
            pairs(lines - 1),
            pairs(others * (2 * lines - 1)),
            pairs(n_band),
            pltpu.SemaphoreType.REGULAR((max(n_dom.bit_length() - 2, 1),)),
        ],
        compiler_params=pltpu.CompilerParams(collective_id=0, has_side_effects=True, vmem_limit_bytes=44 << 20),
    )(*[pltpu.with_memory_space_constraint(value, pltpu.HBM) for value in (
        states_in, stiffness, cell_scale, potential[None, :], inv_mass_sqrt[None, :],
        cell_nodes, shared_nodes[None, :],
    )])
    return pl.pallas_call(
        finish,
        out_shape=tuple(jax.ShapeDtypeStruct(value.shape, F32) for value in found),
        in_specs=[in_vmem, in_vmem],
        out_specs=(pl.BlockSpec(memory_space=pltpu.HBM),) * 2,
        scratch_shapes=[pltpu.SemaphoreType.DMA((2,))],
    )(*[pltpu.with_memory_space_constraint(value, pltpu.VMEM) for value in found])


def solution(mesh):
    n_band, n_dom = mesh.shape["band"], mesh.shape["dom"]
    return jax.shard_map(
        functools.partial(per_device, n_band, n_dom),
        mesh=mesh,
        in_specs=(P("band", "dom"), P(), P("dom"), P("dom"), P("dom"), P("dom", None), P("dom")),
        out_specs=(P("band", "dom"), P("band", None)),
        check_vma=False,
    )
```

```python
import functools

import jax
import jax.numpy as jnp
from jax import lax
from jax.experimental import pallas as pl
from jax.experimental.pallas import tpu as pltpu
from jax.sharding import PartitionSpec as P

DEGREE = 3
CENTER = 1.0
HALF_WIDTH = 4.0
LANES = 128
PLACES = 2
CHUNKS = 4
F32, BF16 = jnp.float32, jnp.bfloat16


def stacked_parts(value):
    high = value.astype(BF16)
    low = (value - high.astype(F32)).astype(BF16)
    return jnp.concatenate([high, low], axis=0)


def folded(value):
    half = value.shape[0] // 2
    return value[:half] + value[half:]


def dot(a, b):
    return jnp.dot(a, b, preferred_element_type=F32)


def dot_nt(a, b):
    return lax.dot_general(a, b, (((1,), (1,)), ((), ())), preferred_element_type=F32)


def narrow(value):
    return value.astype(jnp.int16)


def one_hot(a, b):
    return jnp.where(a == b, jnp.array(1, BF16), jnp.array(0, BF16))


def kernel(
    n_band, n_dom,
    x_hbm, stiff_hbm, scale_hbm, pot_hbm, mass_hbm, cells_hbm, shared_hbm,
    filt_ref, margin_ref,
    x_ref, stiff_ref, scale_ref, pot_ref, mass_ref, cells_ref, shared_ref, load_sem,
    idx, stiff_pad, weight_main, weight_rest, gather, scatter, spread, lead,
    lead_send, lead_recv, ret_send, ret_recv, part_send, part_recv,
    uu, yy, xx, zz, tt, weight_edge, block_send, block_recv, last_cross,
    own_send, own_recv, own_all, cross_send, cross_all, final,
    lead_sem, ret_sem, part_sem, cross_last_sem, block_sem,
    own_pair_sem, own_line_sem, cross_sem, final_sem, known_sem,
):
    rows, owned = x_ref.shape
    cells, npc = cells_ref.shape
    shared = shared_ref.shape[1]
    width = idx.shape[1]
    main = weight_main.shape[1]
    rest = width - main
    local = owned + shared
    lines = n_dom // PLACES
    band, dom = lax.axis_index("band"), lax.axis_index("dom")
    after, before = lax.rem(dom + 1, n_dom), lax.rem(dom + n_dom - 1, n_dom)
    place, line = lax.rem(dom, PLACES), dom // PLACES
    partner = line * PLACES + 1 - place

    def turned(value, by, size):
        return lax.rem(value + by, size)

    def at(b, d):
        return {"band": b, "dom": d}

    def spot(l, p):
        return turned(line, l, lines) * PLACES + p

    pairs = (
        (shared_hbm, shared_ref), (mass_hbm, mass_ref), (pot_hbm, pot_ref), (x_hbm, x_ref),
        (cells_hbm, cells_ref), (stiff_hbm, stiff_ref), (scale_hbm, scale_ref))
    loads = [pltpu.make_async_copy(src, dst, load_sem.at[k]) for k, (src, dst) in enumerate(pairs)]
    first_loads, later_loads = loads[:4], loads[4:]
    barrier = pltpu.get_barrier_semaphore()
    others = [at(turned(band, k, n_band), dom) for k in range(1, n_band)]
    greeted = [at(band, after), at(band, before)] + others
    for device in greeted:
        pl.semaphore_signal(barrier, inc=1, device_id=device)
    for load in loads:
        load.start()

    rounds = []
    reach = 1
    while reach * 4 <= n_dom or not rounds:
        there = [at(band, lax.rem(dom + reach, n_dom)), at(band, lax.rem(dom + n_dom - reach, n_dom))]
        rounds.append(there + (others if reach == 1 else []))
        reach *= 2

    def tell(r):
        for device in rounds[r]:
            pl.semaphore_signal(known_sem.at[r], inc=1, device_id=device)

    def learn(r):
        pl.semaphore_wait(known_sem.at[r], len(rounds[r]))

    def remote(src, dst, sems, slot, device):
        return pltpu.make_async_remote_copy(
            src_ref=src, dst_ref=dst, send_sem=sems.at[0, slot], recv_sem=sems.at[1, slot],
            device_id=device, device_id_type=pl.DeviceIdType.MESH)

    started = []

    def send(*args):
        copy = remote(*args)
        copy.start()
        started.append(copy)
        return copy

    for load in first_loads:
        load.wait()
    mass, pot = mass_ref[...], pot_ref[...]
    shared_row = shared_ref[...]
    lead[0:rows, :] = x_ref[...]
    lead[rows:rows + 8, :] = jnp.concatenate(
        [mass, pot, jnp.zeros((6, owned), F32)], axis=0)
    wanted = jnp.broadcast_to(shared_row, (rows + 8, shared))
    lane_of, tile_of = wanted & (LANES - 1), wanted >> 7
    picked = None
    for k in range(owned // LANES):
        found = jnp.take_along_axis(lead[:, k * LANES:(k + 1) * LANES], lane_of, axis=1)
        picked = found if picked is None else jnp.where(tile_of == k, found, picked)
    lead_send[...] = picked
    pl.semaphore_wait(barrier, len(greeted))
    lead_copy = send(lead_send, lead_recv, lead_sem, 0, at(band, before))
    tell(0)

    for load in later_loads:
        load.wait()
    uu[...] = stacked_parts(mass * x_ref[...])
    idx[...] = jnp.full(idx.shape, -1, jnp.int32)
    idx[0:cells, 0:npc] = cells_ref[...]
    node = narrow(lax.broadcasted_iota(jnp.int32, (LANES, width), 0))
    lane = narrow(lax.broadcasted_iota(jnp.int32, (width, LANES), 1))
    shared_col = jnp.broadcast_to(shared_row, (LANES, shared)).T
    shared_wide = narrow(jnp.concatenate([shared_col] * (width // LANES), axis=1))
    shared_tall = narrow(jnp.broadcast_to(shared_row, (width, shared)))
    for c in range(cells):
        span = slice(c * width, (c + 1) * width)
        slot_row = narrow(jnp.broadcast_to(idx[c:c + 1, :], (LANES, width)))
        for k in range(local // LANES):
            tile = slice(k * LANES, (k + 1) * LANES)
            gather[tile, span] = one_hot(node + jnp.int16(k * LANES), slot_row)
        gather[local:, span] = one_hot(shared_wide, slot_row)
        yy[:, span] = dot(uu[...], gather[0:owned, span])
    for c in range(cells):
        span = slice(c * width, (c + 1) * width)
        slot_col = narrow(jnp.broadcast_to(idx[c:c + 1, :], (LANES, width)).T)
        for k in range(local // LANES):
            tile = slice(k * LANES, (k + 1) * LANES)
            scatter[span, tile] = one_hot(lane + jnp.int16(k * LANES), slot_col)
        scatter[span, local:] = one_hot(shared_tall, slot_col)
    short = narrow(shared_col)
    lane = narrow(lax.broadcasted_iota(jnp.int32, (shared, LANES), 1))
    for k in range(owned // LANES):
        spread[:, k * LANES:(k + 1) * LANES] = one_hot(lane + jnp.int16(k * LANES), short)
    stiff_pad[...] = jnp.zeros(stiff_pad.shape, F32)
    stiff_pad[0:npc, 0:npc] = stiff_ref[...]
    stiff = stiff_pad[...]
    high = stiff.astype(BF16)
    low = (stiff - high.astype(F32)).astype(BF16)
    top, bottom = slice(0, main), slice(main, width)
    weight_main[...] = jnp.concatenate([high[:, top], high[:, top], low[:, top]], axis=0)
    if rest:
        paired = jnp.concatenate([high[:, bottom], low[:, bottom]], axis=1)
        weight_rest[...] = jnp.concatenate([paired, paired], axis=0)

    def triple(value):
        value_high = value.astype(BF16)
        value_low = (value - value_high.astype(F32)).astype(BF16)
        return jnp.concatenate([value_high, value_low, value_high], axis=1)

    def wide(z_main, z_rest):
        if not rest:
            return z_main
        return jnp.concatenate([z_main, z_rest[:, 0:rest] + z_rest[:, rest:]], axis=1)

    def cell_products(outside):
        for c in range(cells):
            span = slice(c * width, (c + 1) * width)
            y = yy[:, span]
            if outside is not None:
                y = folded(y) + folded(dot(outside, gather[owned:owned + outside.shape[1], span]))
            else:
                y = folded(y)
            xx[c * rows:(c + 1) * rows, :] = triple(y)
        z_main = dot(xx[...], weight_main[...])
        z_rest = dot(xx[:, 0:2 * width], weight_rest[...]) if rest else None
        for c in range(cells):
            state = slice(c * rows, (c + 1) * rows)
            z = wide(z_main[state], z_rest[state] if rest else None)
            zz[:, c * width:(c + 1) * width] = stacked_parts(z * scale_ref[c])

    def border_sums():
        return folded(dot(zz[...], scatter[:, owned:]))

    for c in range(cells):
        span = slice(c * width, (c + 1) * width)
        picks = gather[owned:, span]
        z = wide(
            dot(jnp.concatenate([picks, picks], axis=1), weight_main[width:, :]),
            dot(picks, weight_rest[0:width, :]) if rest else None)
        tt[:, span] = stacked_parts(z * scale_ref[c])
    response = folded(dot(tt[...], scatter[:, owned:]))
    response_high = response.astype(BF16)
    response_low = (response - response_high.astype(F32)).astype(BF16)
    weight_edge[...] = jnp.concatenate([response_high, response_high, response_low], axis=0)

    mass_shared, pot_shared = lead_send[rows:rows + 1, :], lead_send[rows + 1:rows + 2, :]
    partial = x_ref[...]
    current_shared = lead_send[0:rows, :]
    previous, previous_shared = None, None
    returned = None
    for t in range(DEGREE):
        last = t == DEGREE - 1
        factor = (1.0 if t == 0 else 2.0) / HALF_WIDTH
        if t:
            uu[...] = stacked_parts(mass * partial)
            for c in range(cells):
                span = slice(c * width, (c + 1) * width)
                yy[:, span] = dot(uu[...], gather[0:owned, span])
        cell_products(None)
        inside = border_sums()
        if t == 0:
            lead_copy.wait_recv()
            learn(0)
            if len(rounds) > 1:
                tell(1)
            mass_ghost = lead_recv[rows:rows + 1, :]
            ghost = lead_recv[0:rows, :]
            fix = None
            outside = mass_ghost * ghost
        else:
            ret_copy.wait_recv()
            part_copy.wait_recv()
            for r in range(t, len(rounds) if last else t + 1):
                learn(r)
                if r + 1 < len(rounds):
                    tell(r + 1)
            fix = earlier * mass_shared * ret_recv[t - 1]
            ghost = part_recv[t - 1] + earlier * mass_ghost * returned
            current_shared = part + fix
            outside = jnp.concatenate([mass_ghost * ghost, mass_shared * fix], axis=1)
        used = outside.shape[1]
        edge = jnp.concatenate(
            [weight_edge[k * 2 * shared:k * 2 * shared + used, :] for k in range(3)], axis=0)
        border = inside + dot(triple(outside), edge)
        returned = border[:, 0:shared]
        ret_send[t] = returned
        ret_copy = send(ret_send.at[t], ret_recv.at[t], ret_sem, t, at(band, after))
        if last:
            for k in range(1, n_band):
                other = turned(band, k, n_band)

                @pl.when(place == jnp.where(band < other, 0, 1))
                def _():
                    remote(ret_send.at[t], last_cross.at[n_band - k - 1], cross_last_sem,
                           k - 1, at(other, after)).start()
        else:
            part = factor * (
                mass_shared * border[:, shared:] + (pot_shared - CENTER) * current_shared)
            if t:
                part = part - previous_shared
            part_send[t] = part
            part_copy = send(part_send.at[t], part_recv.at[t], part_sem, t, at(band, before))
        cell_products(stacked_parts(outside))
        current = partial
        if t:
            current = current + folded(dot(stacked_parts(fix), spread[...]))
        step = owned // CHUNKS if last else owned
        parts = []
        for j in range(owned // step):
            span = slice(j * step, (j + 1) * step)
            sums = folded(dot(zz[...], scatter[:, span]))
            piece = factor * (mass[:, span] * sums + (pot[:, span] - CENTER) * current[:, span])
            if t:
                piece = piece - previous[:, span]
            parts.append(piece)
            if last:
                block_send[j] = piece
                for k in range(1, n_band):
                    other = turned(band, k, n_band)
                    leads = place == jnp.where(band < other, 0, 1)

                    @pl.when(jnp.logical_not(leads))
                    def _():
                        remote(block_send.at[j], block_recv.at[n_band - k - 1, j], block_sem,
                               (k - 1) * CHUNKS + j, at(other, dom)).start()
        partial = jnp.concatenate(parts, axis=1) if last else parts[0]
        previous, previous_shared = current, current_shared
        earlier = factor

    scaling = 1.0 / (owned * n_dom)

    def packed(block):
        return jnp.concatenate([block[0:rows // 2], block[rows // 2:]], axis=1) * scaling

    def product(mine, theirs):
        both = folded(dot_nt(mine, theirs))
        return packed(both[:, 0:rows] + both[:, rows:])

    def mended(block, returned):
        fix = stacked_parts(earlier * mass_shared * returned)
        return block + folded(dot(fix, spread[...]))

    ret_copy.wait_recv()
    filtered = mended(partial, ret_recv[DEGREE - 1])
    filt_ref[...] = filtered
    uu[...] = stacked_parts(filtered)
    own_send[0] = product(uu[...], uu[...])
    pair_copy = send(own_send.at[0], own_recv, own_pair_sem, 0, at(band, partner))
    span = 2 * lines - 1
    for k in range(1, n_band):
        other = turned(band, k, n_band)
        leads = place == jnp.where(band < other, 0, 1)

        @pl.when(leads)
        def _():
            remote(ret_send.at[0], last_cross.at[k - 1], cross_last_sem, n_band - k - 1,
                   at(other, after)).wait_recv()
            fixes = stacked_parts(earlier * mass_shared * last_cross[k - 1])
            sums = [0.0, 0.0]
            for j in range(CHUNKS):
                remote(block_send.at[j], block_recv.at[k - 1, j], block_sem,
                       (n_band - k - 1) * CHUNKS + j, at(other, dom)).wait_recv()
                part = slice(j * step, (j + 1) * step)
                theirs = stacked_parts(
                    block_recv[k - 1, j] + folded(dot(fixes, spread[:, part])))
                mine = uu[:, part]
                sums[0] = sums[0] + folded(dot_nt(mine, theirs))
                sums[1] = sums[1] + folded(dot_nt(theirs, mine))
            for j in range(2):
                cross_send[k - 1, j] = packed(sums[j][:, 0:rows] + sums[j][:, rows:])
            for l in [*range(1, lines), 0]:
                off = jnp.where(2 * line < lines, lines - l, l) if l else 0
                if l:
                    remote(cross_send.at[k - 1, 0], cross_all.at[k - 1, off], cross_sem,
                           (k - 1) * span + off - 1, at(band, spot(off, place))).start()
                remote(cross_send.at[k - 1, 1], cross_all.at[n_band - k - 1, lines + off],
                       cross_sem, (k - 1) * span + lines - 1 + off,
                       at(other, spot(off, 1 - place))).start()

    pair_copy.wait_recv()
    own_send[1] = own_send[0] + own_recv[...]
    gathers = place == jnp.where(band == 0, 1, 0)

    @pl.when(gathers)
    def _():
        for l in range(1, lines):
            remote(own_send.at[1], own_all.at[l], own_line_sem, l - 1,
                   at(band, spot(l, place))).start()

    for k in range(1, n_band):
        other = turned(band, k, n_band)
        leads = place == jnp.where(band < other, 0, 1)

        @pl.when(leads)
        def _():
            total = cross_send[k - 1, 0]
            waits = []
            for l in range(lines):
                if l:
                    waits.append(remote(
                        cross_send.at[k - 1, 0], cross_all.at[k - 1, l], cross_sem,
                        (k - 1) * span + l - 1, at(band, spot(l, place))))
                waits.append(remote(
                    cross_send.at[k - 1, 1], cross_all.at[k - 1, lines + l], cross_sem,
                    (n_band - k - 1) * span + lines - 1 + l, at(other, spot(l, 1 - place))))
            for copy in waits:
                copy.wait_recv()
            for l in range(1, 2 * lines):
                total = total + cross_all[k - 1, l]
            final[k] = total
            remote(final.at[k], final.at[k], final_sem, k, at(band, partner)).start()

    @pl.when(gathers)
    def _():
        for l in range(1, lines):
            remote(own_send.at[1], own_all.at[l], own_line_sem, l - 1,
                   at(band, spot(l, place))).wait()
        total = own_send[1]
        for l in range(1, lines):
            total = total + own_all[l]
        final[0] = total
        remote(final.at[0], final.at[0], final_sem, 0, at(band, partner)).start()

    for k in range(n_band):
        other = turned(band, k, n_band)
        holds = place == jnp.where(band < other, 0, 1) if k else gathers
        copy = remote(final.at[k], final.at[k], final_sem, k, at(band, partner))

        @pl.when(holds)
        def _():
            copy.wait_send()

        @pl.when(jnp.logical_not(holds))
        def _():
            copy.wait_recv()

    pieces = []
    for b in range(n_band):
        piece = final[0]
        for k in range(1, n_band):
            piece = jnp.where(turned(band, k, n_band) == b, final[k], piece)
        pieces.append(jnp.concatenate([piece[:, 0:rows], piece[:, rows:]], axis=0))
    margin_ref[...] = jnp.concatenate(pieces, axis=1)
    for copy in started:
        copy.wait_send()
    for k in range(1, n_band):
        other = turned(band, k, n_band)
        leads = place == jnp.where(band < other, 0, 1)

        @pl.when(leads)
        def _():
            remote(ret_send.at[0], last_cross.at[k - 1], cross_last_sem, k - 1,
                   at(other, after)).wait_send()
            for l in range(lines):
                if l:
                    remote(cross_send.at[k - 1, 0], cross_all.at[k - 1, l], cross_sem,
                           (k - 1) * span + l - 1, at(band, spot(l, place))).wait_send()
                remote(cross_send.at[k - 1, 1], cross_all.at[k - 1, lines + l], cross_sem,
                       (k - 1) * span + lines - 1 + l,
                       at(other, spot(l, 1 - place))).wait_send()

        @pl.when(jnp.logical_not(leads))
        def _():
            for j in range(CHUNKS):
                remote(block_send.at[j], block_recv.at[k - 1, j], block_sem,
                       (k - 1) * CHUNKS + j, at(other, dom)).wait_send()


def finish(filt_ref, margin_ref, filt_out, margin_out, sem):
    copies = [
        pltpu.make_async_copy(filt_ref, filt_out, sem.at[0]),
        pltpu.make_async_copy(margin_ref, margin_out, sem.at[1])]
    for copy in copies:
        copy.start()
    for copy in copies:
        copy.wait()


def rounded_up(value):
    return -(-value // LANES) * LANES


def per_device(
    n_band, n_dom,
    states_in, stiffness, cell_scale, potential, inv_mass_sqrt, cell_nodes, shared_nodes
):
    rows, owned = states_in.shape
    cells, npc = cell_nodes.shape
    shared = shared_nodes.shape[0]
    width = rounded_up(npc)
    nodes = owned + 2 * shared
    states = n_band * rows
    main = width // (2 * LANES) * 2 * LANES
    rest = width - main
    lines = n_dom // PLACES
    others = n_band - 1
    block = (rows // 2, 2 * rows)
    pairs = lambda count: pltpu.SemaphoreType.DMA((2, count))
    vmem = pltpu.VMEM
    in_vmem = pl.BlockSpec(memory_space=pltpu.VMEM)
    found = pl.pallas_call(
        functools.partial(kernel, n_band, n_dom),
        out_shape=(
            jax.ShapeDtypeStruct((rows, owned), F32),
            jax.ShapeDtypeStruct((rows, states), F32),
        ),
        in_specs=[pl.BlockSpec(memory_space=pltpu.HBM)] * 7,
        out_specs=(in_vmem, in_vmem),
        scratch_shapes=[
            vmem((rows, owned), F32),
            vmem((npc, npc), F32),
            pltpu.SMEM((cells,), F32),
            vmem((1, owned), F32),
            vmem((1, owned), F32),
            vmem((cells, npc), jnp.int32),
            vmem((1, shared), jnp.int32),
            pltpu.SemaphoreType.DMA((7,)),
            vmem((-(-cells // 8) * 8, width), jnp.int32),
            vmem((width, width), F32),
            vmem((3 * width, main), BF16),
            vmem((2 * width, 2 * max(rest, LANES)), BF16),
            vmem((nodes, cells * width), BF16),
            vmem((cells * width, nodes), BF16),
            vmem((shared, owned), BF16),
            vmem((rows + 8, owned), F32),
            vmem((rows + 8, shared), F32),
            vmem((rows + 8, shared), F32),
            vmem((DEGREE, rows, shared), F32),
            vmem((DEGREE, rows, shared), F32),
            vmem((DEGREE - 1, rows, shared), F32),
            vmem((DEGREE - 1, rows, shared), F32),
            vmem((2 * rows, owned), BF16),
            vmem((2 * rows, cells * width), F32),
            vmem((cells * rows, 3 * width), BF16),
            vmem((2 * rows, cells * width), BF16),
            vmem((4 * shared, cells * width), BF16),
            vmem((6 * shared, 2 * shared), BF16),
            vmem((CHUNKS, rows, owned // CHUNKS), F32),
            vmem((others, CHUNKS, rows, owned // CHUNKS), F32),
            vmem((others, rows, shared), F32),
            vmem((2, *block), F32),
            vmem(block, F32),
            vmem((lines, *block), F32),
            vmem((others, 2, *block), F32),
            vmem((others, 2 * lines, *block), F32),
            vmem((n_band, *block), F32),
            pairs(1),
            pairs(DEGREE),
            pairs(DEGREE - 1),
            pairs(others),
            pairs(others * CHUNKS),
            pairs(1),
            pairs(lines - 1),
            pairs(others * (2 * lines - 1)),
            pairs(n_band),
            pltpu.SemaphoreType.REGULAR((max(n_dom.bit_length() - 2, 1),)),
        ],
        compiler_params=pltpu.CompilerParams(collective_id=0, has_side_effects=True, vmem_limit_bytes=44 << 20),
    )(*[pltpu.with_memory_space_constraint(value, pltpu.HBM) for value in (
        states_in, stiffness, cell_scale, potential[None, :], inv_mass_sqrt[None, :],
        cell_nodes, shared_nodes[None, :],
    )])
    return pl.pallas_call(
        finish,
        out_shape=tuple(jax.ShapeDtypeStruct(value.shape, F32) for value in found),
        in_specs=[in_vmem, in_vmem],
        out_specs=(pl.BlockSpec(memory_space=pltpu.HBM),) * 2,
        scratch_shapes=[pltpu.SemaphoreType.DMA((2,))],
    )(*[pltpu.with_memory_space_constraint(value, pltpu.VMEM) for value in found])


def solution(mesh):
    n_band, n_dom = mesh.shape["band"], mesh.shape["dom"]
    return jax.shard_map(
        functools.partial(per_device, n_band, n_dom),
        mesh=mesh,
        in_specs=(P("band", "dom"), P(), P("dom"), P("dom"), P("dom"), P("dom", None), P("dom")),
        out_specs=(P("band", "dom"), P("band", None)),
        check_vma=False,
    )
```

```python
import functools

import jax
import jax.numpy as jnp
from jax import lax
from jax.experimental import pallas as pl
from jax.experimental.pallas import tpu as pltpu
from jax.sharding import PartitionSpec as P

DEGREE = 3
CENTER = 1.0
HALF_WIDTH = 4.0
LANES = 128
PLACES = 2
CHUNKS = 4
F32, BF16 = jnp.float32, jnp.bfloat16


def stacked_parts(value):
    high = value.astype(BF16)
    low = (value - high.astype(F32)).astype(BF16)
    return jnp.concatenate([high, low], axis=0)


def folded(value):
    half = value.shape[0] // 2
    return value[:half] + value[half:]


def dot(a, b):
    return jnp.dot(a, b, preferred_element_type=F32)


def dot_nt(a, b):
    return lax.dot_general(a, b, (((1,), (1,)), ((), ())), preferred_element_type=F32)


def narrow(value):
    return value.astype(jnp.int16)


def one_hot(a, b):
    return jnp.where(a == b, jnp.array(1, BF16), jnp.array(0, BF16))


def kernel(
    n_band, n_dom,
    x_hbm, stiff_hbm, scale_hbm, pot_hbm, mass_hbm, cells_hbm, shared_hbm,
    filt_ref, margin_ref,
    x_ref, stiff_ref, scale_ref, pot_ref, mass_ref, cells_ref, shared_ref, load_sem,
    idx, stiff_pad, weight_main, weight_rest, gather, scatter, spread, lead,
    lead_send, lead_recv, ret_send, ret_recv, part_send, part_recv,
    uu, yy, xx, zz, tt, weight_edge, weight_own, block_send, block_recv, last_cross,
    own_send, own_recv, own_all, cross_send, cross_all, final,
    lead_sem, ret_sem, part_sem, cross_last_sem, block_sem,
    own_pair_sem, own_line_sem, cross_sem, final_sem, known_sem,
):
    rows, owned = x_ref.shape
    cells, npc = cells_ref.shape
    shared = shared_ref.shape[1]
    width = idx.shape[1]
    main = weight_main.shape[1]
    rest = width - main
    local = owned + shared
    lines = n_dom // PLACES
    band, dom = lax.axis_index("band"), lax.axis_index("dom")
    after, before = lax.rem(dom + 1, n_dom), lax.rem(dom + n_dom - 1, n_dom)
    place, line = lax.rem(dom, PLACES), dom // PLACES
    partner = line * PLACES + 1 - place

    def turned(value, by, size):
        return lax.rem(value + by, size)

    def at(b, d):
        return {"band": b, "dom": d}

    def spot(l, p):
        return turned(line, l, lines) * PLACES + p

    pairs = (
        (shared_hbm, shared_ref), (mass_hbm, mass_ref), (pot_hbm, pot_ref), (x_hbm, x_ref),
        (cells_hbm, cells_ref), (stiff_hbm, stiff_ref), (scale_hbm, scale_ref))
    loads = [pltpu.make_async_copy(src, dst, load_sem.at[k]) for k, (src, dst) in enumerate(pairs)]
    first_loads, later_loads = loads[:4], loads[4:]
    barrier = pltpu.get_barrier_semaphore()
    others = [at(turned(band, k, n_band), dom) for k in range(1, n_band)]
    greeted = [at(band, after), at(band, before)] + others
    for device in greeted:
        pl.semaphore_signal(barrier, inc=1, device_id=device)
    for load in loads:
        load.start()

    rounds = []
    reach = 1
    while reach * 4 <= n_dom or not rounds:
        there = [at(band, lax.rem(dom + reach, n_dom)), at(band, lax.rem(dom + n_dom - reach, n_dom))]
        rounds.append(there + (others if reach == 1 else []))
        reach *= 2

    def tell(r):
        for device in rounds[r]:
            pl.semaphore_signal(known_sem.at[r], inc=1, device_id=device)

    def learn(r):
        pl.semaphore_wait(known_sem.at[r], len(rounds[r]))

    def remote(src, dst, sems, slot, device):
        return pltpu.make_async_remote_copy(
            src_ref=src, dst_ref=dst, send_sem=sems.at[0, slot], recv_sem=sems.at[1, slot],
            device_id=device, device_id_type=pl.DeviceIdType.MESH)

    started = []

    def send(*args):
        copy = remote(*args)
        copy.start()
        started.append(copy)
        return copy

    for load in first_loads:
        load.wait()
    mass, pot = mass_ref[...], pot_ref[...]
    shared_row = shared_ref[...]
    lead[0:rows, :] = x_ref[...]
    lead[rows:rows + 8, :] = jnp.concatenate(
        [mass, pot, jnp.zeros((6, owned), F32)], axis=0)
    wanted = jnp.broadcast_to(shared_row, (rows + 8, shared))
    lane_of, tile_of = wanted & (LANES - 1), wanted >> 7
    picked = None
    for k in range(owned // LANES):
        found = jnp.take_along_axis(lead[:, k * LANES:(k + 1) * LANES], lane_of, axis=1)
        picked = found if picked is None else jnp.where(tile_of == k, found, picked)
    lead_send[...] = picked
    pl.semaphore_wait(barrier, len(greeted))
    lead_copy = send(lead_send, lead_recv, lead_sem, 0, at(band, before))
    tell(0)

    for load in later_loads:
        load.wait()
    uu[...] = stacked_parts(mass * x_ref[...])
    idx[...] = jnp.full(idx.shape, -1, jnp.int32)
    idx[0:cells, 0:npc] = cells_ref[...]
    node = narrow(lax.broadcasted_iota(jnp.int32, (LANES, width), 0))
    lane = narrow(lax.broadcasted_iota(jnp.int32, (width, LANES), 1))
    shared_col = jnp.broadcast_to(shared_row, (LANES, shared)).T
    shared_wide = narrow(jnp.concatenate([shared_col] * (width // LANES), axis=1))
    shared_tall = narrow(jnp.broadcast_to(shared_row, (width, shared)))
    for c in range(cells):
        span = slice(c * width, (c + 1) * width)
        slot_row = narrow(jnp.broadcast_to(idx[c:c + 1, :], (LANES, width)))
        for k in range(local // LANES):
            tile = slice(k * LANES, (k + 1) * LANES)
            gather[tile, span] = one_hot(node + jnp.int16(k * LANES), slot_row)
        gather[local:, span] = one_hot(shared_wide, slot_row)
        yy[:, span] = dot(uu[...], gather[0:owned, span])
    for c in range(cells):
        span = slice(c * width, (c + 1) * width)
        slot_col = narrow(jnp.broadcast_to(idx[c:c + 1, :], (LANES, width)).T)
        for k in range(local // LANES):
            tile = slice(k * LANES, (k + 1) * LANES)
            scatter[span, tile] = one_hot(lane + jnp.int16(k * LANES), slot_col)
        scatter[span, local:] = one_hot(shared_tall, slot_col)
    short = narrow(shared_col)
    lane = narrow(lax.broadcasted_iota(jnp.int32, (shared, LANES), 1))
    for k in range(owned // LANES):
        spread[:, k * LANES:(k + 1) * LANES] = one_hot(lane + jnp.int16(k * LANES), short)
    stiff_pad[...] = jnp.zeros(stiff_pad.shape, F32)
    stiff_pad[0:npc, 0:npc] = stiff_ref[...]
    stiff = stiff_pad[...]
    high = stiff.astype(BF16)
    low = (stiff - high.astype(F32)).astype(BF16)
    top, bottom = slice(0, main), slice(main, width)
    weight_main[...] = jnp.concatenate([high[:, top], high[:, top], low[:, top]], axis=0)
    if rest:
        paired = jnp.concatenate([high[:, bottom], low[:, bottom]], axis=1)
        weight_rest[...] = jnp.concatenate([paired, paired], axis=0)

    def triple(value):
        value_high = value.astype(BF16)
        value_low = (value - value_high.astype(F32)).astype(BF16)
        return jnp.concatenate([value_high, value_low, value_high], axis=1)

    def wide(z_main, z_rest):
        if not rest:
            return z_main
        return jnp.concatenate([z_main, z_rest[:, 0:rest] + z_rest[:, rest:]], axis=1)

    def cell_products(outside):
        for c in range(cells):
            span = slice(c * width, (c + 1) * width)
            y = yy[:, span]
            if outside is not None:
                y = folded(y) + folded(dot(outside, gather[owned:owned + outside.shape[1], span]))
            else:
                y = folded(y)
            xx[c * rows:(c + 1) * rows, :] = triple(y)
        z_main = dot(xx[...], weight_main[...])
        z_rest = dot(xx[:, 0:2 * width], weight_rest[...]) if rest else None
        for c in range(cells):
            state = slice(c * rows, (c + 1) * rows)
            z = wide(z_main[state], z_rest[state] if rest else None)
            zz[:, c * width:(c + 1) * width] = stacked_parts(z * scale_ref[c])

    def border_sums():
        return folded(dot(zz[...], scatter[:, owned:]))

    for c in range(cells):
        span = slice(c * width, (c + 1) * width)
        picks = gather[owned:, span]
        z = wide(
            dot(jnp.concatenate([picks, picks], axis=1), weight_main[width:, :]),
            dot(picks, weight_rest[0:width, :]) if rest else None)
        tt[:, span] = stacked_parts(z * scale_ref[c])

    def response(columns):
        value = folded(dot(tt[...], scatter[:, columns]))
        value_high = value.astype(BF16)
        value_low = (value - value_high.astype(F32)).astype(BF16)
        return jnp.concatenate([value_high, value_high, value_low], axis=0)

    weight_edge[...] = response(slice(owned, owned + 2 * shared))

    mass_shared, pot_shared = lead_send[rows:rows + 1, :], lead_send[rows + 1:rows + 2, :]
    partial = x_ref[...]
    current_shared = lead_send[0:rows, :]
    previous, previous_shared = None, None
    returned = None
    for t in range(DEGREE):
        last = t == DEGREE - 1
        factor = (1.0 if t == 0 else 2.0) / HALF_WIDTH
        if t:
            uu[...] = stacked_parts(mass * partial)
            for c in range(cells):
                span = slice(c * width, (c + 1) * width)
                yy[:, span] = dot(uu[...], gather[0:owned, span])
        cell_products(None)
        inside = border_sums()
        step = owned // CHUNKS if last else owned
        if last:
            for j in range(CHUNKS):
                block_send[j] = folded(dot(zz[...], scatter[:, j * step:(j + 1) * step]))
        if t == 0:
            lead_copy.wait_recv()
            learn(0)
            if len(rounds) > 1:
                tell(1)
            mass_ghost = lead_recv[rows:rows + 1, :]
            ghost = lead_recv[0:rows, :]
            fix = None
            outside = mass_ghost * ghost
        else:
            ret_copy.wait_recv()
            part_copy.wait_recv()
            for r in range(t, len(rounds) if last else t + 1):
                learn(r)
                if r + 1 < len(rounds):
                    tell(r + 1)
            fix = earlier * mass_shared * ret_recv[t - 1]
            ghost = part_recv[t - 1] + earlier * mass_ghost * returned
            current_shared = part + fix
            outside = jnp.concatenate([mass_ghost * ghost, mass_shared * fix], axis=1)
        used = outside.shape[1]
        edge = jnp.concatenate(
            [weight_edge[k * 2 * shared:k * 2 * shared + used, :] for k in range(3)], axis=0)
        arrived = triple(outside)
        border = inside + dot(arrived, edge)
        returned = border[:, 0:shared]
        ret_send[t] = returned
        ret_copy = send(ret_send.at[t], ret_recv.at[t], ret_sem, t, at(band, after))
        if last:
            for k in range(1, n_band):
                other = turned(band, k, n_band)

                @pl.when(place == jnp.where(band < other, 0, 1))
                def _():
                    remote(ret_send.at[t], last_cross.at[n_band - k - 1], cross_last_sem,
                           k - 1, at(other, after)).start()
        else:
            part = factor * (
                mass_shared * border[:, shared:] + (pot_shared - CENTER) * current_shared)
            if t:
                part = part - previous_shared
            part_send[t] = part
            part_copy = send(part_send.at[t], part_recv.at[t], part_sem, t, at(band, before))
        if not last:
            cell_products(stacked_parts(outside))
        current = partial
        if t:
            current = current + folded(dot(stacked_parts(fix), spread[...]))
        parts = []
        for j in range(owned // step):
            span = slice(j * step, (j + 1) * step)
            if last:
                sums = block_send[j] + dot(arrived, weight_own[:, span])
            else:
                sums = folded(dot(zz[...], scatter[:, span]))
            piece = factor * (mass[:, span] * sums + (pot[:, span] - CENTER) * current[:, span])
            if t:
                piece = piece - previous[:, span]
            parts.append(piece)
            if last:
                block_send[j] = piece
                for k in range(1, n_band):
                    other = turned(band, k, n_band)
                    leads = place == jnp.where(band < other, 0, 1)

                    @pl.when(jnp.logical_not(leads))
                    def _():
                        remote(block_send.at[j], block_recv.at[n_band - k - 1, j], block_sem,
                               (k - 1) * CHUNKS + j, at(other, dom)).start()
        partial = jnp.concatenate(parts, axis=1) if last else parts[0]
        if not last:
            share = owned // (DEGREE - 1)
            columns = slice(t * share, (t + 1) * share)
            weight_own[:, columns] = response(columns)
        previous, previous_shared = current, current_shared
        earlier = factor

    scaling = 1.0 / (owned * n_dom)

    def packed(block):
        return jnp.concatenate([block[0:rows // 2], block[rows // 2:]], axis=1) * scaling

    def product(mine, theirs):
        both = folded(dot_nt(mine, theirs))
        return packed(both[:, 0:rows] + both[:, rows:])

    def mended(block, returned):
        fix = stacked_parts(earlier * mass_shared * returned)
        return block + folded(dot(fix, spread[...]))

    ret_copy.wait_recv()
    filtered = mended(partial, ret_recv[DEGREE - 1])
    filt_ref[...] = filtered
    uu[...] = stacked_parts(filtered)
    own_send[0] = product(uu[...], uu[...])
    pair_copy = send(own_send.at[0], own_recv, own_pair_sem, 0, at(band, partner))
    span = 2 * lines - 1
    for k in range(1, n_band):
        other = turned(band, k, n_band)
        leads = place == jnp.where(band < other, 0, 1)

        @pl.when(leads)
        def _():
            remote(ret_send.at[0], last_cross.at[k - 1], cross_last_sem, n_band - k - 1,
                   at(other, after)).wait_recv()
            fixes = stacked_parts(earlier * mass_shared * last_cross[k - 1])
            sums = [0.0, 0.0]
            for j in range(CHUNKS):
                remote(block_send.at[j], block_recv.at[k - 1, j], block_sem,
                       (n_band - k - 1) * CHUNKS + j, at(other, dom)).wait_recv()
                part = slice(j * step, (j + 1) * step)
                theirs = stacked_parts(
                    block_recv[k - 1, j] + folded(dot(fixes, spread[:, part])))
                mine = uu[:, part]
                sums[0] = sums[0] + folded(dot_nt(mine, theirs))
                sums[1] = sums[1] + folded(dot_nt(theirs, mine))
            for j in range(2):
                cross_send[k - 1, j] = packed(sums[j][:, 0:rows] + sums[j][:, rows:])
            for l in [*range(1, lines), 0]:
                off = jnp.where(2 * line < lines, lines - l, l) if l else 0
                if l:
                    remote(cross_send.at[k - 1, 0], cross_all.at[k - 1, off], cross_sem,
                           (k - 1) * span + off - 1, at(band, spot(off, place))).start()
                remote(cross_send.at[k - 1, 1], cross_all.at[n_band - k - 1, lines + off],
                       cross_sem, (k - 1) * span + lines - 1 + off,
                       at(other, spot(off, 1 - place))).start()

    pair_copy.wait_recv()
    own_send[1] = own_send[0] + own_recv[...]
    gathers = place == jnp.where(band == 0, 1, 0)

    @pl.when(gathers)
    def _():
        for l in range(1, lines):
            remote(own_send.at[1], own_all.at[l], own_line_sem, l - 1,
                   at(band, spot(l, place))).start()

    for k in range(1, n_band):
        other = turned(band, k, n_band)
        leads = place == jnp.where(band < other, 0, 1)

        @pl.when(leads)
        def _():
            total = cross_send[k - 1, 0]
            waits = []
            for l in range(lines):
                if l:
                    waits.append(remote(
                        cross_send.at[k - 1, 0], cross_all.at[k - 1, l], cross_sem,
                        (k - 1) * span + l - 1, at(band, spot(l, place))))
                waits.append(remote(
                    cross_send.at[k - 1, 1], cross_all.at[k - 1, lines + l], cross_sem,
                    (n_band - k - 1) * span + lines - 1 + l, at(other, spot(l, 1 - place))))
            for copy in waits:
                copy.wait_recv()
            for l in range(1, 2 * lines):
                total = total + cross_all[k - 1, l]
            final[k] = total
            remote(final.at[k], final.at[k], final_sem, k, at(band, partner)).start()

    @pl.when(gathers)
    def _():
        for l in range(1, lines):
            remote(own_send.at[1], own_all.at[l], own_line_sem, l - 1,
                   at(band, spot(l, place))).wait()
        total = own_send[1]
        for l in range(1, lines):
            total = total + own_all[l]
        final[0] = total
        remote(final.at[0], final.at[0], final_sem, 0, at(band, partner)).start()

    for k in range(n_band):
        other = turned(band, k, n_band)
        holds = place == jnp.where(band < other, 0, 1) if k else gathers
        copy = remote(final.at[k], final.at[k], final_sem, k, at(band, partner))

        @pl.when(holds)
        def _():
            copy.wait_send()

        @pl.when(jnp.logical_not(holds))
        def _():
            copy.wait_recv()

    pieces = []
    for b in range(n_band):
        piece = final[0]
        for k in range(1, n_band):
            piece = jnp.where(turned(band, k, n_band) == b, final[k], piece)
        pieces.append(jnp.concatenate([piece[:, 0:rows], piece[:, rows:]], axis=0))
    margin_ref[...] = jnp.concatenate(pieces, axis=1)
    for copy in started:
        copy.wait_send()
    for k in range(1, n_band):
        other = turned(band, k, n_band)
        leads = place == jnp.where(band < other, 0, 1)

        @pl.when(leads)
        def _():
            remote(ret_send.at[0], last_cross.at[k - 1], cross_last_sem, k - 1,
                   at(other, after)).wait_send()
            for l in range(lines):
                if l:
                    remote(cross_send.at[k - 1, 0], cross_all.at[k - 1, l], cross_sem,
                           (k - 1) * span + l - 1, at(band, spot(l, place))).wait_send()
                remote(cross_send.at[k - 1, 1], cross_all.at[k - 1, lines + l], cross_sem,
                       (k - 1) * span + lines - 1 + l,
                       at(other, spot(l, 1 - place))).wait_send()

        @pl.when(jnp.logical_not(leads))
        def _():
            for j in range(CHUNKS):
                remote(block_send.at[j], block_recv.at[k - 1, j], block_sem,
                       (k - 1) * CHUNKS + j, at(other, dom)).wait_send()


def finish(filt_ref, margin_ref, filt_out, margin_out, sem):
    copies = [
        pltpu.make_async_copy(filt_ref, filt_out, sem.at[0]),
        pltpu.make_async_copy(margin_ref, margin_out, sem.at[1])]
    for copy in copies:
        copy.start()
    for copy in copies:
        copy.wait()


def rounded_up(value):
    return -(-value // LANES) * LANES


def per_device(
    n_band, n_dom,
    states_in, stiffness, cell_scale, potential, inv_mass_sqrt, cell_nodes, shared_nodes
):
    rows, owned = states_in.shape
    cells, npc = cell_nodes.shape
    shared = shared_nodes.shape[0]
    width = rounded_up(npc)
    nodes = owned + 2 * shared
    states = n_band * rows
    main = width // (2 * LANES) * 2 * LANES
    rest = width - main
    lines = n_dom // PLACES
    others = n_band - 1
    block = (rows // 2, 2 * rows)
    pairs = lambda count: pltpu.SemaphoreType.DMA((2, count))
    vmem = pltpu.VMEM
    in_vmem = pl.BlockSpec(memory_space=pltpu.VMEM)
    found = pl.pallas_call(
        functools.partial(kernel, n_band, n_dom),
        out_shape=(
            jax.ShapeDtypeStruct((rows, owned), F32),
            jax.ShapeDtypeStruct((rows, states), F32),
        ),
        in_specs=[pl.BlockSpec(memory_space=pltpu.HBM)] * 7,
        out_specs=(in_vmem, in_vmem),
        scratch_shapes=[
            vmem((rows, owned), F32),
            vmem((npc, npc), F32),
            pltpu.SMEM((cells,), F32),
            vmem((1, owned), F32),
            vmem((1, owned), F32),
            vmem((cells, npc), jnp.int32),
            vmem((1, shared), jnp.int32),
            pltpu.SemaphoreType.DMA((7,)),
            vmem((-(-cells // 8) * 8, width), jnp.int32),
            vmem((width, width), F32),
            vmem((3 * width, main), BF16),
            vmem((2 * width, 2 * max(rest, LANES)), BF16),
            vmem((nodes, cells * width), BF16),
            vmem((cells * width, nodes), BF16),
            vmem((shared, owned), BF16),
            vmem((rows + 8, owned), F32),
            vmem((rows + 8, shared), F32),
            vmem((rows + 8, shared), F32),
            vmem((DEGREE, rows, shared), F32),
            vmem((DEGREE, rows, shared), F32),
            vmem((DEGREE - 1, rows, shared), F32),
            vmem((DEGREE - 1, rows, shared), F32),
            vmem((2 * rows, owned), BF16),
            vmem((2 * rows, cells * width), F32),
            vmem((cells * rows, 3 * width), BF16),
            vmem((2 * rows, cells * width), BF16),
            vmem((4 * shared, cells * width), BF16),
            vmem((6 * shared, 2 * shared), BF16),
            vmem((6 * shared, owned), BF16),
            vmem((CHUNKS, rows, owned // CHUNKS), F32),
            vmem((others, CHUNKS, rows, owned // CHUNKS), F32),
            vmem((others, rows, shared), F32),
            vmem((2, *block), F32),
            vmem(block, F32),
            vmem((lines, *block), F32),
            vmem((others, 2, *block), F32),
            vmem((others, 2 * lines, *block), F32),
            vmem((n_band, *block), F32),
            pairs(1),
            pairs(DEGREE),
            pairs(DEGREE - 1),
            pairs(others),
            pairs(others * CHUNKS),
            pairs(1),
            pairs(lines - 1),
            pairs(others * (2 * lines - 1)),
            pairs(n_band),
            pltpu.SemaphoreType.REGULAR((max(n_dom.bit_length() - 2, 1),)),
        ],
        compiler_params=pltpu.CompilerParams(collective_id=0, has_side_effects=True, vmem_limit_bytes=44 << 20),
    )(*[pltpu.with_memory_space_constraint(value, pltpu.HBM) for value in (
        states_in, stiffness, cell_scale, potential[None, :], inv_mass_sqrt[None, :],
        cell_nodes, shared_nodes[None, :],
    )])
    return pl.pallas_call(
        finish,
        out_shape=tuple(jax.ShapeDtypeStruct(value.shape, F32) for value in found),
        in_specs=[in_vmem, in_vmem],
        out_specs=(pl.BlockSpec(memory_space=pltpu.HBM),) * 2,
        scratch_shapes=[pltpu.SemaphoreType.DMA((2,))],
    )(*[pltpu.with_memory_space_constraint(value, pltpu.VMEM) for value in found])


def solution(mesh):
    n_band, n_dom = mesh.shape["band"], mesh.shape["dom"]
    return jax.shard_map(
        functools.partial(per_device, n_band, n_dom),
        mesh=mesh,
        in_specs=(P("band", "dom"), P(), P("dom"), P("dom"), P("dom"), P("dom", None), P("dom")),
        out_specs=(P("band", "dom"), P("band", None)),
        check_vma=False,
    )
```

```python
import functools

import jax
import jax.numpy as jnp
from jax import lax
from jax.experimental import pallas as pl
from jax.experimental.pallas import tpu as pltpu
from jax.sharding import PartitionSpec as P

DEGREE = 3
CENTER = 1.0
HALF_WIDTH = 4.0
LANES = 128
PLACES = 2
CHUNKS = 4
F32, BF16 = jnp.float32, jnp.bfloat16


def stacked_parts(value):
    high = value.astype(BF16)
    low = (value - high.astype(F32)).astype(BF16)
    return jnp.concatenate([high, low], axis=0)


def folded(value):
    half = value.shape[0] // 2
    return value[:half] + value[half:]


def dot(a, b):
    return jnp.dot(a, b, preferred_element_type=F32)


def dot_nt(a, b):
    return lax.dot_general(a, b, (((1,), (1,)), ((), ())), preferred_element_type=F32)


def narrow(value):
    return value.astype(jnp.int16)


def one_hot(a, b):
    return jnp.where(a == b, jnp.array(1, BF16), jnp.array(0, BF16))


def kernel(
    n_band, n_dom,
    x_hbm, stiff_hbm, scale_hbm, pot_hbm, mass_hbm, cells_hbm, shared_hbm,
    filt_ref, margin_ref,
    x_ref, stiff_ref, scale_ref, pot_ref, mass_ref, cells_ref, shared_ref, load_sem,
    idx, stiff_pad, weight_main, weight_rest, gather, scatter, spread, lead,
    lead_send, lead_recv, ret_send, ret_recv, part_send, part_recv,
    uu, yy, xx, zz, tt, weight_edge, block_send, block_recv, last_cross,
    own_send, own_recv, own_all, cross_send, cross_all, final,
    lead_sem, ret_sem, part_sem, cross_last_sem, block_sem,
    own_pair_sem, own_line_sem, cross_sem, final_sem, known_sem,
):
    rows, owned = x_ref.shape
    cells, npc = cells_ref.shape
    shared = shared_ref.shape[1]
    width = idx.shape[1]
    main = weight_main.shape[1]
    rest = width - main
    local = owned + shared
    lines = n_dom // PLACES
    band, dom = lax.axis_index("band"), lax.axis_index("dom")
    after, before = lax.rem(dom + 1, n_dom), lax.rem(dom + n_dom - 1, n_dom)
    place, line = lax.rem(dom, PLACES), dom // PLACES
    partner = line * PLACES + 1 - place

    def turned(value, by, size):
        return lax.rem(value + by, size)

    def at(b, d):
        return {"band": b, "dom": d}

    def spot(l, p):
        return turned(line, l, lines) * PLACES + p

    pairs = (
        (shared_hbm, shared_ref), (mass_hbm, mass_ref), (pot_hbm, pot_ref), (x_hbm, x_ref),
        (cells_hbm, cells_ref), (stiff_hbm, stiff_ref), (scale_hbm, scale_ref))
    loads = [pltpu.make_async_copy(src, dst, load_sem.at[k]) for k, (src, dst) in enumerate(pairs)]
    first_loads, later_loads = loads[:5], loads[5:]
    barrier = pltpu.get_barrier_semaphore()
    others = [at(turned(band, k, n_band), dom) for k in range(1, n_band)]
    greeted = [at(band, after), at(band, before)] + others
    for device in greeted:
        pl.semaphore_signal(barrier, inc=1, device_id=device)
    for load in loads:
        load.start()

    rounds = []
    reach = 1
    while reach * 4 <= n_dom or not rounds:
        there = [at(band, lax.rem(dom + reach, n_dom)), at(band, lax.rem(dom + n_dom - reach, n_dom))]
        rounds.append(there + (others if reach == 1 else []))
        reach *= 2

    def tell(r):
        for device in rounds[r]:
            pl.semaphore_signal(known_sem.at[r], inc=1, device_id=device)

    def learn(r):
        pl.semaphore_wait(known_sem.at[r], len(rounds[r]))

    def remote(src, dst, sems, slot, device):
        return pltpu.make_async_remote_copy(
            src_ref=src, dst_ref=dst, send_sem=sems.at[0, slot], recv_sem=sems.at[1, slot],
            device_id=device, device_id_type=pl.DeviceIdType.MESH)

    started = []

    def send(*args):
        copy = remote(*args)
        copy.start()
        started.append(copy)
        return copy

    for load in first_loads:
        load.wait()
    mass, pot = mass_ref[...], pot_ref[...]
    shared_row = shared_ref[...]
    lead[0:rows, :] = x_ref[...]
    lead[rows:rows + 8, :] = jnp.concatenate(
        [mass, pot, jnp.zeros((6, owned), F32)], axis=0)
    wanted = jnp.broadcast_to(shared_row, (rows + 8, shared))
    lane_of, tile_of = wanted & (LANES - 1), wanted >> 7
    picked = None
    for k in range(owned // LANES):
        found = jnp.take_along_axis(lead[:, k * LANES:(k + 1) * LANES], lane_of, axis=1)
        picked = found if picked is None else jnp.where(tile_of == k, found, picked)
    lead_send[...] = picked
    uu[...] = stacked_parts(mass * x_ref[...])
    idx[...] = jnp.full(idx.shape, -1, jnp.int32)
    idx[0:cells, 0:npc] = cells_ref[...]
    node = narrow(lax.broadcasted_iota(jnp.int32, (LANES, width), 0))
    lane = narrow(lax.broadcasted_iota(jnp.int32, (width, LANES), 1))
    shared_col = jnp.broadcast_to(shared_row, (LANES, shared)).T
    shared_wide = narrow(jnp.concatenate([shared_col] * (width // LANES), axis=1))
    shared_tall = narrow(jnp.broadcast_to(shared_row, (width, shared)))
    for c in range(cells):
        span = slice(c * width, (c + 1) * width)
        slot_row = narrow(jnp.broadcast_to(idx[c:c + 1, :], (LANES, width)))
        for k in range(local // LANES):
            tile = slice(k * LANES, (k + 1) * LANES)
            gather[tile, span] = one_hot(node + jnp.int16(k * LANES), slot_row)
        gather[local:, span] = one_hot(shared_wide, slot_row)
    pl.semaphore_wait(barrier, len(greeted))
    lead_copy = send(lead_send, lead_recv, lead_sem, 0, at(band, before))
    tell(0)

    for load in later_loads:
        load.wait()
    for c in range(cells):
        span = slice(c * width, (c + 1) * width)
        yy[:, span] = dot(uu[...], gather[0:owned, span])
        slot_col = narrow(jnp.broadcast_to(idx[c:c + 1, :], (LANES, width)).T)
        for k in range(local // LANES):
            tile = slice(k * LANES, (k + 1) * LANES)
            scatter[span, tile] = one_hot(lane + jnp.int16(k * LANES), slot_col)
        scatter[span, local:] = one_hot(shared_tall, slot_col)
    short = narrow(shared_col)
    lane = narrow(lax.broadcasted_iota(jnp.int32, (shared, LANES), 1))
    for k in range(owned // LANES):
        spread[:, k * LANES:(k + 1) * LANES] = one_hot(lane + jnp.int16(k * LANES), short)
    stiff_pad[...] = jnp.zeros(stiff_pad.shape, F32)
    stiff_pad[0:npc, 0:npc] = stiff_ref[...]
    stiff = stiff_pad[...]
    high = stiff.astype(BF16)
    low = (stiff - high.astype(F32)).astype(BF16)
    top, bottom = slice(0, main), slice(main, width)
    weight_main[...] = jnp.concatenate([high[:, top], high[:, top], low[:, top]], axis=0)
    if rest:
        paired = jnp.concatenate([high[:, bottom], low[:, bottom]], axis=1)
        weight_rest[...] = jnp.concatenate([paired, paired], axis=0)

    def triple(value):
        value_high = value.astype(BF16)
        value_low = (value - value_high.astype(F32)).astype(BF16)
        return jnp.concatenate([value_high, value_low, value_high], axis=1)

    def wide(z_main, z_rest):
        if not rest:
            return z_main
        return jnp.concatenate([z_main, z_rest[:, 0:rest] + z_rest[:, rest:]], axis=1)

    def cell_products(outside):
        for c in range(cells):
            span = slice(c * width, (c + 1) * width)
            y = yy[:, span]
            if outside is not None:
                y = folded(y) + folded(dot(outside, gather[owned:owned + outside.shape[1], span]))
            else:
                y = folded(y)
            xx[c * rows:(c + 1) * rows, :] = triple(y)
        z_main = dot(xx[...], weight_main[...])
        z_rest = dot(xx[:, 0:2 * width], weight_rest[...]) if rest else None
        for c in range(cells):
            state = slice(c * rows, (c + 1) * rows)
            z = wide(z_main[state], z_rest[state] if rest else None)
            zz[:, c * width:(c + 1) * width] = stacked_parts(z * scale_ref[c])

    def border_sums():
        return folded(dot(zz[...], scatter[:, owned:]))

    for c in range(cells):
        span = slice(c * width, (c + 1) * width)
        picks = gather[owned:, span]
        z = wide(
            dot(jnp.concatenate([picks, picks], axis=1), weight_main[width:, :]),
            dot(picks, weight_rest[0:width, :]) if rest else None)
        tt[:, span] = stacked_parts(z * scale_ref[c])
    response = folded(dot(tt[...], scatter[:, owned:]))
    response_high = response.astype(BF16)
    response_low = (response - response_high.astype(F32)).astype(BF16)
    weight_edge[...] = jnp.concatenate([response_high, response_high, response_low], axis=0)

    mass_shared, pot_shared = lead_send[rows:rows + 1, :], lead_send[rows + 1:rows + 2, :]
    partial = x_ref[...]
    current_shared = lead_send[0:rows, :]
    previous, previous_shared = None, None
    returned = None
    for t in range(DEGREE):
        last = t == DEGREE - 1
        factor = (1.0 if t == 0 else 2.0) / HALF_WIDTH
        if t:
            uu[...] = stacked_parts(mass * partial)
            for c in range(cells):
                span = slice(c * width, (c + 1) * width)
                yy[:, span] = dot(uu[...], gather[0:owned, span])
        cell_products(None)
        inside = border_sums()
        if t == 0:
            lead_copy.wait_recv()
            learn(0)
            if len(rounds) > 1:
                tell(1)
            mass_ghost = lead_recv[rows:rows + 1, :]
            ghost = lead_recv[0:rows, :]
            fix = None
            outside = mass_ghost * ghost
        else:
            ret_copy.wait_recv()
            part_copy.wait_recv()
            for r in range(t, len(rounds) if last else t + 1):
                learn(r)
                if r + 1 < len(rounds):
                    tell(r + 1)
            fix = earlier * mass_shared * ret_recv[t - 1]
            ghost = part_recv[t - 1] + earlier * mass_ghost * returned
            current_shared = part + fix
            outside = jnp.concatenate([mass_ghost * ghost, mass_shared * fix], axis=1)
        used = outside.shape[1]
        edge = jnp.concatenate(
            [weight_edge[k * 2 * shared:k * 2 * shared + used, :] for k in range(3)], axis=0)
        border = inside + dot(triple(outside), edge)
        returned = border[:, 0:shared]
        ret_send[t] = returned
        ret_copy = send(ret_send.at[t], ret_recv.at[t], ret_sem, t, at(band, after))
        if last:
            for k in range(1, n_band):
                other = turned(band, k, n_band)

                @pl.when(place == jnp.where(band < other, 0, 1))
                def _():
                    remote(ret_send.at[t], last_cross.at[n_band - k - 1], cross_last_sem,
                           k - 1, at(other, after)).start()
        else:
            part = factor * (
                mass_shared * border[:, shared:] + (pot_shared - CENTER) * current_shared)
            if t:
                part = part - previous_shared
            part_send[t] = part
            part_copy = send(part_send.at[t], part_recv.at[t], part_sem, t, at(band, before))
        cell_products(stacked_parts(outside))
        current = partial
        if t:
            current = current + folded(dot(stacked_parts(fix), spread[...]))
        step = owned // CHUNKS if last else owned
        parts = []
        for j in range(owned // step):
            span = slice(j * step, (j + 1) * step)
            sums = folded(dot(zz[...], scatter[:, span]))
            piece = factor * (mass[:, span] * sums + (pot[:, span] - CENTER) * current[:, span])
            if t:
                piece = piece - previous[:, span]
            parts.append(piece)
            if last:
                block_send[j] = piece
                for k in range(1, n_band):
                    other = turned(band, k, n_band)
                    leads = place == jnp.where(band < other, 0, 1)

                    @pl.when(jnp.logical_not(leads))
                    def _():
                        remote(block_send.at[j], block_recv.at[n_band - k - 1, j], block_sem,
                               (k - 1) * CHUNKS + j, at(other, dom)).start()
        partial = jnp.concatenate(parts, axis=1) if last else parts[0]
        previous, previous_shared = current, current_shared
        earlier = factor

    scaling = 1.0 / (owned * n_dom)

    def packed(block):
        return jnp.concatenate([block[0:rows // 2], block[rows // 2:]], axis=1) * scaling

    def product(mine, theirs):
        both = folded(dot_nt(mine, theirs))
        return packed(both[:, 0:rows] + both[:, rows:])

    def mended(block, returned):
        fix = stacked_parts(earlier * mass_shared * returned)
        return block + folded(dot(fix, spread[...]))

    ret_copy.wait_recv()
    filtered = mended(partial, ret_recv[DEGREE - 1])
    filt_ref[...] = filtered
    uu[...] = stacked_parts(filtered)
    own_send[0] = product(uu[...], uu[...])
    pair_copy = send(own_send.at[0], own_recv, own_pair_sem, 0, at(band, partner))
    span = 2 * lines - 1
    for k in range(1, n_band):
        other = turned(band, k, n_band)
        leads = place == jnp.where(band < other, 0, 1)

        @pl.when(leads)
        def _():
            remote(ret_send.at[0], last_cross.at[k - 1], cross_last_sem, n_band - k - 1,
                   at(other, after)).wait_recv()
            fixes = stacked_parts(earlier * mass_shared * last_cross[k - 1])
            sums = [0.0, 0.0]
            for j in range(CHUNKS):
                remote(block_send.at[j], block_recv.at[k - 1, j], block_sem,
                       (n_band - k - 1) * CHUNKS + j, at(other, dom)).wait_recv()
                part = slice(j * step, (j + 1) * step)
                theirs = stacked_parts(
                    block_recv[k - 1, j] + folded(dot(fixes, spread[:, part])))
                mine = uu[:, part]
                sums[0] = sums[0] + folded(dot_nt(mine, theirs))
                sums[1] = sums[1] + folded(dot_nt(theirs, mine))
            for j in range(2):
                cross_send[k - 1, j] = packed(sums[j][:, 0:rows] + sums[j][:, rows:])
            for l in [*range(1, lines), 0]:
                off = jnp.where(2 * line < lines, lines - l, l) if l else 0
                if l:
                    remote(cross_send.at[k - 1, 0], cross_all.at[k - 1, off], cross_sem,
                           (k - 1) * span + off - 1, at(band, spot(off, place))).start()
                remote(cross_send.at[k - 1, 1], cross_all.at[n_band - k - 1, lines + off],
                       cross_sem, (k - 1) * span + lines - 1 + off,
                       at(other, spot(off, 1 - place))).start()

    pair_copy.wait_recv()
    own_send[1] = own_send[0] + own_recv[...]
    gathers = place == jnp.where(band == 0, 1, 0)

    @pl.when(gathers)
    def _():
        for l in range(1, lines):
            remote(own_send.at[1], own_all.at[l], own_line_sem, l - 1,
                   at(band, spot(l, place))).start()

    for k in range(1, n_band):
        other = turned(band, k, n_band)
        leads = place == jnp.where(band < other, 0, 1)

        @pl.when(leads)
        def _():
            total = cross_send[k - 1, 0]
            waits = []
            for l in range(lines):
                if l:
                    waits.append(remote(
                        cross_send.at[k - 1, 0], cross_all.at[k - 1, l], cross_sem,
                        (k - 1) * span + l - 1, at(band, spot(l, place))))
                waits.append(remote(
                    cross_send.at[k - 1, 1], cross_all.at[k - 1, lines + l], cross_sem,
                    (n_band - k - 1) * span + lines - 1 + l, at(other, spot(l, 1 - place))))
            for copy in waits:
                copy.wait_recv()
            for l in range(1, 2 * lines):
                total = total + cross_all[k - 1, l]
            final[k] = total
            remote(final.at[k], final.at[k], final_sem, k, at(band, partner)).start()

    @pl.when(gathers)
    def _():
        for l in range(1, lines):
            remote(own_send.at[1], own_all.at[l], own_line_sem, l - 1,
                   at(band, spot(l, place))).wait()
        total = own_send[1]
        for l in range(1, lines):
            total = total + own_all[l]
        final[0] = total
        remote(final.at[0], final.at[0], final_sem, 0, at(band, partner)).start()

    for k in range(n_band):
        other = turned(band, k, n_band)
        holds = place == jnp.where(band < other, 0, 1) if k else gathers
        copy = remote(final.at[k], final.at[k], final_sem, k, at(band, partner))

        @pl.when(holds)
        def _():
            copy.wait_send()

        @pl.when(jnp.logical_not(holds))
        def _():
            copy.wait_recv()

    pieces = []
    for b in range(n_band):
        piece = final[0]
        for k in range(1, n_band):
            piece = jnp.where(turned(band, k, n_band) == b, final[k], piece)
        pieces.append(jnp.concatenate([piece[:, 0:rows], piece[:, rows:]], axis=0))
    margin_ref[...] = jnp.concatenate(pieces, axis=1)
    for copy in started:
        copy.wait_send()
    for k in range(1, n_band):
        other = turned(band, k, n_band)
        leads = place == jnp.where(band < other, 0, 1)

        @pl.when(leads)
        def _():
            remote(ret_send.at[0], last_cross.at[k - 1], cross_last_sem, k - 1,
                   at(other, after)).wait_send()
            for l in range(lines):
                if l:
                    remote(cross_send.at[k - 1, 0], cross_all.at[k - 1, l], cross_sem,
                           (k - 1) * span + l - 1, at(band, spot(l, place))).wait_send()
                remote(cross_send.at[k - 1, 1], cross_all.at[k - 1, lines + l], cross_sem,
                       (k - 1) * span + lines - 1 + l,
                       at(other, spot(l, 1 - place))).wait_send()

        @pl.when(jnp.logical_not(leads))
        def _():
            for j in range(CHUNKS):
                remote(block_send.at[j], block_recv.at[k - 1, j], block_sem,
                       (k - 1) * CHUNKS + j, at(other, dom)).wait_send()


def finish(filt_ref, margin_ref, filt_out, margin_out, sem):
    copies = [
        pltpu.make_async_copy(filt_ref, filt_out, sem.at[0]),
        pltpu.make_async_copy(margin_ref, margin_out, sem.at[1])]
    for copy in copies:
        copy.start()
    for copy in copies:
        copy.wait()


def rounded_up(value):
    return -(-value // LANES) * LANES


def per_device(
    n_band, n_dom,
    states_in, stiffness, cell_scale, potential, inv_mass_sqrt, cell_nodes, shared_nodes
):
    rows, owned = states_in.shape
    cells, npc = cell_nodes.shape
    shared = shared_nodes.shape[0]
    width = rounded_up(npc)
    nodes = owned + 2 * shared
    states = n_band * rows
    main = width // (2 * LANES) * 2 * LANES
    rest = width - main
    lines = n_dom // PLACES
    others = n_band - 1
    block = (rows // 2, 2 * rows)
    pairs = lambda count: pltpu.SemaphoreType.DMA((2, count))
    vmem = pltpu.VMEM
    in_vmem = pl.BlockSpec(memory_space=pltpu.VMEM)
    found = pl.pallas_call(
        functools.partial(kernel, n_band, n_dom),
        out_shape=(
            jax.ShapeDtypeStruct((rows, owned), F32),
            jax.ShapeDtypeStruct((rows, states), F32),
        ),
        in_specs=[pl.BlockSpec(memory_space=pltpu.HBM)] * 7,
        out_specs=(in_vmem, in_vmem),
        scratch_shapes=[
            vmem((rows, owned), F32),
            vmem((npc, npc), F32),
            pltpu.SMEM((cells,), F32),
            vmem((1, owned), F32),
            vmem((1, owned), F32),
            vmem((cells, npc), jnp.int32),
            vmem((1, shared), jnp.int32),
            pltpu.SemaphoreType.DMA((7,)),
            vmem((-(-cells // 8) * 8, width), jnp.int32),
            vmem((width, width), F32),
            vmem((3 * width, main), BF16),
            vmem((2 * width, 2 * max(rest, LANES)), BF16),
            vmem((nodes, cells * width), BF16),
            vmem((cells * width, nodes), BF16),
            vmem((shared, owned), BF16),
            vmem((rows + 8, owned), F32),
            vmem((rows + 8, shared), F32),
            vmem((rows + 8, shared), F32),
            vmem((DEGREE, rows, shared), F32),
            vmem((DEGREE, rows, shared), F32),
            vmem((DEGREE - 1, rows, shared), F32),
            vmem((DEGREE - 1, rows, shared), F32),
            vmem((2 * rows, owned), BF16),
            vmem((2 * rows, cells * width), F32),
            vmem((cells * rows, 3 * width), BF16),
            vmem((2 * rows, cells * width), BF16),
            vmem((4 * shared, cells * width), BF16),
            vmem((6 * shared, 2 * shared), BF16),
            vmem((CHUNKS, rows, owned // CHUNKS), F32),
            vmem((others, CHUNKS, rows, owned // CHUNKS), F32),
            vmem((others, rows, shared), F32),
            vmem((2, *block), F32),
            vmem(block, F32),
            vmem((lines, *block), F32),
            vmem((others, 2, *block), F32),
            vmem((others, 2 * lines, *block), F32),
            vmem((n_band, *block), F32),
            pairs(1),
            pairs(DEGREE),
            pairs(DEGREE - 1),
            pairs(others),
            pairs(others * CHUNKS),
            pairs(1),
            pairs(lines - 1),
            pairs(others * (2 * lines - 1)),
            pairs(n_band),
            pltpu.SemaphoreType.REGULAR((max(n_dom.bit_length() - 2, 1),)),
        ],
        compiler_params=pltpu.CompilerParams(collective_id=0, has_side_effects=True, vmem_limit_bytes=44 << 20),
    )(*[pltpu.with_memory_space_constraint(value, pltpu.HBM) for value in (
        states_in, stiffness, cell_scale, potential[None, :], inv_mass_sqrt[None, :],
        cell_nodes, shared_nodes[None, :],
    )])
    return pl.pallas_call(
        finish,
        out_shape=tuple(jax.ShapeDtypeStruct(value.shape, F32) for value in found),
        in_specs=[in_vmem, in_vmem],
        out_specs=(pl.BlockSpec(memory_space=pltpu.HBM),) * 2,
        scratch_shapes=[pltpu.SemaphoreType.DMA((2,))],
    )(*[pltpu.with_memory_space_constraint(value, pltpu.VMEM) for value in found])


def solution(mesh):
    n_band, n_dom = mesh.shape["band"], mesh.shape["dom"]
    return jax.shard_map(
        functools.partial(per_device, n_band, n_dom),
        mesh=mesh,
        in_specs=(P("band", "dom"), P(), P("dom"), P("dom"), P("dom"), P("dom", None), P("dom")),
        out_specs=(P("band", "dom"), P("band", None)),
        check_vma=False,
    )
```

```python
import functools

import jax
import jax.numpy as jnp
from jax import lax
from jax.experimental import pallas as pl
from jax.experimental.pallas import tpu as pltpu
from jax.sharding import PartitionSpec as P

DEGREE = 3
CENTER = 1.0
HALF_WIDTH = 4.0
LANES = 128
PLACES = 2
CHUNKS = 4
F32, BF16 = jnp.float32, jnp.bfloat16


def stacked_parts(value):
    high = value.astype(BF16)
    low = (value - high.astype(F32)).astype(BF16)
    return jnp.concatenate([high, low], axis=0)


def folded(value):
    half = value.shape[0] // 2
    return value[:half] + value[half:]


def dot(a, b):
    return jnp.dot(a, b, preferred_element_type=F32)


def dot_nt(a, b):
    return lax.dot_general(a, b, (((1,), (1,)), ((), ())), preferred_element_type=F32)


def narrow(value):
    return value.astype(jnp.int16)


def one_hot(a, b):
    return jnp.where(a == b, jnp.array(1, BF16), jnp.array(0, BF16))


def kernel(
    n_band, n_dom,
    x_hbm, stiff_hbm, scale_hbm, pot_hbm, mass_hbm, cells_hbm, shared_hbm,
    filt_ref, margin_ref,
    x_ref, stiff_ref, scale_ref, pot_ref, mass_ref, cells_ref, shared_ref, load_sem,
    idx, stiff_pad, weight_main, weight_rest, gather, scatter, spread, lead,
    lead_send, lead_recv, ret_send, ret_recv, part_send, part_recv,
    uu, yy, xx, zz, tt, weight_edge, block_send, block_recv, last_cross,
    own_send, own_recv, own_all, cross_send, cross_all, final,
    lead_sem, ret_sem, part_sem, cross_last_sem, block_sem,
    own_pair_sem, own_line_sem, cross_sem, final_sem, known_sem,
):
    rows, owned = x_ref.shape
    cells, npc = cells_ref.shape
    shared = shared_ref.shape[1]
    width = idx.shape[1]
    main = weight_main.shape[1]
    rest = width - main
    local = owned + shared
    lines = n_dom // PLACES
    band, dom = lax.axis_index("band"), lax.axis_index("dom")
    after, before = lax.rem(dom + 1, n_dom), lax.rem(dom + n_dom - 1, n_dom)
    place, line = lax.rem(dom, PLACES), dom // PLACES
    partner = line * PLACES + 1 - place

    def turned(value, by, size):
        return lax.rem(value + by, size)

    def at(b, d):
        return {"band": b, "dom": d}

    def spot(l, p):
        return turned(line, l, lines) * PLACES + p

    pairs = (
        (shared_hbm, shared_ref), (mass_hbm, mass_ref), (pot_hbm, pot_ref), (x_hbm, x_ref),
        (cells_hbm, cells_ref), (stiff_hbm, stiff_ref), (scale_hbm, scale_ref))
    loads = [pltpu.make_async_copy(src, dst, load_sem.at[k]) for k, (src, dst) in enumerate(pairs)]
    first_loads, later_loads = loads[:5], loads[5:]
    barrier = pltpu.get_barrier_semaphore()
    others = [at(turned(band, k, n_band), dom) for k in range(1, n_band)]
    greeted = [at(band, after), at(band, before)] + others
    for device in greeted:
        pl.semaphore_signal(barrier, inc=1, device_id=device)
    for load in loads:
        load.start()

    rounds = []
    reach = 1
    while reach * 4 <= n_dom or not rounds:
        there = [at(band, lax.rem(dom + reach, n_dom)), at(band, lax.rem(dom + n_dom - reach, n_dom))]
        rounds.append(there + (others if reach == 1 else []))
        reach *= 2

    def tell(r):
        for device in rounds[r]:
            pl.semaphore_signal(known_sem.at[r], inc=1, device_id=device)

    def learn(r):
        pl.semaphore_wait(known_sem.at[r], len(rounds[r]))

    def remote(src, dst, sems, slot, device):
        return pltpu.make_async_remote_copy(
            src_ref=src, dst_ref=dst, send_sem=sems.at[0, slot], recv_sem=sems.at[1, slot],
            device_id=device, device_id_type=pl.DeviceIdType.MESH)

    started = []

    def send(*args):
        copy = remote(*args)
        copy.start()
        started.append(copy)
        return copy

    for load in first_loads:
        load.wait()
    mass, pot = mass_ref[...], pot_ref[...]
    shared_row = shared_ref[...]
    lead[0:rows, :] = x_ref[...]
    lead[rows:rows + 8, :] = jnp.concatenate(
        [mass, pot, jnp.zeros((6, owned), F32)], axis=0)
    wanted = jnp.broadcast_to(shared_row, (rows + 8, shared))
    lane_of, tile_of = wanted & (LANES - 1), wanted >> 7
    picked = None
    for k in range(owned // LANES):
        found = jnp.take_along_axis(lead[:, k * LANES:(k + 1) * LANES], lane_of, axis=1)
        picked = found if picked is None else jnp.where(tile_of == k, found, picked)
    lead_send[...] = picked
    uu[...] = stacked_parts(mass * x_ref[...])
    idx[...] = jnp.full(idx.shape, -1, jnp.int32)
    idx[0:cells, 0:npc] = cells_ref[...]
    node = narrow(lax.broadcasted_iota(jnp.int32, (LANES, width), 0))
    lane = narrow(lax.broadcasted_iota(jnp.int32, (width, LANES), 1))
    shared_col = jnp.broadcast_to(shared_row, (LANES, shared)).T
    shared_wide = narrow(jnp.concatenate([shared_col] * (width // LANES), axis=1))
    shared_tall = narrow(jnp.broadcast_to(shared_row, (width, shared)))
    for c in range(cells):
        span = slice(c * width, (c + 1) * width)
        slot_row = narrow(jnp.broadcast_to(idx[c:c + 1, :], (LANES, width)))
        for k in range(local // LANES):
            tile = slice(k * LANES, (k + 1) * LANES)
            gather[tile, span] = one_hot(node + jnp.int16(k * LANES), slot_row)
        gather[local:, span] = one_hot(shared_wide, slot_row)
    pl.semaphore_wait(barrier, len(greeted))
    lead_copy = send(lead_send, lead_recv, lead_sem, 0, at(band, before))
    tell(0)

    for load in later_loads:
        load.wait()
    for c in range(cells):
        span = slice(c * width, (c + 1) * width)
        yy[:, span] = dot(uu[...], gather[0:owned, span])
        slot_col = narrow(jnp.broadcast_to(idx[c:c + 1, :], (LANES, width)).T)
        for k in range(local // LANES):
            tile = slice(k * LANES, (k + 1) * LANES)
            scatter[span, tile] = one_hot(lane + jnp.int16(k * LANES), slot_col)
        scatter[span, local:] = one_hot(shared_tall, slot_col)
    short = narrow(shared_col)
    lane = narrow(lax.broadcasted_iota(jnp.int32, (shared, LANES), 1))
    for k in range(owned // LANES):
        spread[:, k * LANES:(k + 1) * LANES] = one_hot(lane + jnp.int16(k * LANES), short)
    stiff_pad[...] = jnp.zeros(stiff_pad.shape, F32)
    stiff_pad[0:npc, 0:npc] = stiff_ref[...]
    stiff = stiff_pad[...]
    high = stiff.astype(BF16)
    low = (stiff - high.astype(F32)).astype(BF16)
    top, bottom = slice(0, main), slice(main, width)
    weight_main[...] = jnp.concatenate([high[:, top], high[:, top], low[:, top]], axis=0)
    if rest:
        paired = jnp.concatenate([high[:, bottom], low[:, bottom]], axis=1)
        weight_rest[...] = jnp.concatenate([paired, paired], axis=0)

    def triple(value):
        value_high = value.astype(BF16)
        value_low = (value - value_high.astype(F32)).astype(BF16)
        return jnp.concatenate([value_high, value_low, value_high], axis=1)

    def wide(z_main, z_rest):
        if not rest:
            return z_main
        return jnp.concatenate([z_main, z_rest[:, 0:rest] + z_rest[:, rest:]], axis=1)

    def cell_products(outside):
        for c in range(cells):
            span = slice(c * width, (c + 1) * width)
            y = yy[:, span]
            if outside is not None:
                y = folded(y) + folded(dot(outside, gather[owned:owned + outside.shape[1], span]))
            else:
                y = folded(y)
            xx[c * rows:(c + 1) * rows, :] = triple(y)
        z_main = dot(xx[...], weight_main[...])
        z_rest = dot(xx[:, 0:2 * width], weight_rest[...]) if rest else None
        for c in range(cells):
            state = slice(c * rows, (c + 1) * rows)
            z = wide(z_main[state], z_rest[state] if rest else None)
            zz[:, c * width:(c + 1) * width] = stacked_parts(z * scale_ref[c])

    def border_sums():
        return folded(dot(zz[...], scatter[:, owned:]))

    for c in range(cells):
        span = slice(c * width, (c + 1) * width)
        picks = gather[owned:, span]
        z = wide(
            dot(jnp.concatenate([picks, picks], axis=1), weight_main[width:, :]),
            dot(picks, weight_rest[0:width, :]) if rest else None)
        tt[:, span] = stacked_parts(z * scale_ref[c])
    response = folded(dot(tt[...], scatter[:, owned:]))
    response_high = response.astype(BF16)
    response_low = (response - response_high.astype(F32)).astype(BF16)
    weight_edge[...] = jnp.concatenate([response_high, response_high, response_low], axis=0)

    mass_shared, pot_shared = lead_send[rows:rows + 1, :], lead_send[rows + 1:rows + 2, :]
    partial = x_ref[...]
    current_shared = lead_send[0:rows, :]
    previous, previous_shared = None, None
    returned = None
    for t in range(DEGREE):
        last = t == DEGREE - 1
        factor = (1.0 if t == 0 else 2.0) / HALF_WIDTH
        if t:
            uu[...] = stacked_parts(mass * partial)
            for c in range(cells):
                span = slice(c * width, (c + 1) * width)
                yy[:, span] = dot(uu[...], gather[0:owned, span])
        cell_products(None)
        inside = border_sums()
        if t == 0:
            lead_copy.wait_recv()
            learn(0)
            if len(rounds) > 1:
                tell(1)
            mass_ghost = lead_recv[rows:rows + 1, :]
            ghost = lead_recv[0:rows, :]
            fix = None
            outside = mass_ghost * ghost
        else:
            ret_copy.wait_recv()
            part_copy.wait_recv()
            for r in range(t, len(rounds) if last else t + 1):
                learn(r)
                if r + 1 < len(rounds):
                    tell(r + 1)
            fix = earlier * mass_shared * ret_recv[t - 1]
            ghost = part_recv[t - 1] + earlier * mass_ghost * returned
            current_shared = part + fix
            outside = jnp.concatenate([mass_ghost * ghost, mass_shared * fix], axis=1)
        used = outside.shape[1]
        edge = jnp.concatenate(
            [weight_edge[k * 2 * shared:k * 2 * shared + used, :] for k in range(3)], axis=0)
        border = inside + dot(triple(outside), edge)
        returned = border[:, 0:shared]
        ret_send[t] = returned
        ret_copy = send(ret_send.at[t], ret_recv.at[t], ret_sem, t, at(band, after))
        if not last:
            part = factor * (
                mass_shared * border[:, shared:] + (pot_shared - CENTER) * current_shared)
            if t:
                part = part - previous_shared
            part_send[t] = part
            part_copy = send(part_send.at[t], part_recv.at[t], part_sem, t, at(band, before))
        cell_products(stacked_parts(outside))
        current = partial
        if t:
            current = current + folded(dot(stacked_parts(fix), spread[...]))
        step = owned // CHUNKS if last else owned
        parts = []
        for j in range(owned // step):
            span = slice(j * step, (j + 1) * step)
            sums = folded(dot(zz[...], scatter[:, span]))
            piece = factor * (mass[:, span] * sums + (pot[:, span] - CENTER) * current[:, span])
            if t:
                piece = piece - previous[:, span]
            parts.append(piece)
            if last:
                block_send[j] = piece
                for k in range(1, n_band):
                    other = turned(band, k, n_band)
                    leads = place == jnp.where(band < other, 0, 1)

                    @pl.when(jnp.logical_not(leads))
                    def _():
                        remote(block_send.at[j], block_recv.at[n_band - k - 1, j], block_sem,
                               (k - 1) * CHUNKS + j, at(other, dom)).start()

                    if j == 0:
                        @pl.when(leads)
                        def _():
                            remote(ret_send.at[t], last_cross.at[n_band - k - 1],
                                   cross_last_sem, k - 1, at(other, after)).start()
        partial = jnp.concatenate(parts, axis=1) if last else parts[0]
        previous, previous_shared = current, current_shared
        earlier = factor

    scaling = 1.0 / (owned * n_dom)

    def packed(block):
        return jnp.concatenate([block[0:rows // 2], block[rows // 2:]], axis=1) * scaling

    def product(mine, theirs):
        both = folded(dot_nt(mine, theirs))
        return packed(both[:, 0:rows] + both[:, rows:])

    def mended(block, returned):
        fix = stacked_parts(earlier * mass_shared * returned)
        return block + folded(dot(fix, spread[...]))

    ret_copy.wait_recv()
    filtered = mended(partial, ret_recv[DEGREE - 1])
    filt_ref[...] = filtered
    uu[...] = stacked_parts(filtered)
    own_send[0] = product(uu[...], uu[...])
    pair_copy = send(own_send.at[0], own_recv, own_pair_sem, 0, at(band, partner))
    span = 2 * lines - 1
    for k in range(1, n_band):
        other = turned(band, k, n_band)
        leads = place == jnp.where(band < other, 0, 1)

        @pl.when(leads)
        def _():
            remote(ret_send.at[0], last_cross.at[k - 1], cross_last_sem, n_band - k - 1,
                   at(other, after)).wait_recv()
            fixes = stacked_parts(earlier * mass_shared * last_cross[k - 1])
            sums = [0.0, 0.0]
            for j in range(CHUNKS):
                remote(block_send.at[j], block_recv.at[k - 1, j], block_sem,
                       (n_band - k - 1) * CHUNKS + j, at(other, dom)).wait_recv()
                part = slice(j * step, (j + 1) * step)
                theirs = stacked_parts(
                    block_recv[k - 1, j] + folded(dot(fixes, spread[:, part])))
                mine = uu[:, part]
                sums[0] = sums[0] + folded(dot_nt(mine, theirs))
                sums[1] = sums[1] + folded(dot_nt(theirs, mine))
            for j in range(2):
                cross_send[k - 1, j] = packed(sums[j][:, 0:rows] + sums[j][:, rows:])
            for off in [*range(1, lines), 0]:
                if off:
                    remote(cross_send.at[k - 1, 0], cross_all.at[k - 1, off], cross_sem,
                           (k - 1) * span + off - 1, at(band, spot(off, place))).start()
                remote(cross_send.at[k - 1, 1], cross_all.at[n_band - k - 1, lines + off],
                       cross_sem, (k - 1) * span + lines - 1 + off,
                       at(other, spot(off, 1 - place))).start()

    pair_copy.wait_recv()
    own_send[1] = own_send[0] + own_recv[...]
    gathers = place == jnp.where(band == 0, 1, 0)

    @pl.when(gathers)
    def _():
        for l in range(1, lines):
            remote(own_send.at[1], own_all.at[l], own_line_sem, l - 1,
                   at(band, spot(l, place))).start()

    for k in range(1, n_band):
        other = turned(band, k, n_band)
        leads = place == jnp.where(band < other, 0, 1)

        @pl.when(leads)
        def _():
            total = cross_send[k - 1, 0]
            waits = []
            for l in range(lines):
                if l:
                    waits.append(remote(
                        cross_send.at[k - 1, 0], cross_all.at[k - 1, l], cross_sem,
                        (k - 1) * span + l - 1, at(band, spot(l, place))))
                waits.append(remote(
                    cross_send.at[k - 1, 1], cross_all.at[k - 1, lines + l], cross_sem,
                    (n_band - k - 1) * span + lines - 1 + l, at(other, spot(l, 1 - place))))
            for copy in waits:
                copy.wait_recv()
            for l in range(1, 2 * lines):
                total = total + cross_all[k - 1, l]
            final[k] = total
            remote(final.at[k], final.at[k], final_sem, k, at(band, partner)).start()

    @pl.when(gathers)
    def _():
        for l in range(1, lines):
            remote(own_send.at[1], own_all.at[l], own_line_sem, l - 1,
                   at(band, spot(l, place))).wait()
        total = own_send[1]
        for l in range(1, lines):
            total = total + own_all[l]
        final[0] = total
        remote(final.at[0], final.at[0], final_sem, 0, at(band, partner)).start()

    for k in range(n_band):
        other = turned(band, k, n_band)
        holds = place == jnp.where(band < other, 0, 1) if k else gathers
        copy = remote(final.at[k], final.at[k], final_sem, k, at(band, partner))

        @pl.when(holds)
        def _():
            copy.wait_send()

        @pl.when(jnp.logical_not(holds))
        def _():
            copy.wait_recv()

    pieces = []
    for b in range(n_band):
        piece = final[0]
        for k in range(1, n_band):
            piece = jnp.where(turned(band, k, n_band) == b, final[k], piece)
        pieces.append(jnp.concatenate([piece[:, 0:rows], piece[:, rows:]], axis=0))
    margin_ref[...] = jnp.concatenate(pieces, axis=1)
    for copy in started:
        copy.wait_send()
    for k in range(1, n_band):
        other = turned(band, k, n_band)
        leads = place == jnp.where(band < other, 0, 1)

        @pl.when(leads)
        def _():
            remote(ret_send.at[0], last_cross.at[k - 1], cross_last_sem, k - 1,
                   at(other, after)).wait_send()
            for l in range(lines):
                if l:
                    remote(cross_send.at[k - 1, 0], cross_all.at[k - 1, l], cross_sem,
                           (k - 1) * span + l - 1, at(band, spot(l, place))).wait_send()
                remote(cross_send.at[k - 1, 1], cross_all.at[k - 1, lines + l], cross_sem,
                       (k - 1) * span + lines - 1 + l,
                       at(other, spot(l, 1 - place))).wait_send()

        @pl.when(jnp.logical_not(leads))
        def _():
            for j in range(CHUNKS):
                remote(block_send.at[j], block_recv.at[k - 1, j], block_sem,
                       (k - 1) * CHUNKS + j, at(other, dom)).wait_send()


def finish(filt_ref, margin_ref, filt_out, margin_out, sem):
    copies = [
        pltpu.make_async_copy(filt_ref, filt_out, sem.at[0]),
        pltpu.make_async_copy(margin_ref, margin_out, sem.at[1])]
    for copy in copies:
        copy.start()
    for copy in copies:
        copy.wait()


def rounded_up(value):
    return -(-value // LANES) * LANES


def per_device(
    n_band, n_dom,
    states_in, stiffness, cell_scale, potential, inv_mass_sqrt, cell_nodes, shared_nodes
):
    rows, owned = states_in.shape
    cells, npc = cell_nodes.shape
    shared = shared_nodes.shape[0]
    width = rounded_up(npc)
    nodes = owned + 2 * shared
    states = n_band * rows
    main = width // (2 * LANES) * 2 * LANES
    rest = width - main
    lines = n_dom // PLACES
    others = n_band - 1
    block = (rows // 2, 2 * rows)
    pairs = lambda count: pltpu.SemaphoreType.DMA((2, count))
    vmem = pltpu.VMEM
    in_vmem = pl.BlockSpec(memory_space=pltpu.VMEM)
    found = pl.pallas_call(
        functools.partial(kernel, n_band, n_dom),
        out_shape=(
            jax.ShapeDtypeStruct((rows, owned), F32),
            jax.ShapeDtypeStruct((rows, states), F32),
        ),
        in_specs=[pl.BlockSpec(memory_space=pltpu.HBM)] * 7,
        out_specs=(in_vmem, in_vmem),
        scratch_shapes=[
            vmem((rows, owned), F32),
            vmem((npc, npc), F32),
            pltpu.SMEM((cells,), F32),
            vmem((1, owned), F32),
            vmem((1, owned), F32),
            vmem((cells, npc), jnp.int32),
            vmem((1, shared), jnp.int32),
            pltpu.SemaphoreType.DMA((7,)),
            vmem((-(-cells // 8) * 8, width), jnp.int32),
            vmem((width, width), F32),
            vmem((3 * width, main), BF16),
            vmem((2 * width, 2 * max(rest, LANES)), BF16),
            vmem((nodes, cells * width), BF16),
            vmem((cells * width, nodes), BF16),
            vmem((shared, owned), BF16),
            vmem((rows + 8, owned), F32),
            vmem((rows + 8, shared), F32),
            vmem((rows + 8, shared), F32),
            vmem((DEGREE, rows, shared), F32),
            vmem((DEGREE, rows, shared), F32),
            vmem((DEGREE - 1, rows, shared), F32),
            vmem((DEGREE - 1, rows, shared), F32),
            vmem((2 * rows, owned), BF16),
            vmem((2 * rows, cells * width), F32),
            vmem((cells * rows, 3 * width), BF16),
            vmem((2 * rows, cells * width), BF16),
            vmem((4 * shared, cells * width), BF16),
            vmem((6 * shared, 2 * shared), BF16),
            vmem((CHUNKS, rows, owned // CHUNKS), F32),
            vmem((others, CHUNKS, rows, owned // CHUNKS), F32),
            vmem((others, rows, shared), F32),
            vmem((2, *block), F32),
            vmem(block, F32),
            vmem((lines, *block), F32),
            vmem((others, 2, *block), F32),
            vmem((others, 2 * lines, *block), F32),
            vmem((n_band, *block), F32),
            pairs(1),
            pairs(DEGREE),
            pairs(DEGREE - 1),
            pairs(others),
            pairs(others * CHUNKS),
            pairs(1),
            pairs(lines - 1),
            pairs(others * (2 * lines - 1)),
            pairs(n_band),
            pltpu.SemaphoreType.REGULAR((max(n_dom.bit_length() - 2, 1),)),
        ],
        compiler_params=pltpu.CompilerParams(collective_id=0, has_side_effects=True, vmem_limit_bytes=44 << 20),
    )(*[pltpu.with_memory_space_constraint(value, pltpu.HBM) for value in (
        states_in, stiffness, cell_scale, potential[None, :], inv_mass_sqrt[None, :],
        cell_nodes, shared_nodes[None, :],
    )])
    return pl.pallas_call(
        finish,
        out_shape=tuple(jax.ShapeDtypeStruct(value.shape, F32) for value in found),
        in_specs=[in_vmem, in_vmem],
        out_specs=(pl.BlockSpec(memory_space=pltpu.HBM),) * 2,
        scratch_shapes=[pltpu.SemaphoreType.DMA((2,))],
    )(*[pltpu.with_memory_space_constraint(value, pltpu.VMEM) for value in found])


def solution(mesh):
    n_band, n_dom = mesh.shape["band"], mesh.shape["dom"]
    return jax.shard_map(
        functools.partial(per_device, n_band, n_dom),
        mesh=mesh,
        in_specs=(P("band", "dom"), P(), P("dom"), P("dom"), P("dom"), P("dom", None), P("dom")),
        out_specs=(P("band", "dom"), P("band", None)),
        check_vma=False,
    )
```

```python
import functools

import jax
import jax.numpy as jnp
from jax import lax
from jax.experimental import pallas as pl
from jax.experimental.pallas import tpu as pltpu
from jax.sharding import PartitionSpec as P

DEGREE = 3
CENTER = 1.0
HALF_WIDTH = 4.0
LANES = 128
PLACES = 2
CHUNKS = 4
F32, BF16 = jnp.float32, jnp.bfloat16


def stacked_parts(value):
    high = value.astype(BF16)
    low = (value - high.astype(F32)).astype(BF16)
    return jnp.concatenate([high, low], axis=0)


def folded(value):
    half = value.shape[0] // 2
    return value[:half] + value[half:]


def dot(a, b):
    return jnp.dot(a, b, preferred_element_type=F32)


def dot_nt(a, b):
    return lax.dot_general(a, b, (((1,), (1,)), ((), ())), preferred_element_type=F32)


def narrow(value):
    return value.astype(jnp.int16)


def one_hot(a, b):
    return jnp.where(a == b, jnp.array(1, BF16), jnp.array(0, BF16))


def kernel(
    n_band, n_dom,
    x_hbm, stiff_hbm, scale_hbm, pot_hbm, mass_hbm, cells_hbm, shared_hbm,
    filt_ref, margin_ref,
    x_ref, stiff_ref, scale_ref, pot_ref, mass_ref, cells_ref, shared_ref, load_sem,
    idx, stiff_pad, weight_main, weight_rest, gather, scatter, spread, lead,
    lead_send, lead_recv, ret_send, ret_recv, part_send, part_recv,
    uu, yy, xx, zz, tt, weight_edge, block_send, block_recv, last_cross,
    own_send, own_recv, own_all, cross_send, cross_all, final,
    lead_sem, ret_sem, part_sem, cross_last_sem, block_sem,
    own_pair_sem, own_line_sem, cross_sem, final_sem, known_sem,
):
    rows, owned = x_ref.shape
    cells, npc = cells_ref.shape
    shared = shared_ref.shape[1]
    width = idx.shape[1]
    main = weight_main.shape[1]
    rest = width - main
    local = owned + shared
    lines = n_dom // PLACES
    band, dom = lax.axis_index("band"), lax.axis_index("dom")
    after, before = lax.rem(dom + 1, n_dom), lax.rem(dom + n_dom - 1, n_dom)
    place, line = lax.rem(dom, PLACES), dom // PLACES
    partner = line * PLACES + 1 - place

    def turned(value, by, size):
        return lax.rem(value + by, size)

    def at(b, d):
        return {"band": b, "dom": d}

    def spot(l, p):
        return turned(line, l, lines) * PLACES + p

    pairs = (
        (shared_hbm, shared_ref), (mass_hbm, mass_ref), (pot_hbm, pot_ref), (x_hbm, x_ref),
        (cells_hbm, cells_ref), (stiff_hbm, stiff_ref), (scale_hbm, scale_ref))
    loads = [pltpu.make_async_copy(src, dst, load_sem.at[k]) for k, (src, dst) in enumerate(pairs)]
    first_loads, later_loads = loads[:5], loads[5:]
    barrier = pltpu.get_barrier_semaphore()
    others = [at(turned(band, k, n_band), dom) for k in range(1, n_band)]
    greeted = [at(band, after), at(band, before)] + others
    for device in greeted:
        pl.semaphore_signal(barrier, inc=1, device_id=device)
    for load in loads:
        load.start()

    rounds = []
    reach = 1
    while reach * 4 <= n_dom or not rounds:
        there = [at(band, lax.rem(dom + reach, n_dom)), at(band, lax.rem(dom + n_dom - reach, n_dom))]
        rounds.append(there + (others if reach == 1 else []))
        reach *= 2

    def tell(r):
        for device in rounds[r]:
            pl.semaphore_signal(known_sem.at[r], inc=1, device_id=device)

    def learn(r):
        pl.semaphore_wait(known_sem.at[r], len(rounds[r]))

    def remote(src, dst, sems, slot, device):
        return pltpu.make_async_remote_copy(
            src_ref=src, dst_ref=dst, send_sem=sems.at[0, slot], recv_sem=sems.at[1, slot],
            device_id=device, device_id_type=pl.DeviceIdType.MESH)

    started = []

    def send(*args):
        copy = remote(*args)
        copy.start()
        started.append(copy)
        return copy

    for load in first_loads:
        load.wait()
    mass, pot = mass_ref[...], pot_ref[...]
    shared_row = shared_ref[...]
    lead[0:rows, :] = x_ref[...]
    lead[rows:rows + 8, :] = jnp.concatenate(
        [mass, pot, jnp.zeros((6, owned), F32)], axis=0)
    wanted = jnp.broadcast_to(shared_row, (rows + 8, shared))
    lane_of, tile_of = wanted & (LANES - 1), wanted >> 7
    picked = None
    for k in range(owned // LANES):
        found = jnp.take_along_axis(lead[:, k * LANES:(k + 1) * LANES], lane_of, axis=1)
        picked = found if picked is None else jnp.where(tile_of == k, found, picked)
    lead_send[...] = picked
    uu[...] = stacked_parts(mass * x_ref[...])
    idx[...] = jnp.full(idx.shape, -1, jnp.int32)
    idx[0:cells, 0:npc] = cells_ref[...]
    node = narrow(lax.broadcasted_iota(jnp.int32, (LANES, width), 0))
    lane = narrow(lax.broadcasted_iota(jnp.int32, (width, LANES), 1))
    shared_col = jnp.broadcast_to(shared_row, (LANES, shared)).T
    shared_wide = narrow(jnp.concatenate([shared_col] * (width // LANES), axis=1))
    shared_tall = narrow(jnp.broadcast_to(shared_row, (width, shared)))
    for c in range(cells):
        span = slice(c * width, (c + 1) * width)
        slot_row = narrow(jnp.broadcast_to(idx[c:c + 1, :], (LANES, width)))
        for k in range(local // LANES):
            tile = slice(k * LANES, (k + 1) * LANES)
            gather[tile, span] = one_hot(node + jnp.int16(k * LANES), slot_row)
        gather[local:, span] = one_hot(shared_wide, slot_row)
        yy[:, span] = dot(uu[...], gather[0:owned, span])
    pl.semaphore_wait(barrier, len(greeted))
    lead_copy = send(lead_send, lead_recv, lead_sem, 0, at(band, before))
    tell(0)

    for load in later_loads:
        load.wait()
    for c in range(cells):
        span = slice(c * width, (c + 1) * width)
        slot_col = narrow(jnp.broadcast_to(idx[c:c + 1, :], (LANES, width)).T)
        for k in range(local // LANES):
            tile = slice(k * LANES, (k + 1) * LANES)
            scatter[span, tile] = one_hot(lane + jnp.int16(k * LANES), slot_col)
        scatter[span, local:] = one_hot(shared_tall, slot_col)
    short = narrow(shared_col)
    lane = narrow(lax.broadcasted_iota(jnp.int32, (shared, LANES), 1))
    for k in range(owned // LANES):
        spread[:, k * LANES:(k + 1) * LANES] = one_hot(lane + jnp.int16(k * LANES), short)
    stiff_pad[...] = jnp.zeros(stiff_pad.shape, F32)
    stiff_pad[0:npc, 0:npc] = stiff_ref[...]
    stiff = stiff_pad[...]
    high = stiff.astype(BF16)
    low = (stiff - high.astype(F32)).astype(BF16)
    top, bottom = slice(0, main), slice(main, width)
    weight_main[...] = jnp.concatenate([high[:, top], high[:, top], low[:, top]], axis=0)
    if rest:
        paired = jnp.concatenate([high[:, bottom], low[:, bottom]], axis=1)
        weight_rest[...] = jnp.concatenate([paired, paired], axis=0)

    def triple(value):
        value_high = value.astype(BF16)
        value_low = (value - value_high.astype(F32)).astype(BF16)
        return jnp.concatenate([value_high, value_low, value_high], axis=1)

    def wide(z_main, z_rest):
        if not rest:
            return z_main
        return jnp.concatenate([z_main, z_rest[:, 0:rest] + z_rest[:, rest:]], axis=1)

    def cell_products(outside):
        for c in range(cells):
            span = slice(c * width, (c + 1) * width)
            y = yy[:, span]
            if outside is not None:
                y = folded(y) + folded(dot(outside, gather[owned:owned + outside.shape[1], span]))
            else:
                y = folded(y)
            xx[c * rows:(c + 1) * rows, :] = triple(y)
        z_main = dot(xx[...], weight_main[...])
        z_rest = dot(xx[:, 0:2 * width], weight_rest[...]) if rest else None
        for c in range(cells):
            state = slice(c * rows, (c + 1) * rows)
            z = wide(z_main[state], z_rest[state] if rest else None)
            zz[:, c * width:(c + 1) * width] = stacked_parts(z * scale_ref[c])

    def border_sums():
        return folded(dot(zz[...], scatter[:, owned:]))

    for c in range(cells):
        span = slice(c * width, (c + 1) * width)
        picks = gather[owned:, span]
        z = wide(
            dot(jnp.concatenate([picks, picks], axis=1), weight_main[width:, :]),
            dot(picks, weight_rest[0:width, :]) if rest else None)
        tt[:, span] = stacked_parts(z * scale_ref[c])
    response = folded(dot(tt[...], scatter[:, owned:]))
    response_high = response.astype(BF16)
    response_low = (response - response_high.astype(F32)).astype(BF16)
    weight_edge[...] = jnp.concatenate([response_high, response_high, response_low], axis=0)

    mass_shared, pot_shared = lead_send[rows:rows + 1, :], lead_send[rows + 1:rows + 2, :]
    partial = x_ref[...]
    current_shared = lead_send[0:rows, :]
    previous, previous_shared = None, None
    returned = None
    for t in range(DEGREE):
        last = t == DEGREE - 1
        factor = (1.0 if t == 0 else 2.0) / HALF_WIDTH
        if t:
            uu[...] = stacked_parts(mass * partial)
            for c in range(cells):
                span = slice(c * width, (c + 1) * width)
                yy[:, span] = dot(uu[...], gather[0:owned, span])
        cell_products(None)
        inside = border_sums()
        if t == 0:
            lead_copy.wait_recv()
            learn(0)
            if len(rounds) > 1:
                tell(1)
            mass_ghost = lead_recv[rows:rows + 1, :]
            ghost = lead_recv[0:rows, :]
            fix = None
            outside = mass_ghost * ghost
        else:
            ret_copy.wait_recv()
            part_copy.wait_recv()
            for r in range(t, len(rounds) if last else t + 1):
                learn(r)
                if r + 1 < len(rounds):
                    tell(r + 1)
            fix = earlier * mass_shared * ret_recv[t - 1]
            ghost = part_recv[t - 1] + earlier * mass_ghost * returned
            current_shared = part + fix
            outside = jnp.concatenate([mass_ghost * ghost, mass_shared * fix], axis=1)
        used = outside.shape[1]
        edge = jnp.concatenate(
            [weight_edge[k * 2 * shared:k * 2 * shared + used, :] for k in range(3)], axis=0)
        border = inside + dot(triple(outside), edge)
        returned = border[:, 0:shared]
        ret_send[t] = returned
        ret_copy = send(ret_send.at[t], ret_recv.at[t], ret_sem, t, at(band, after))
        if not last:
            part = factor * (
                mass_shared * border[:, shared:] + (pot_shared - CENTER) * current_shared)
            if t:
                part = part - previous_shared
            part_send[t] = part
            part_copy = send(part_send.at[t], part_recv.at[t], part_sem, t, at(band, before))
        cell_products(stacked_parts(outside))
        current = partial
        if t:
            current = current + folded(dot(stacked_parts(fix), spread[...]))
        step = owned // CHUNKS if last else owned
        parts = []
        for j in range(owned // step):
            span = slice(j * step, (j + 1) * step)
            sums = folded(dot(zz[...], scatter[:, span]))
            piece = factor * (mass[:, span] * sums + (pot[:, span] - CENTER) * current[:, span])
            if t:
                piece = piece - previous[:, span]
            parts.append(piece)
            if last:
                block_send[j] = piece
                for k in range(1, n_band):
                    other = turned(band, k, n_band)
                    leads = place == jnp.where(band < other, 0, 1)

                    @pl.when(jnp.logical_not(leads))
                    def _():
                        remote(block_send.at[j], block_recv.at[n_band - k - 1, j], block_sem,
                               (k - 1) * CHUNKS + j, at(other, dom)).start()

                    if j == 0:
                        @pl.when(leads)
                        def _():
                            remote(ret_send.at[t], last_cross.at[n_band - k - 1],
                                   cross_last_sem, k - 1, at(other, after)).start()
        partial = jnp.concatenate(parts, axis=1) if last else parts[0]
        previous, previous_shared = current, current_shared
        earlier = factor

    scaling = 1.0 / (owned * n_dom)

    def packed(block):
        return jnp.concatenate([block[0:rows // 2], block[rows // 2:]], axis=1) * scaling

    def product(mine, theirs):
        both = folded(dot_nt(mine, theirs))
        return packed(both[:, 0:rows] + both[:, rows:])

    def mended(block, returned):
        fix = stacked_parts(earlier * mass_shared * returned)
        return block + folded(dot(fix, spread[...]))

    ret_copy.wait_recv()
    filtered = mended(partial, ret_recv[DEGREE - 1])
    filt_ref[...] = filtered
    uu[...] = stacked_parts(filtered)
    own_send[0] = product(uu[...], uu[...])
    pair_copy = send(own_send.at[0], own_recv, own_pair_sem, 0, at(band, partner))
    span = 2 * lines - 1
    for k in range(1, n_band):
        other = turned(band, k, n_band)
        leads = place == jnp.where(band < other, 0, 1)

        @pl.when(leads)
        def _():
            remote(ret_send.at[0], last_cross.at[k - 1], cross_last_sem, n_band - k - 1,
                   at(other, after)).wait_recv()
            fixes = stacked_parts(earlier * mass_shared * last_cross[k - 1])
            sums = [0.0, 0.0]
            for j in range(CHUNKS):
                remote(block_send.at[j], block_recv.at[k - 1, j], block_sem,
                       (n_band - k - 1) * CHUNKS + j, at(other, dom)).wait_recv()
                part = slice(j * step, (j + 1) * step)
                theirs = stacked_parts(
                    block_recv[k - 1, j] + folded(dot(fixes, spread[:, part])))
                mine = uu[:, part]
                sums[0] = sums[0] + folded(dot_nt(mine, theirs))
                sums[1] = sums[1] + folded(dot_nt(theirs, mine))
            for j in range(2):
                cross_send[k - 1, j] = packed(sums[j][:, 0:rows] + sums[j][:, rows:])
            for off in [*range(1, lines), 0]:
                if off:
                    remote(cross_send.at[k - 1, 0], cross_all.at[k - 1, off], cross_sem,
                           (k - 1) * span + off - 1, at(band, spot(off, place))).start()
                remote(cross_send.at[k - 1, 1], cross_all.at[n_band - k - 1, lines + off],
                       cross_sem, (k - 1) * span + lines - 1 + off,
                       at(other, spot(off, 1 - place))).start()

    pair_copy.wait_recv()
    own_send[1] = own_send[0] + own_recv[...]
    gathers = place == jnp.where(band == 0, 1, 0)

    @pl.when(gathers)
    def _():
        for l in range(1, lines):
            remote(own_send.at[1], own_all.at[l], own_line_sem, l - 1,
                   at(band, spot(l, place))).start()

    for k in range(1, n_band):
        other = turned(band, k, n_band)
        leads = place == jnp.where(band < other, 0, 1)

        @pl.when(leads)
        def _():
            total = cross_send[k - 1, 0]
            waits = []
            for l in range(lines):
                if l:
                    waits.append(remote(
                        cross_send.at[k - 1, 0], cross_all.at[k - 1, l], cross_sem,
                        (k - 1) * span + l - 1, at(band, spot(l, place))))
                waits.append(remote(
                    cross_send.at[k - 1, 1], cross_all.at[k - 1, lines + l], cross_sem,
                    (n_band - k - 1) * span + lines - 1 + l, at(other, spot(l, 1 - place))))
            for copy in waits:
                copy.wait_recv()
            for l in range(1, 2 * lines):
                total = total + cross_all[k - 1, l]
            final[k] = total
            remote(final.at[k], final.at[k], final_sem, k, at(band, partner)).start()

    @pl.when(gathers)
    def _():
        for l in range(1, lines):
            remote(own_send.at[1], own_all.at[l], own_line_sem, l - 1,
                   at(band, spot(l, place))).wait()
        total = own_send[1]
        for l in range(1, lines):
            total = total + own_all[l]
        final[0] = total
        remote(final.at[0], final.at[0], final_sem, 0, at(band, partner)).start()

    for k in range(n_band):
        other = turned(band, k, n_band)
        holds = place == jnp.where(band < other, 0, 1) if k else gathers
        copy = remote(final.at[k], final.at[k], final_sem, k, at(band, partner))

        @pl.when(holds)
        def _():
            copy.wait_send()

        @pl.when(jnp.logical_not(holds))
        def _():
            copy.wait_recv()

    pieces = []
    for b in range(n_band):
        piece = final[0]
        for k in range(1, n_band):
            piece = jnp.where(turned(band, k, n_band) == b, final[k], piece)
        pieces.append(jnp.concatenate([piece[:, 0:rows], piece[:, rows:]], axis=0))
    margin_ref[...] = jnp.concatenate(pieces, axis=1)
    for copy in started:
        copy.wait_send()
    for k in range(1, n_band):
        other = turned(band, k, n_band)
        leads = place == jnp.where(band < other, 0, 1)

        @pl.when(leads)
        def _():
            remote(ret_send.at[0], last_cross.at[k - 1], cross_last_sem, k - 1,
                   at(other, after)).wait_send()
            for l in range(lines):
                if l:
                    remote(cross_send.at[k - 1, 0], cross_all.at[k - 1, l], cross_sem,
                           (k - 1) * span + l - 1, at(band, spot(l, place))).wait_send()
                remote(cross_send.at[k - 1, 1], cross_all.at[k - 1, lines + l], cross_sem,
                       (k - 1) * span + lines - 1 + l,
                       at(other, spot(l, 1 - place))).wait_send()

        @pl.when(jnp.logical_not(leads))
        def _():
            for j in range(CHUNKS):
                remote(block_send.at[j], block_recv.at[k - 1, j], block_sem,
                       (k - 1) * CHUNKS + j, at(other, dom)).wait_send()


def finish(filt_ref, margin_ref, filt_out, margin_out, sem):
    copies = [
        pltpu.make_async_copy(filt_ref, filt_out, sem.at[0]),
        pltpu.make_async_copy(margin_ref, margin_out, sem.at[1])]
    for copy in copies:
        copy.start()
    for copy in copies:
        copy.wait()


def rounded_up(value):
    return -(-value // LANES) * LANES


def per_device(
    n_band, n_dom,
    states_in, stiffness, cell_scale, potential, inv_mass_sqrt, cell_nodes, shared_nodes
):
    rows, owned = states_in.shape
    cells, npc = cell_nodes.shape
    shared = shared_nodes.shape[0]
    width = rounded_up(npc)
    nodes = owned + 2 * shared
    states = n_band * rows
    main = width // (2 * LANES) * 2 * LANES
    rest = width - main
    lines = n_dom // PLACES
    others = n_band - 1
    block = (rows // 2, 2 * rows)
    pairs = lambda count: pltpu.SemaphoreType.DMA((2, count))
    vmem = pltpu.VMEM
    in_vmem = pl.BlockSpec(memory_space=pltpu.VMEM)
    found = pl.pallas_call(
        functools.partial(kernel, n_band, n_dom),
        out_shape=(
            jax.ShapeDtypeStruct((rows, owned), F32),
            jax.ShapeDtypeStruct((rows, states), F32),
        ),
        in_specs=[pl.BlockSpec(memory_space=pltpu.HBM)] * 7,
        out_specs=(in_vmem, in_vmem),
        scratch_shapes=[
            vmem((rows, owned), F32),
            vmem((npc, npc), F32),
            pltpu.SMEM((cells,), F32),
            vmem((1, owned), F32),
            vmem((1, owned), F32),
            vmem((cells, npc), jnp.int32),
            vmem((1, shared), jnp.int32),
            pltpu.SemaphoreType.DMA((7,)),
            vmem((-(-cells // 8) * 8, width), jnp.int32),
            vmem((width, width), F32),
            vmem((3 * width, main), BF16),
            vmem((2 * width, 2 * max(rest, LANES)), BF16),
            vmem((nodes, cells * width), BF16),
            vmem((cells * width, nodes), BF16),
            vmem((shared, owned), BF16),
            vmem((rows + 8, owned), F32),
            vmem((rows + 8, shared), F32),
            vmem((rows + 8, shared), F32),
            vmem((DEGREE, rows, shared), F32),
            vmem((DEGREE, rows, shared), F32),
            vmem((DEGREE - 1, rows, shared), F32),
            vmem((DEGREE - 1, rows, shared), F32),
            vmem((2 * rows, owned), BF16),
            vmem((2 * rows, cells * width), F32),
            vmem((cells * rows, 3 * width), BF16),
            vmem((2 * rows, cells * width), BF16),
            vmem((4 * shared, cells * width), BF16),
            vmem((6 * shared, 2 * shared), BF16),
            vmem((CHUNKS, rows, owned // CHUNKS), F32),
            vmem((others, CHUNKS, rows, owned // CHUNKS), F32),
            vmem((others, rows, shared), F32),
            vmem((2, *block), F32),
            vmem(block, F32),
            vmem((lines, *block), F32),
            vmem((others, 2, *block), F32),
            vmem((others, 2 * lines, *block), F32),
            vmem((n_band, *block), F32),
            pairs(1),
            pairs(DEGREE),
            pairs(DEGREE - 1),
            pairs(others),
            pairs(others * CHUNKS),
            pairs(1),
            pairs(lines - 1),
            pairs(others * (2 * lines - 1)),
            pairs(n_band),
            pltpu.SemaphoreType.REGULAR((max(n_dom.bit_length() - 2, 1),)),
        ],
        compiler_params=pltpu.CompilerParams(collective_id=0, has_side_effects=True, vmem_limit_bytes=44 << 20),
    )(*[pltpu.with_memory_space_constraint(value, pltpu.HBM) for value in (
        states_in, stiffness, cell_scale, potential[None, :], inv_mass_sqrt[None, :],
        cell_nodes, shared_nodes[None, :],
    )])
    return pl.pallas_call(
        finish,
        out_shape=tuple(jax.ShapeDtypeStruct(value.shape, F32) for value in found),
        in_specs=[in_vmem, in_vmem],
        out_specs=(pl.BlockSpec(memory_space=pltpu.HBM),) * 2,
        scratch_shapes=[pltpu.SemaphoreType.DMA((2,))],
    )(*[pltpu.with_memory_space_constraint(value, pltpu.VMEM) for value in found])


def solution(mesh):
    n_band, n_dom = mesh.shape["band"], mesh.shape["dom"]
    return jax.shard_map(
        functools.partial(per_device, n_band, n_dom),
        mesh=mesh,
        in_specs=(P("band", "dom"), P(), P("dom"), P("dom"), P("dom"), P("dom", None), P("dom")),
        out_specs=(P("band", "dom"), P("band", None)),
        check_vma=False,
    )
```

```python
import functools

import jax
import jax.numpy as jnp
from jax import lax
from jax.experimental import pallas as pl
from jax.experimental.pallas import tpu as pltpu
from jax.sharding import PartitionSpec as P

DEGREE = 3
CENTER = 1.0
HALF_WIDTH = 4.0
LANES = 128
PLACES = 2
CHUNKS = 4
F32, BF16 = jnp.float32, jnp.bfloat16


def stacked_parts(value):
    high = value.astype(BF16)
    low = (value - high.astype(F32)).astype(BF16)
    return jnp.concatenate([high, low], axis=0)


def folded(value):
    half = value.shape[0] // 2
    return value[:half] + value[half:]


def dot(a, b):
    return jnp.dot(a, b, preferred_element_type=F32)


def dot_nt(a, b):
    return lax.dot_general(a, b, (((1,), (1,)), ((), ())), preferred_element_type=F32)


def narrow(value):
    return value.astype(jnp.int16)


def one_hot(a, b):
    return jnp.where(a == b, jnp.array(1, BF16), jnp.array(0, BF16))


def kernel(
    n_band, n_dom,
    x_hbm, stiff_hbm, scale_hbm, pot_hbm, mass_hbm, cells_hbm, shared_hbm,
    filt_ref, margin_ref,
    x_ref, stiff_ref, scale_ref, pot_ref, mass_ref, cells_ref, shared_ref, load_sem,
    idx, stiff_pad, weight_main, weight_rest, gather, scatter, spread, lead,
    lead_send, lead_recv, ret_send, ret_recv, part_send, part_recv,
    uu, yy, xx, zz, tt, weight_edge, block_send, block_recv, last_cross,
    own_send, own_recv, own_all, cross_send, cross_all, final,
    lead_sem, ret_sem, part_sem, cross_last_sem, block_sem,
    own_pair_sem, own_line_sem, cross_sem, final_sem, known_sem,
):
    rows, owned = x_ref.shape
    cells, npc = cells_ref.shape
    shared = shared_ref.shape[1]
    width = idx.shape[1]
    main = weight_main.shape[1]
    rest = width - main
    local = owned + shared
    lines = n_dom // PLACES
    band, dom = lax.axis_index("band"), lax.axis_index("dom")
    after, before = lax.rem(dom + 1, n_dom), lax.rem(dom + n_dom - 1, n_dom)
    place, line = lax.rem(dom, PLACES), dom // PLACES
    partner = line * PLACES + 1 - place

    def turned(value, by, size):
        return lax.rem(value + by, size)

    def at(b, d):
        return {"band": b, "dom": d}

    def spot(l, p):
        return turned(line, l, lines) * PLACES + p

    pairs = (
        (shared_hbm, shared_ref), (mass_hbm, mass_ref), (pot_hbm, pot_ref), (x_hbm, x_ref),
        (cells_hbm, cells_ref), (stiff_hbm, stiff_ref), (scale_hbm, scale_ref))
    loads = [pltpu.make_async_copy(src, dst, load_sem.at[k]) for k, (src, dst) in enumerate(pairs)]
    first_loads, later_loads = loads[:5], loads[5:]
    barrier = pltpu.get_barrier_semaphore()
    others = [at(turned(band, k, n_band), dom) for k in range(1, n_band)]
    greeted = [at(band, after), at(band, before)] + others
    for device in greeted:
        pl.semaphore_signal(barrier, inc=1, device_id=device)
    for load in loads:
        load.start()

    rounds = []
    reach = 1
    while reach * 4 <= n_dom or not rounds:
        there = [at(band, lax.rem(dom + reach, n_dom)), at(band, lax.rem(dom + n_dom - reach, n_dom))]
        rounds.append(there + (others if reach == 1 else []))
        reach *= 2

    def tell(r):
        for device in rounds[r]:
            pl.semaphore_signal(known_sem.at[r], inc=1, device_id=device)

    def learn(r):
        pl.semaphore_wait(known_sem.at[r], len(rounds[r]))

    def remote(src, dst, sems, slot, device):
        return pltpu.make_async_remote_copy(
            src_ref=src, dst_ref=dst, send_sem=sems.at[0, slot], recv_sem=sems.at[1, slot],
            device_id=device, device_id_type=pl.DeviceIdType.MESH)

    started = []

    def send(*args):
        copy = remote(*args)
        copy.start()
        started.append(copy)
        return copy

    for load in first_loads:
        load.wait()
    mass, pot = mass_ref[...], pot_ref[...]
    shared_row = shared_ref[...]
    lead[0:rows, :] = x_ref[...]
    lead[rows:rows + 8, :] = jnp.concatenate(
        [mass, pot, jnp.zeros((6, owned), F32)], axis=0)
    wanted = jnp.broadcast_to(shared_row, (rows + 8, shared))
    lane_of, tile_of = wanted & (LANES - 1), wanted >> 7
    picked = None
    for k in range(owned // LANES):
        found = jnp.take_along_axis(lead[:, k * LANES:(k + 1) * LANES], lane_of, axis=1)
        picked = found if picked is None else jnp.where(tile_of == k, found, picked)
    lead_send[...] = picked
    uu[...] = stacked_parts(mass * x_ref[...])
    idx[...] = jnp.full(idx.shape, -1, jnp.int32)
    idx[0:cells, 0:npc] = cells_ref[...]
    node = narrow(lax.broadcasted_iota(jnp.int32, (LANES, width), 0))
    lane = narrow(lax.broadcasted_iota(jnp.int32, (width, LANES), 1))
    shared_col = jnp.broadcast_to(shared_row, (LANES, shared)).T
    shared_wide = narrow(jnp.concatenate([shared_col] * (width // LANES), axis=1))
    shared_tall = narrow(jnp.broadcast_to(shared_row, (width, shared)))
    for c in range(cells):
        span = slice(c * width, (c + 1) * width)
        slot_row = narrow(jnp.broadcast_to(idx[c:c + 1, :], (LANES, width)))
        for k in range(local // LANES):
            tile = slice(k * LANES, (k + 1) * LANES)
            gather[tile, span] = one_hot(node + jnp.int16(k * LANES), slot_row)
        gather[local:, span] = one_hot(shared_wide, slot_row)
        yy[:, span] = dot(uu[...], gather[0:owned, span])
    pl.semaphore_wait(barrier, len(greeted))
    lead_copy = send(lead_send, lead_recv, lead_sem, 0, at(band, before))
    tell(0)

    for load in later_loads:
        load.wait()
    for c in range(cells):
        span = slice(c * width, (c + 1) * width)
        slot_col = narrow(jnp.broadcast_to(idx[c:c + 1, :], (LANES, width)).T)
        for k in range(local // LANES):
            tile = slice(k * LANES, (k + 1) * LANES)
            scatter[span, tile] = one_hot(lane + jnp.int16(k * LANES), slot_col)
        scatter[span, local:] = one_hot(shared_tall, slot_col)
    short = narrow(shared_col)
    lane = narrow(lax.broadcasted_iota(jnp.int32, (shared, LANES), 1))
    for k in range(owned // LANES):
        spread[:, k * LANES:(k + 1) * LANES] = one_hot(lane + jnp.int16(k * LANES), short)
    stiff_pad[...] = jnp.zeros(stiff_pad.shape, F32)
    stiff_pad[0:npc, 0:npc] = stiff_ref[...]
    stiff = stiff_pad[...]
    high = stiff.astype(BF16)
    low = (stiff - high.astype(F32)).astype(BF16)
    top, bottom = slice(0, main), slice(main, width)
    weight_main[...] = jnp.concatenate([high[:, top], high[:, top], low[:, top]], axis=0)
    if rest:
        paired = jnp.concatenate([high[:, bottom], low[:, bottom]], axis=1)
        weight_rest[...] = jnp.concatenate([paired, paired], axis=0)

    def triple(value):
        value_high = value.astype(BF16)
        value_low = (value - value_high.astype(F32)).astype(BF16)
        return jnp.concatenate([value_high, value_low, value_high], axis=1)

    def wide(z_main, z_rest):
        if not rest:
            return z_main
        return jnp.concatenate([z_main, z_rest[:, 0:rest] + z_rest[:, rest:]], axis=1)

    def cell_products(outside):
        for c in range(cells):
            span = slice(c * width, (c + 1) * width)
            y = yy[:, span]
            if outside is not None:
                y = folded(y) + folded(dot(outside, gather[owned:owned + outside.shape[1], span]))
            else:
                y = folded(y)
            xx[c * rows:(c + 1) * rows, :] = triple(y)
        z_main = dot(xx[...], weight_main[...])
        z_rest = dot(xx[:, 0:2 * width], weight_rest[...]) if rest else None
        for c in range(cells):
            state = slice(c * rows, (c + 1) * rows)
            z = wide(z_main[state], z_rest[state] if rest else None)
            zz[:, c * width:(c + 1) * width] = stacked_parts(z * scale_ref[c])

    def border_sums():
        return folded(dot(zz[...], scatter[:, owned:]))

    for c in range(cells):
        span = slice(c * width, (c + 1) * width)
        picks = gather[owned:, span]
        z = wide(
            dot(jnp.concatenate([picks, picks], axis=1), weight_main[width:, :]),
            dot(picks, weight_rest[0:width, :]) if rest else None)
        tt[:, span] = stacked_parts(z * scale_ref[c])
    response = folded(dot(tt[...], scatter[:, owned:]))
    response_high = response.astype(BF16)
    response_low = (response - response_high.astype(F32)).astype(BF16)
    weight_edge[...] = jnp.concatenate([response_high, response_high, response_low], axis=0)

    mass_shared, pot_shared = lead_send[rows:rows + 1, :], lead_send[rows + 1:rows + 2, :]
    partial = x_ref[...]
    current_shared = lead_send[0:rows, :]
    previous, previous_shared = None, None
    returned = None
    for t in range(DEGREE):
        last = t == DEGREE - 1
        factor = (1.0 if t == 0 else 2.0) / HALF_WIDTH
        if t:
            uu[...] = stacked_parts(mass * partial)
            for c in range(cells):
                span = slice(c * width, (c + 1) * width)
                yy[:, span] = dot(uu[...], gather[0:owned, span])
        cell_products(None)
        inside = border_sums()
        if t == 0:
            lead_copy.wait_recv()
            learn(0)
            if len(rounds) > 1:
                tell(1)
            mass_ghost = lead_recv[rows:rows + 1, :]
            ghost = lead_recv[0:rows, :]
            fix = None
            outside = mass_ghost * ghost
        else:
            ret_copy.wait_recv()
            part_copy.wait_recv()
            for r in range(t, len(rounds) if last else t + 1):
                learn(r)
                if r + 1 < len(rounds):
                    tell(r + 1)
            fix = earlier * mass_shared * ret_recv[t - 1]
            ghost = part_recv[t - 1] + earlier * mass_ghost * returned
            current_shared = part + fix
            outside = jnp.concatenate([mass_ghost * ghost, mass_shared * fix], axis=1)
        used = outside.shape[1]
        edge = jnp.concatenate(
            [weight_edge[k * 2 * shared:k * 2 * shared + used, :] for k in range(3)], axis=0)
        border = inside + dot(triple(outside), edge)
        returned = border[:, 0:shared]
        ret_send[t] = returned
        ret_copy = send(ret_send.at[t], ret_recv.at[t], ret_sem, t, at(band, after))
        if not last:
            part = factor * (
                mass_shared * border[:, shared:] + (pot_shared - CENTER) * current_shared)
            if t:
                part = part - previous_shared
            part_send[t] = part
            part_copy = send(part_send.at[t], part_recv.at[t], part_sem, t, at(band, before))
        cell_products(stacked_parts(outside))
        current = partial
        if t:
            current = current + folded(dot(stacked_parts(fix), spread[...]))
        step = owned // CHUNKS if last else owned
        parts = []
        for j in range(owned // step):
            span = slice(j * step, (j + 1) * step)
            sums = folded(dot(zz[...], scatter[:, span]))
            piece = factor * (mass[:, span] * sums + (pot[:, span] - CENTER) * current[:, span])
            if t:
                piece = piece - previous[:, span]
            parts.append(piece)
            if last:
                block_send[j] = piece
                for k in range(1, n_band):
                    other = turned(band, k, n_band)
                    leads = place == jnp.where(band < other, 1, 0)

                    @pl.when(jnp.logical_not(leads))
                    def _():
                        remote(block_send.at[j], block_recv.at[n_band - k - 1, j], block_sem,
                               (k - 1) * CHUNKS + j, at(other, dom)).start()

                    if j == 0:
                        @pl.when(leads)
                        def _():
                            remote(ret_send.at[t], last_cross.at[n_band - k - 1],
                                   cross_last_sem, k - 1, at(other, after)).start()
        partial = jnp.concatenate(parts, axis=1) if last else parts[0]
        previous, previous_shared = current, current_shared
        earlier = factor

    scaling = 1.0 / (owned * n_dom)

    def packed(block):
        return jnp.concatenate([block[0:rows // 2], block[rows // 2:]], axis=1) * scaling

    def product(mine, theirs):
        both = folded(dot_nt(mine, theirs))
        return packed(both[:, 0:rows] + both[:, rows:])

    def mended(block, returned):
        fix = stacked_parts(earlier * mass_shared * returned)
        return block + folded(dot(fix, spread[...]))

    ret_copy.wait_recv()
    filtered = mended(partial, ret_recv[DEGREE - 1])
    filt_ref[...] = filtered
    uu[...] = stacked_parts(filtered)
    own_send[0] = product(uu[...], uu[...])
    pair_copy = send(own_send.at[0], own_recv, own_pair_sem, 0, at(band, partner))
    span = 2 * lines - 1
    for k in range(1, n_band):
        other = turned(band, k, n_band)
        leads = place == jnp.where(band < other, 1, 0)

        @pl.when(leads)
        def _():
            remote(ret_send.at[0], last_cross.at[k - 1], cross_last_sem, n_band - k - 1,
                   at(other, after)).wait_recv()
            fixes = stacked_parts(earlier * mass_shared * last_cross[k - 1])
            sums = [0.0, 0.0]
            for j in range(CHUNKS):
                remote(block_send.at[j], block_recv.at[k - 1, j], block_sem,
                       (n_band - k - 1) * CHUNKS + j, at(other, dom)).wait_recv()
                part = slice(j * step, (j + 1) * step)
                theirs = stacked_parts(
                    block_recv[k - 1, j] + folded(dot(fixes, spread[:, part])))
                mine = uu[:, part]
                sums[0] = sums[0] + folded(dot_nt(mine, theirs))
                sums[1] = sums[1] + folded(dot_nt(theirs, mine))
            for j in range(2):
                cross_send[k - 1, j] = packed(sums[j][:, 0:rows] + sums[j][:, rows:])
            for off in [*range(1, lines), 0]:
                if off:
                    remote(cross_send.at[k - 1, 0], cross_all.at[k - 1, off], cross_sem,
                           (k - 1) * span + off - 1, at(band, spot(off, place))).start()
                remote(cross_send.at[k - 1, 1], cross_all.at[n_band - k - 1, lines + off],
                       cross_sem, (k - 1) * span + lines - 1 + off,
                       at(other, spot(off, 1 - place))).start()

    pair_copy.wait_recv()
    own_send[1] = own_send[0] + own_recv[...]
    gathers = place == jnp.where(band == 0, 0, 1)

    @pl.when(gathers)
    def _():
        for l in range(1, lines):
            remote(own_send.at[1], own_all.at[l], own_line_sem, l - 1,
                   at(band, spot(l, place))).start()

    for k in range(1, n_band):
        other = turned(band, k, n_band)
        leads = place == jnp.where(band < other, 1, 0)

        @pl.when(leads)
        def _():
            total = cross_send[k - 1, 0]
            waits = []
            for l in range(lines):
                if l:
                    waits.append(remote(
                        cross_send.at[k - 1, 0], cross_all.at[k - 1, l], cross_sem,
                        (k - 1) * span + l - 1, at(band, spot(l, place))))
                waits.append(remote(
                    cross_send.at[k - 1, 1], cross_all.at[k - 1, lines + l], cross_sem,
                    (n_band - k - 1) * span + lines - 1 + l, at(other, spot(l, 1 - place))))
            for copy in waits:
                copy.wait_recv()
            for l in range(1, 2 * lines):
                total = total + cross_all[k - 1, l]
            final[k] = total
            remote(final.at[k], final.at[k], final_sem, k, at(band, partner)).start()

    @pl.when(gathers)
    def _():
        for l in range(1, lines):
            remote(own_send.at[1], own_all.at[l], own_line_sem, l - 1,
                   at(band, spot(l, place))).wait()
        total = own_send[1]
        for l in range(1, lines):
            total = total + own_all[l]
        final[0] = total
        remote(final.at[0], final.at[0], final_sem, 0, at(band, partner)).start()

    for k in range(n_band):
        other = turned(band, k, n_band)
        holds = place == jnp.where(band < other, 1, 0) if k else gathers
        copy = remote(final.at[k], final.at[k], final_sem, k, at(band, partner))

        @pl.when(holds)
        def _():
            copy.wait_send()

        @pl.when(jnp.logical_not(holds))
        def _():
            copy.wait_recv()

    pieces = []
    for b in range(n_band):
        piece = final[0]
        for k in range(1, n_band):
            piece = jnp.where(turned(band, k, n_band) == b, final[k], piece)
        pieces.append(jnp.concatenate([piece[:, 0:rows], piece[:, rows:]], axis=0))
    margin_ref[...] = jnp.concatenate(pieces, axis=1)
    for copy in started:
        copy.wait_send()
    for k in range(1, n_band):
        other = turned(band, k, n_band)
        leads = place == jnp.where(band < other, 1, 0)

        @pl.when(leads)
        def _():
            remote(ret_send.at[0], last_cross.at[k - 1], cross_last_sem, k - 1,
                   at(other, after)).wait_send()
            for l in range(lines):
                if l:
                    remote(cross_send.at[k - 1, 0], cross_all.at[k - 1, l], cross_sem,
                           (k - 1) * span + l - 1, at(band, spot(l, place))).wait_send()
                remote(cross_send.at[k - 1, 1], cross_all.at[k - 1, lines + l], cross_sem,
                       (k - 1) * span + lines - 1 + l,
                       at(other, spot(l, 1 - place))).wait_send()

        @pl.when(jnp.logical_not(leads))
        def _():
            for j in range(CHUNKS):
                remote(block_send.at[j], block_recv.at[k - 1, j], block_sem,
                       (k - 1) * CHUNKS + j, at(other, dom)).wait_send()


def finish(filt_ref, margin_ref, filt_out, margin_out, sem):
    copies = [
        pltpu.make_async_copy(filt_ref, filt_out, sem.at[0]),
        pltpu.make_async_copy(margin_ref, margin_out, sem.at[1])]
    for copy in copies:
        copy.start()
    for copy in copies:
        copy.wait()


def rounded_up(value):
    return -(-value // LANES) * LANES


def per_device(
    n_band, n_dom,
    states_in, stiffness, cell_scale, potential, inv_mass_sqrt, cell_nodes, shared_nodes
):
    rows, owned = states_in.shape
    cells, npc = cell_nodes.shape
    shared = shared_nodes.shape[0]
    width = rounded_up(npc)
    nodes = owned + 2 * shared
    states = n_band * rows
    main = width // (2 * LANES) * 2 * LANES
    rest = width - main
    lines = n_dom // PLACES
    others = n_band - 1
    block = (rows // 2, 2 * rows)
    pairs = lambda count: pltpu.SemaphoreType.DMA((2, count))
    vmem = pltpu.VMEM
    in_vmem = pl.BlockSpec(memory_space=pltpu.VMEM)
    found = pl.pallas_call(
        functools.partial(kernel, n_band, n_dom),
        out_shape=(
            jax.ShapeDtypeStruct((rows, owned), F32),
            jax.ShapeDtypeStruct((rows, states), F32),
        ),
        in_specs=[pl.BlockSpec(memory_space=pltpu.HBM)] * 7,
        out_specs=(in_vmem, in_vmem),
        scratch_shapes=[
            vmem((rows, owned), F32),
            vmem((npc, npc), F32),
            pltpu.SMEM((cells,), F32),
            vmem((1, owned), F32),
            vmem((1, owned), F32),
            vmem((cells, npc), jnp.int32),
            vmem((1, shared), jnp.int32),
            pltpu.SemaphoreType.DMA((7,)),
            vmem((-(-cells // 8) * 8, width), jnp.int32),
            vmem((width, width), F32),
            vmem((3 * width, main), BF16),
            vmem((2 * width, 2 * max(rest, LANES)), BF16),
            vmem((nodes, cells * width), BF16),
            vmem((cells * width, nodes), BF16),
            vmem((shared, owned), BF16),
            vmem((rows + 8, owned), F32),
            vmem((rows + 8, shared), F32),
            vmem((rows + 8, shared), F32),
            vmem((DEGREE, rows, shared), F32),
            vmem((DEGREE, rows, shared), F32),
            vmem((DEGREE - 1, rows, shared), F32),
            vmem((DEGREE - 1, rows, shared), F32),
            vmem((2 * rows, owned), BF16),
            vmem((2 * rows, cells * width), F32),
            vmem((cells * rows, 3 * width), BF16),
            vmem((2 * rows, cells * width), BF16),
            vmem((4 * shared, cells * width), BF16),
            vmem((6 * shared, 2 * shared), BF16),
            vmem((CHUNKS, rows, owned // CHUNKS), F32),
            vmem((others, CHUNKS, rows, owned // CHUNKS), F32),
            vmem((others, rows, shared), F32),
            vmem((2, *block), F32),
            vmem(block, F32),
            vmem((lines, *block), F32),
            vmem((others, 2, *block), F32),
            vmem((others, 2 * lines, *block), F32),
            vmem((n_band, *block), F32),
            pairs(1),
            pairs(DEGREE),
            pairs(DEGREE - 1),
            pairs(others),
            pairs(others * CHUNKS),
            pairs(1),
            pairs(lines - 1),
            pairs(others * (2 * lines - 1)),
            pairs(n_band),
            pltpu.SemaphoreType.REGULAR((max(n_dom.bit_length() - 2, 1),)),
        ],
        compiler_params=pltpu.CompilerParams(collective_id=0, has_side_effects=True, vmem_limit_bytes=44 << 20),
    )(*[pltpu.with_memory_space_constraint(value, pltpu.HBM) for value in (
        states_in, stiffness, cell_scale, potential[None, :], inv_mass_sqrt[None, :],
        cell_nodes, shared_nodes[None, :],
    )])
    return pl.pallas_call(
        finish,
        out_shape=tuple(jax.ShapeDtypeStruct(value.shape, F32) for value in found),
        in_specs=[in_vmem, in_vmem],
        out_specs=(pl.BlockSpec(memory_space=pltpu.HBM),) * 2,
        scratch_shapes=[pltpu.SemaphoreType.DMA((2,))],
    )(*[pltpu.with_memory_space_constraint(value, pltpu.VMEM) for value in found])


def solution(mesh):
    n_band, n_dom = mesh.shape["band"], mesh.shape["dom"]
    return jax.shard_map(
        functools.partial(per_device, n_band, n_dom),
        mesh=mesh,
        in_specs=(P("band", "dom"), P(), P("dom"), P("dom"), P("dom"), P("dom", None), P("dom")),
        out_specs=(P("band", "dom"), P("band", None)),
        check_vma=False,
    )
```
